32 devices in a mesh: batch: 4 (over y, x), seq: 4 (over z), frames: 2 (over core).
Axes of the slice: x: 2, y: 2, z: 4, core: 2. Of those that a mesh axis runs over, the one named last changes fastest.
Arguments:
- frames_in: bfloat16 [4, 4, 2, 192, 1024], P('batch', 'seq', 'frames'), may hold values from -6 to 6
- skip_in: bfloat16 [4, 4, 2, 192, 1024], P('batch', 'seq', 'frames'), may hold values from -6 to 6
- lengths: int32 [4, 2, 3], P('batch', 'frames'), may hold values from 1 to 512, 736 in all within a row
- cotangent: bfloat16 [4, 4, 2, 192, 1024], P('batch', 'seq', 'frames'), may hold values from -6 to 6
- w_skip: bfloat16 [2048, 1024], P('frames'), may hold values from -0.125 to 0.125
- w_qkv: bfloat16 [1024, 3072], P('frames'), may hold values from -0.1875 to 0.1875
- w_out: bfloat16 [1024, 1024], P('frames'), may hold values from -0.5 to 0.5
- w_up: bfloat16 [1024, 4096], P('frames'), may hold values from -0.1875 to 0.1875
- w_down: bfloat16 [4096, 1024], P('frames'), may hold values from -0.09375 to 0.09375
- skip_bias: bfloat16 [1024], P('frames'), may hold values from -3 to 3
- norm1_gain: bfloat16 [1024], P('frames'), may hold values from 0.25 to 1.75
- norm1_bias: bfloat16 [1024], P('frames'), may hold values from -3 to 3
- out_bias: bfloat16 [1024], P('frames'), may hold values from -3 to 3
- norm2_gain: bfloat16 [1024], P('frames'), may hold values from 0.25 to 1.75
- norm2_bias: bfloat16 [1024], P('frames'), may hold values from -3 to 3
- up_bias: bfloat16 [4096], P('frames'), may hold values from -3 to 3
- down_bias: bfloat16 [1024], P('frames'), may hold values from -3 to 3
Outputs:
- output: bfloat16 [4, 4, 2, 192, 1024], P('batch', 'seq', 'frames')
- input_grad: float32 [4, 4, 2, 192, 1024], P('batch', 'seq', 'frames')
- skip_grad: float32 [4, 4, 2, 192, 1024], P('batch', 'seq', 'frames')
- grad_w_skip: float32 [2048, 1024], P('frames')
- grad_w_qkv: float32 [1024, 3072], P('frames')
- grad_w_out: float32 [1024, 1024], P('frames')
- grad_w_up: float32 [1024, 4096], P('frames')
- grad_w_down: float32 [4096, 1024], P('frames')
- grad_skip_bias: float32 [1024], P('frames')
- grad_norm1_gain: float32 [1024], P('frames')
- grad_norm1_bias: float32 [1024], P('frames')
- grad_out_bias: float32 [1024], P('frames')
- grad_norm2_gain: float32 [1024], P('frames')
- grad_norm2_bias: float32 [1024], P('frames')
- grad_up_bias: float32 [4096], P('frames')
- grad_down_bias: float32 [1024], P('frames')
The draws below stay inside these ranges and needn't reach their ends.
Inputs may be any that keep to these rules, and one draw needn't show every extreme that they name: `lengths`: in every group the utterances lie end to end from its first frame and fill all but its last 32 frames, which are padding; in every group the longest utterance has exactly 512 frames.
All inputs are finite; a program needn't handle non-finite values.
Results may differ from the reference program's by a relative error of at most 0.012.
Values may be sent and summed in bfloat16 or wider, within the bound.
No kernel may reach another device: no remote copies, remote signals or barrier semaphores. Data moves between devices by JAX's collectives and lax.ppermute only.
A program may use at most 320 MiB of HBM per device.

```python
import math
import jax
import jax.numpy as jnp
import numpy as np
from jax import lax

D = 1024
HEADS = 16
HD = 64
FF = 4096
TOK_DEV = 192
UTTS = 3
N_BATCH = 4
N_SEQ = 4
N_FRAMES = 2


def shard_levels(rng, extent, split, smallest, top_value):
    factor_of = 1.0
    for dim, blocks in split:
        heights = jax.random.uniform(jax.random.fold_in(jax.random.fold_in(rng, 6), dim), (blocks,), jnp.float32, smallest / len(split), top_value / len(split))
        factor_of = factor_of * jnp.repeat(jnp.exp(heights), extent[dim] // blocks).reshape((-1,) + (1,) * (len(extent) - 1 - dim))
    return factor_of


def profile(count, total, most, slope):
    loads = [(1 << 20) // math.isqrt(rank ** slope) + 1 for rank in range(2, count + 1)]
    surplus, given = total - most - (count - 1), [1] * (count - 1)
    while surplus > 0:
        movable = [i for i in range(count - 1) if given[i] < most]
        pool, left = sum([loads[i] for i in movable]), surplus
        for i in movable:
            more = min(most - given[i], max(1, left * loads[i] // pool), surplus)
            given[i] = given[i] + more
            surplus = surplus - more
    return np.array([most] + given)


def uneven(own_key, number_of, total, limit, skew):
    if number_of == 2:
        one = jax.random.randint(own_key, (), max(1, total - limit), min(limit, total - 1) + 1)
        return jnp.stack([one, total - one])
    sizes = jnp.asarray(profile(number_of, total, limit, skew), jnp.int32)
    twos = (number_of - 1) // 2
    donor, receiver = sizes[1:1 + 2 * twos:2], sizes[2:2 + 2 * twos:2]
    slack = jnp.minimum(donor - 1, limit - receiver)
    passed = jax.random.randint(jax.random.fold_in(own_key, 1), (twos,), 0, 1 << 20) % (slack + 1)
    sizes = sizes.at[1:1 + 2 * twos:2].set(donor - passed).at[2:2 + 2 * twos:2].set(receiver + passed)
    return sizes[jax.random.permutation(jax.random.fold_in(own_key, 2), number_of)]


def scatter_about(own_key, shape, deviation, limit, pieces=(), kind=jnp.bfloat16):
    drawn = jax.random.normal(own_key, shape, jnp.float32) * deviation
    if len(pieces) > 0:
        drawn = shard_levels(own_key, shape, pieces, -0.22, 0.18) * drawn
    return jnp.clip(drawn, min=-limit, max=limit).astype(kind)


def setup_inputs(seed: int = 0) -> dict:
    seeds = jax.random.split(jax.random.key(seed), 18)
    frames_in = scatter_about(seeds[0], (N_BATCH, N_SEQ, N_FRAMES, TOK_DEV, D), 1.0, 6.0, ((0, 4), (1, 4), (2, 2)))
    skip_in = scatter_about(seeds[1], (N_BATCH, N_SEQ, N_FRAMES, TOK_DEV, D), 1.0, 6.0, ((0, 4), (1, 4), (2, 2)))
    lengths = jax.vmap(lambda own: uneven(own, UTTS, N_SEQ * TOK_DEV - TOK_DEV // 6, 2 * TOK_DEV * N_SEQ // 3, 2))(jax.random.split(seeds[2], N_BATCH * N_FRAMES)).reshape((N_BATCH, N_FRAMES, UTTS)).astype(jnp.int32)
    cotangent = scatter_about(seeds[3], (N_BATCH, N_SEQ, N_FRAMES, TOK_DEV, D), 1.0, 6.0, ((0, 4), (1, 4), (2, 2)))
    w_skip = scatter_about(seeds[4], (2 * D, D), (2 * D) ** -0.5, 0.125, ((0, 2),))
    w_qkv = scatter_about(seeds[5], (D, 3 * D), D ** -0.5, 0.1875, ((0, 2),))
    w_out = scatter_about(seeds[6], (D, D), (D // 8) ** -0.5, 0.5, ((0, 2),))
    w_up = scatter_about(seeds[7], (D, FF), D ** -0.5, 0.1875, ((0, 2),))
    w_down = scatter_about(seeds[8], (FF, D), FF ** -0.5, 0.09375, ((0, 2),))
    skip_bias = scatter_about(seeds[9], (D,), 0.5, 3.0, ((0, 2),))
    norm1_gain = jnp.clip(1.0 + 0.15 * jax.random.normal(seeds[10], (D,), jnp.float32), 0.25, 1.75).astype(jnp.bfloat16)
    norm1_bias = scatter_about(seeds[11], (D,), 0.5, 3.0, ((0, 2),))
    out_bias = scatter_about(seeds[12], (D,), 0.5, 3.0, ((0, 2),))
    norm2_gain = jnp.clip(1.0 + 0.15 * jax.random.normal(seeds[13], (D,), jnp.float32), 0.25, 1.75).astype(jnp.bfloat16)
    norm2_bias = scatter_about(seeds[14], (D,), 0.5, 3.0, ((0, 2),))
    up_bias = scatter_about(seeds[15], (FF,), 0.5, 3.0, ((0, 2),))
    down_bias = scatter_about(seeds[16], (D,), 0.5, 3.0, ((0, 2),))
    return {"frames_in": frames_in, "skip_in": skip_in, "lengths": lengths, "cotangent": cotangent, "w_skip": w_skip, "w_qkv": w_qkv, "w_out": w_out, "w_up": w_up, "w_down": w_down, "skip_bias": skip_bias, "norm1_gain": norm1_gain, "norm1_bias": norm1_bias, "out_bias": out_bias, "norm2_gain": norm2_gain, "norm2_bias": norm2_bias, "up_bias": up_bias, "down_bias": down_bias}


@jax.custom_vjp
def low(v):
    return lax.optimization_barrier(v.astype(jnp.bfloat16)).astype(jnp.float32)

@jax.custom_vjp
def low_back(v):
    return v

def low_keep(v):
    return (low(v), None)

def low_pass(kept, grad):
    return (grad,)

def back_keep(v):
    return (v, None)

def back_low(kept, grad):
    return (low(grad),)
low.defvjp(low_keep, low_pass)
low_back.defvjp(back_keep, back_low)

def layer_norm(values, gain, bias):
    row_mean = lax.optimization_barrier(jnp.mean(values, axis=-1, keepdims=True))
    centred = values - row_mean
    variance = lax.optimization_barrier(jnp.mean(centred * centred, axis=-1, keepdims=True))
    return centred * lax.rsqrt(variance + 1e-05) * gain + bias

def matmul(left_side, right_side):
    return jnp.dot(left_side, right_side, precision=lax.Precision.HIGHEST)

def segment_ids(utt_lengths, count):
    bounds = jnp.cumsum(utt_lengths, dtype=jnp.int32)
    position = jnp.arange(count, dtype=jnp.int32)
    return lax.optimization_barrier(jnp.sum((position[:, None] >= bounds[None, :]).astype(jnp.int32), axis=1, dtype=jnp.int32))

def block_count(length):
    count = max(1, length // 512)
    while length % count:
        count = count - 1
    return count

def attend_block(queries, q_pos, q_seg, key_rows, value_rows, segment, slopes):
    length = key_rows.shape[0]
    k_pos = jnp.arange(length, dtype=jnp.int32)
    raw_dots = jnp.einsum('qhd,khd->hqk', queries, key_rows, precision=lax.Precision.HIGHEST) * HD ** (-0.5)
    distance = jnp.abs(q_pos[:, None] - k_pos[None, :]).astype(jnp.float32)
    scores = low_back(raw_dots - slopes[:, None, None] * distance[None])
    allowed = (q_seg[:, None] == segment[None, :]) & (segment[None, :] < UTTS)
    scores = jnp.where(allowed[None], scores, -1000000000.0)
    attn_prob = low(jax.nn.softmax(scores, axis=-1))
    mixed = jnp.einsum('hqk,khd->qhd', attn_prob, value_rows, precision=lax.Precision.HIGHEST)
    return mixed * (q_seg < UTTS).astype(jnp.float32)[:, None, None]

def group_forward(params, joined, segment, slopes):
    w_skip, w_qkv, w_out, w_up, w_down, skip_bias, norm1_gain, norm1_bias, out_bias, norm2_gain, norm2_bias, up_bias, down_bias = params
    length = joined.shape[0]
    hidden_z = low_back(matmul(joined, w_skip) + skip_bias)
    normed = low(layer_norm(hidden_z, norm1_gain, norm1_bias))
    projected = low(low_back(matmul(normed, w_qkv))).reshape(length, 3, HEADS, HD)
    count = block_count(length)
    rows_block = length // count
    positions = jnp.arange(length, dtype=jnp.int32)
    block_fn = jax.checkpoint(attend_block)
    key_rows = projected[:, 1]
    value_rows = projected[:, 2]

    def one_block(mapped):
        return block_fn(mapped[0], mapped[1], mapped[2], key_rows, value_rows, segment, slopes)
    attended = lax.map(one_block, (projected[:, 0].reshape(count, rows_block, HEADS, HD), positions.reshape(count, rows_block), segment.reshape(count, rows_block)))
    attended = low(low_back(attended.reshape(length, HEADS * HD)))
    branch = low_back(matmul(attended, w_out) + out_bias)
    resid = hidden_z + branch
    normed_two = low(layer_norm(resid, norm2_gain, norm2_bias))
    pre_act = low_back(matmul(normed_two, w_up) + up_bias)
    activ = low(jax.nn.gelu(pre_act, approximate=False))
    return resid + matmul(activ, w_down) + down_bias

def reference(frames_in, skip_in, lengths, cotangent, w_skip, w_qkv, w_out, w_up, w_down, skip_bias, norm1_gain, norm1_bias, out_bias, norm2_gain, norm2_bias, up_bias, down_bias):
    params = tuple((weight.astype(jnp.float32) for weight in (w_skip, w_qkv, w_out, w_up, w_down, skip_bias, norm1_gain, norm1_bias, out_bias, norm2_gain, norm2_bias, up_bias, down_bias)))
    n_batch, n_seq, n_frames, tok_rows, model_width = frames_in.shape
    length = n_seq * tok_rows

    def regroup(array):
        return array.astype(jnp.float32).transpose(0, 2, 1, 3, 4).reshape(n_batch * n_frames, length, model_width)
    slopes = 2.0 ** (-8.0 * jnp.arange(1, HEADS + 1, dtype=jnp.float32) / HEADS)

    def group_step(totals, mapped):
        frames, skips, cotan, utt_lengths = mapped
        segment = segment_ids(utt_lengths, length)
        joined = jnp.concatenate([frames, skips], axis=1)

        def forward(weights, inputs):
            return group_forward(weights, inputs, segment, slopes)
        result, pull_back = jax.vjp(forward, params, joined)
        grad_weights, grad_joined = pull_back(cotan)
        totals = jax.tree.map(jnp.add, totals, grad_weights)
        return (totals, (result, grad_joined))
    zeros_init = tuple((jnp.zeros(weight.shape, jnp.float32) for weight in params))
    totals, (results, grad_joined) = lax.scan(group_step, zeros_init, (regroup(frames_in), regroup(skip_in), regroup(cotangent), lengths.reshape(n_batch * n_frames, UTTS)))

    def ungroup(array):
        return array.reshape(n_batch, n_frames, n_seq, tok_rows, array.shape[-1]).transpose(0, 2, 1, 3, 4)
    output = ungroup(results).astype(jnp.bfloat16)
    input_grad = ungroup(grad_joined[:, :, :model_width])
    skip_grad = ungroup(grad_joined[:, :, model_width:])
    return (output, input_grad, skip_grad, totals[0], totals[1], totals[2], totals[3], totals[4], totals[5], totals[6], totals[7], totals[8], totals[9], totals[10], totals[11], totals[12])
```

```python
import functools

import jax
import jax.numpy as jnp
from jax import lax
from jax.experimental import pallas as pl
from jax.experimental.pallas import tpu as pltpu
from jax.sharding import PartitionSpec as P

HEADS = 16
HD = 64
UTTS = 3
EPS = 1e-05
MASKED = 1e12
BF16 = jnp.bfloat16
F32 = jnp.float32
INV_SQRT2 = 0.7071067811865476
INV_SQRT_2PI = 0.3989422804014327


def contract_rows(left_side, right_side):
    return lax.dot_general(
        left_side, right_side, (((0,), (0,)), ((), ())), preferred_element_type=F32
    )


def times_transposed(left_side, right_side):
    return lax.dot_general(
        left_side, right_side, (((1,), (1,)), ((), ())), preferred_element_type=F32
    )


def times(left_side, right_side):
    return jnp.dot(left_side, right_side, preferred_element_type=F32)


def pair_rows(block, lane):
    zero = jnp.zeros_like(block)
    return jnp.concatenate(
        [jnp.where(lane < HD, block, zero), jnp.where(lane >= HD, block, zero)], axis=0
    )


def attend_forward_kernel(n_seq, meta, q_ref, k_ref, v_ref, slope_ref, out_ref, prob_ref, dist):
    tok = q_ref.shape[0]
    length = k_ref.shape[0]

    @pl.when(pl.program_id(0) == 0)
    def _():
        shard = meta[0]
        row = lax.broadcasted_iota(jnp.int32, (length, 2 * tok), 0)
        col = lax.broadcasted_iota(jnp.int32, (length, 2 * tok), 1)
        k_pos = row + shard * tok
        k_pos = jnp.where(k_pos >= length, k_pos - length, k_pos)
        q_pos = jnp.where(col >= tok, col - tok, col) + shard * tok
        k_seg = jnp.zeros_like(k_pos)
        q_seg = jnp.zeros_like(q_pos)
        for j in range(UTTS):
            k_seg = k_seg + (k_pos >= meta[1 + j]).astype(jnp.int32)
            q_seg = q_seg + (q_pos >= meta[1 + j]).astype(jnp.int32)
        allowed = (k_seg == q_seg) & (k_seg < UTTS)
        dist[...] = jnp.where(allowed, jnp.abs(k_pos - q_pos).astype(F32), MASKED)

    lane = lax.broadcasted_iota(jnp.int32, (tok, 2 * HD), 1)
    pair = pair_rows(q_ref[...] * jnp.asarray(HD**-0.5, BF16), lane)
    scores = times_transposed(k_ref[...], pair) - slope_ref[0] * dist[...]
    top = jnp.max(scores, axis=0, keepdims=True)
    exp_scores = jnp.exp(scores - top)
    total = jnp.sum(exp_scores, axis=0, keepdims=True)
    prob = (exp_scores * (1.0 / total)).astype(BF16)
    prob_ref[0] = prob
    mixed = times(v_ref[...].T, prob).T
    mixed = jnp.where(lane < HD, mixed[:tok], mixed[tok:])
    row = lax.broadcasted_iota(jnp.int32, (tok, 2 * HD), 0) + meta[0] * tok
    out_ref[...] = jnp.where(row < meta[UTTS], mixed, 0.0).astype(BF16)


def attend_backward_kernel(q_ref, k_ref, v_ref, grad_ref, prob_ref, gq_ref, gk_ref, gv_ref):
    tok = q_ref.shape[0]
    lane = lax.broadcasted_iota(jnp.int32, (tok, 2 * HD), 1)
    scale = jnp.asarray(HD**-0.5, BF16)
    pair_q = pair_rows(q_ref[...] * scale, lane)
    pair_g = pair_rows(grad_ref[...], lane)
    prob_low = prob_ref[0]
    prob = prob_low.astype(F32)
    prob_grad = times_transposed(v_ref[...], pair_g)
    weighted = prob * prob_grad
    delta = jnp.sum(weighted, axis=0, keepdims=True)
    score_low = (weighted - prob * delta).astype(BF16)
    gv_ref[...] = times(prob_low, pair_g).astype(BF16)
    gk_ref[...] = times(score_low, pair_q).astype(BF16)
    mixed = times((k_ref[...] * scale).T, score_low).T
    gq_ref[...] = jnp.where(lane < HD, mixed[:tok], mixed[tok:]).astype(BF16)


def attend_forward(meta, queries, key_rows, value_rows, slopes, n_seq):
    tok, width = queries.shape
    length = key_rows.shape[0]
    pairs = width // (2 * HD)
    return pl.pallas_call(
        functools.partial(attend_forward_kernel, n_seq),
        grid_spec=pltpu.PrefetchScalarGridSpec(
            num_scalar_prefetch=1,
            grid=(pairs,),
            in_specs=[
                pl.BlockSpec((tok, 2 * HD), lambda g, m: (0, g)),
                pl.BlockSpec((length, 2 * HD), lambda g, m: (0, g)),
                pl.BlockSpec((length, 2 * HD), lambda g, m: (0, g)),
                pl.BlockSpec((1, 1, 2 * tok), lambda g, m: (g, 0, 0)),
            ],
            out_specs=[
                pl.BlockSpec((tok, 2 * HD), lambda g, m: (0, g)),
                pl.BlockSpec((1, length, 2 * tok), lambda g, m: (g, 0, 0)),
            ],
            scratch_shapes=[pltpu.VMEM((length, 2 * tok), F32)],
        ),
        out_shape=[
            jax.ShapeDtypeStruct((tok, width), BF16),
            jax.ShapeDtypeStruct((pairs, length, 2 * tok), BF16),
        ],
        cost_estimate=pl.CostEstimate(
            flops=8 * tok * length * width * 2,
            bytes_accessed=4 * length * width + pairs * length * tok * 4,
            transcendentals=tok * length * HEADS,
        ),
        name="attend_forward",
    )(meta, queries, key_rows, value_rows, slopes)


def attend_backward(queries, key_rows, value_rows, grad_heads, prob):
    tok, width = queries.shape
    length = key_rows.shape[0]
    pairs = width // (2 * HD)
    q_spec = pl.BlockSpec((tok, 2 * HD), lambda g: (0, g))
    k_spec = pl.BlockSpec((length, 2 * HD), lambda g: (0, g))
    return pl.pallas_call(
        attend_backward_kernel,
        grid=(pairs,),
        in_specs=[
            q_spec,
            k_spec,
            k_spec,
            q_spec,
            pl.BlockSpec((1, length, 2 * tok), lambda g: (g, 0, 0)),
        ],
        out_specs=[q_spec, k_spec, k_spec],
        out_shape=[
            jax.ShapeDtypeStruct((tok, width), BF16),
            jax.ShapeDtypeStruct((length, width), BF16),
            jax.ShapeDtypeStruct((length, width), BF16),
        ],
        cost_estimate=pl.CostEstimate(
            flops=16 * tok * length * width * 2,
            bytes_accessed=8 * length * width + pairs * length * tok * 4,
            transcendentals=0,
        ),
        name="attend_backward",
    )(queries, key_rows, value_rows, grad_heads, prob)


def middle_kernel(n_pieces, *refs):
    n2_refs = refs[:n_pieces]
    w_refs = refs[n_pieces : 2 * n_pieces]
    bias_ref, gact_ref = refs[2 * n_pieces : 2 * n_pieces + 2]
    act_ref, gup_ref = refs[2 * n_pieces + 2 : 2 * n_pieces + 4]
    gn2_refs = refs[2 * n_pieces + 4 :]
    pre = bias_ref[...]
    for n2_ref, w_ref in zip(n2_refs, w_refs):
        pre = pre + times(n2_ref[...], w_ref[...])
    cdf = 0.5 + 0.5 * lax.erf(pre * INV_SQRT2)
    pdf = jnp.exp(pre * pre * (-0.5)) * INV_SQRT_2PI
    act_ref[...] = (pre * cdf).astype(BF16)
    gup = (gact_ref[...] * (cdf + pre * pdf)).astype(BF16)
    gup_ref[...] = gup
    first = pl.program_id(0) == 0
    for gn2_ref, w_ref in zip(gn2_refs, w_refs):
        term = times_transposed(gup, w_ref[...])

        @pl.when(first)
        def _():
            gn2_ref[...] = term

        @pl.when(jnp.logical_not(first))
        def _():
            gn2_ref[...] += term


def middle(n2_pieces, w_pieces, up_bias, gact, tile=512):
    tok = gact.shape[0]
    hidden = gact.shape[1]
    rows = [w.shape[0] for w in w_pieces]
    n = len(w_pieces)
    return pl.pallas_call(
        functools.partial(middle_kernel, n),
        grid=(hidden // tile,),
        in_specs=[pl.BlockSpec((tok, r), lambda t: (0, 0)) for r in rows]
        + [pl.BlockSpec((r, tile), lambda t: (0, t)) for r in rows]
        + [pl.BlockSpec((1, tile), lambda t: (0, t)), pl.BlockSpec((tok, tile), lambda t: (0, t))],
        out_specs=[pl.BlockSpec((tok, tile), lambda t: (0, t))] * 2
        + [pl.BlockSpec((tok, r), lambda t: (0, 0)) for r in rows],
        out_shape=[jax.ShapeDtypeStruct((tok, hidden), BF16)] * 2
        + [jax.ShapeDtypeStruct((tok, r), F32) for r in rows],
        cost_estimate=pl.CostEstimate(
            flops=4 * tok * hidden * sum(rows),
            bytes_accessed=2 * hidden * sum(rows) + 8 * tok * hidden,
            transcendentals=2 * tok * hidden,
        ),
        name="middle",
    )(*n2_pieces, *w_pieces, up_bias, gact)


def place_kernel(places, meta, own, by_x, by_y, far_low, far_high, *outs):
    plane = meta[1]
    lower = pl.program_id(0) < pl.num_programs(0) // 2

    def put(ref, index):
        start = 0
        for width, out, base in places:
            at = pl.multiple_of(base + index * width, 128)
            outs[out][:, pl.ds(at, width)] = ref[:, start : start + width].astype(F32)
            start = start + width

    put(own, plane)
    put(by_x, plane ^ 1)
    put(by_y, plane ^ 2)

    @pl.when(lower)
    def _():
        put(far_low, plane ^ 3)

    @pl.when(jnp.logical_not(lower))
    def _():
        put(far_high, plane ^ 3)


def place(meta, parts, places, out_widths, n_seq):
    rows, width = parts[0].shape
    block = rows // n_seq
    half = n_seq // 2
    whole = pl.BlockSpec((block, width), lambda j, m: (j, 0))
    low = pl.BlockSpec((block, width), lambda j, m: (jnp.minimum(j, half - 1), 0))
    high = pl.BlockSpec((block, width), lambda j, m: (jnp.maximum(j - half, 0), 0))
    return pl.pallas_call(
        functools.partial(place_kernel, places),
        grid_spec=pltpu.PrefetchScalarGridSpec(
            num_scalar_prefetch=1,
            grid=(n_seq,),
            in_specs=[whole, whole, whole, low, high],
            out_specs=[
                pl.BlockSpec((block, w), lambda j, m: (lax.rem(j + m[0], n_seq), 0))
                for w in out_widths
            ],
        ),
        out_shape=[jax.ShapeDtypeStruct((rows, w), F32) for w in out_widths],
        cost_estimate=pl.CostEstimate(
            flops=0, bytes_accessed=rows * sum(out_widths) * 6, transcendentals=0
        ),
        name="place",
    )(meta, *parts)


def body(
    frames_in,
    skip_in,
    lengths,
    cotangent,
    w_skip,
    w_qkv,
    w_out,
    w_up,
    w_down,
    skip_bias,
    norm1_gain,
    norm1_bias,
    out_bias,
    norm2_gain,
    norm2_bias,
    up_bias,
    down_bias,
):
    tok = frames_in.shape[3]
    width = frames_in.shape[4]
    frames = frames_in.reshape(tok, width)
    skips = skip_in.reshape(tok, width)
    cotan = cotangent.reshape(tok, width)
    n_batch = lax.axis_size("batch")
    n_seq = lax.axis_size("seq")
    n_frames = lax.axis_size("frames")
    assert n_batch == 4 and n_seq % 2 == 0
    paired = n_frames == 2
    plane = lax.axis_index("batch")
    shard = lax.axis_index("seq")
    core = lax.axis_index("frames")

    def over_frames(array):
        return lax.ppermute(array, "frames", [(0, 1), (1, 0)])

    def over_batch(array, bit):
        return lax.ppermute(array, "batch", [(i, i ^ bit) for i in range(n_batch)])

    def to_seq(array, step):
        return lax.ppermute(array, "seq", [(i, (i + step) % n_seq) for i in range(n_seq)])

    def from_seq(array, step):
        return lax.ppermute(array, "seq", [((i + step) % n_seq, i) for i in range(n_seq)])

    def after(array, *others):
        return lax.optimization_barrier((array, *others))[0]

    def gathered(weight):
        if paired:
            return [weight, over_frames(weight)]
        return [lax.all_gather(weight, "frames", axis=0, tiled=True)]

    def columns(array):
        if not paired:
            return [array]
        half = array.shape[1] // 2
        return [
            lax.dynamic_slice_in_dim(array, core * half, half, 1),
            lax.dynamic_slice_in_dim(array, (1 - core) * half, half, 1),
        ]

    def ordered(pieces, axis=1):
        if not paired:
            return pieces[0]
        own, other = pieces
        return jnp.where(
            core == 0,
            jnp.concatenate([own, other], axis=axis),
            jnp.concatenate([other, own], axis=axis),
        )

    def product(pieces, weights):
        total = times(pieces[0], weights[0])
        for piece, weight in zip(pieces[1:], weights[1:]):
            total = total + times(piece, weight)
        return total

    def back_product(array, weights):
        return [times_transposed(array, weight) for weight in weights]

    def left_rows(array):
        if paired:
            own, other = columns(array)
            return jnp.concatenate([own, over_frames(other)], axis=0)
        split = array.reshape(tok_of(array), n_frames, array.shape[1] // n_frames)
        moved = lax.all_to_all(split, "frames", split_axis=1, concat_axis=0, tiled=True)
        return moved.reshape(array.shape[0] * n_frames, array.shape[1] // n_frames)

    def tok_of(array):
        return array.shape[0]

    def right_rows(array):
        if paired:
            return jnp.concatenate([array, over_frames(array)], axis=0)
        return lax.all_gather(array, "frames", axis=0, tiled=True)

    def by_shard(left):
        block = left.shape[1] // n_seq
        return lax.dynamic_slice_in_dim(
            jnp.concatenate([left, left], axis=1), shard * block, left.shape[1], 1
        )

    def by_plane(right):
        block = right.shape[1] // n_batch
        return jnp.concatenate(
            [
                lax.dynamic_slice_in_dim(right, (plane ^ bits) * block, block, 1)
                for bits in (0, 1, 3, 2)
            ],
            axis=1,
        )

    def joined_send(arrays, move):
        sizes = [a.shape[1] for a in arrays]
        moved = move(jnp.concatenate(arrays, axis=1) if len(arrays) > 1 else arrays[0])
        if len(arrays) == 1:
            return [moved]
        ends = [sum(sizes[: i + 1]) for i in range(len(sizes))]
        return [moved[:, e - s : e] for e, s in zip(ends, sizes)]

    def summed_over_groups(terms):
        terms = [(by_shard(left), by_plane(right)) for left, right in terms]
        rows = terms[0][0].shape[1]
        half = rows // 2

        def gemm(low, high, first, last):
            outs = []
            for left, right in terms:
                block = right.shape[1] // n_batch
                outs.append(
                    contract_rows(left[:, low:high], right[:, first * block : last * block])
                )
            return outs

        low_x = [g.astype(BF16) for g in gemm(0, half, 1, 3)]
        high_y = [g.astype(BF16) for g in gemm(half, rows, 2, 4)]
        from_x = joined_send(low_x, lambda a: over_batch(a, 1))
        from_y = joined_send(high_y, lambda a: over_batch(a, 2))
        low_y = [
            (g + r[:, g.shape[1] :].astype(F32)).astype(BF16)
            for g, r in zip(gemm(0, half, 3, 4), from_x)
        ]
        high_x = [
            (g + r[:, : g.shape[1]].astype(F32)).astype(BF16)
            for g, r in zip(gemm(half, rows, 1, 2), from_y)
        ]
        then_y = joined_send(low_y, lambda a: over_batch(a, 2))
        then_x = joined_send(high_x, lambda a: over_batch(a, 1))
        own = []
        for g, fx, fy, ty, tx in zip(gemm(0, rows, 0, 1), from_x, from_y, then_y, then_x):
            n = g.shape[1]
            low = fx[:, :n].astype(F32) + ty.astype(F32)
            high = fy[:, n:].astype(F32) + tx.astype(F32)
            own.append(g + jnp.concatenate([low, high], axis=0))
        own = jnp.concatenate(own, axis=1) if len(own) > 1 else own[0]
        block = rows // n_seq
        total = own[:block]
        for j in range(1, n_seq):
            sent = own[j * block : (j + 1) * block].astype(BF16)
            total = total + to_seq(sent, j).astype(F32)
        total = total.astype(BF16)
        whole = jnp.concatenate(
            [total] + [from_seq(total, j) for j in range(1, n_seq)], axis=0
        )
        by_x = over_batch(whole, 1)
        by_y = over_batch(whole, 2)
        far_low = over_batch(by_y[:half], 1)
        far_high = over_batch(by_x[half:], 2)
        return whole, by_x, by_y, far_low, far_high

    vectors_in = (
        skip_bias,
        norm1_gain,
        norm1_bias,
        out_bias,
        norm2_gain,
        norm2_bias,
        up_bias,
        down_bias,
    )
    sizes = [v.shape[0] for v in vectors_in]
    packed = jnp.concatenate(vectors_in).reshape(1, -1)
    if paired:
        other = over_frames(packed)
        packed = jnp.where(
            core == 0,
            jnp.concatenate([packed, other], axis=0),
            jnp.concatenate([other, packed], axis=0),
        )
    else:
        packed = lax.all_gather(packed, "frames", axis=0, tiled=True)
    packed = packed.astype(F32)
    starts = [sum(sizes[:i]) for i in range(len(sizes))]
    sbias, gain1, bias1, obias, gain2, bias2, ubias, dbias = [
        packed[:, b : b + n].reshape(1, -1) for b, n in zip(starts, sizes)
    ]
    full_skip = gathered(w_skip)
    full_qkv = gathered(after(w_qkv, full_skip[-1]))
    full_down = gathered(after(w_down, full_qkv[-1]))
    full_out = gathered(after(w_out, full_down[-1]))
    full_up = gathered(after(w_up, full_out[-1]))

    joined = [frames, skips] if paired else [jnp.concatenate([frames, skips], axis=1)]
    if paired:
        inputs = [jnp.where(core == 0, frames, skips), jnp.where(core == 0, skips, frames)]
    else:
        inputs = joined
    hidden_z = product(inputs, full_skip) + sbias

    def statistics(values):
        mean = jnp.mean(values, axis=-1, keepdims=True)
        centred = values - mean
        variance = jnp.mean(centred * centred, axis=-1, keepdims=True)
        return mean, lax.rsqrt(variance + EPS)

    mean1, rstd1 = statistics(hidden_z)
    unit1 = (hidden_z - mean1) * rstd1
    n1 = (unit1 * gain1 + bias1).astype(BF16)
    n1_all = [n1] + [from_seq(n1, j) for j in range(1, n_seq)]
    w_q = [w[:, :width] for w in full_qkv]
    w_kv = [w[:, width:] for w in full_qkv]
    qkv_own = product(columns(n1), full_qkv).astype(BF16)
    n1_rest = jnp.concatenate(n1_all[1:], axis=0)
    kv_rest = product(columns(n1_rest), w_kv).astype(BF16)
    queries = qkv_own[:, :width]
    key_rows = jnp.concatenate([qkv_own[:, width : 2 * width], kv_rest[:, :width]], axis=0)
    value_rows = jnp.concatenate([qkv_own[:, 2 * width :], kv_rest[:, width:]], axis=0)
    gact = ordered(back_product(cotan, full_down))
    bounds = jnp.cumsum(lengths.reshape(-1), dtype=jnp.int32)
    meta = jnp.concatenate([shard.astype(jnp.int32).reshape(1), bounds])
    slopes = 2.0 ** (-8.0 * jnp.arange(1, HEADS + 1, dtype=F32) / HEADS)
    slopes = jnp.repeat(slopes, tok).reshape(HEADS // 2, 1, 2 * tok)
    attended, prob = attend_forward(meta, queries, key_rows, value_rows, slopes, n_seq)
    resid = hidden_z + product(columns(attended), full_out) + obias
    mean2, rstd2 = statistics(resid)
    unit2 = (resid - mean2) * rstd2
    n2 = (unit2 * gain2 + bias2).astype(BF16)
    activ, gup, *gn2 = middle(columns(n2), full_up, ubias, gact)
    gn2 = ordered(gn2)
    output = resid + product(columns(activ), full_down) + dbias

    def norm_back(unit, rstd, gain, grad):
        scaled = grad * gain
        mean_e = jnp.mean(scaled, axis=-1, keepdims=True)
        mean_eu = jnp.mean(scaled * unit, axis=-1, keepdims=True)
        return rstd * (scaled - mean_e - unit * mean_eu)

    grad_resid = cotan.astype(F32) + norm_back(unit2, rstd2, gain2, gn2)
    grad_branch = grad_resid.astype(BF16)
    row = lax.broadcasted_iota(jnp.int32, (tok, 1), 0) + shard * tok
    live = row < bounds[UTTS - 1]
    grad_heads = jnp.where(live, ordered(back_product(grad_branch, full_out)), 0.0).astype(BF16)
    gq, gk, gv = attend_backward(queries, key_rows, value_rows, grad_heads, prob)
    gkv = jnp.concatenate([gk, gv], axis=1)
    gn1_rest = ordered(back_product(gkv[tok:], w_kv)).astype(BF16)
    gn1 = ordered(
        [a + b for a, b in zip(back_product(gkv[:tok], w_kv), back_product(gq, w_q))]
    )
    for j in range(1, n_seq):
        gn1 = gn1 + to_seq(gn1_rest[(j - 1) * tok : j * tok], j).astype(F32)
    grad_z = (grad_resid + norm_back(unit1, rstd1, gain1, gn1)).astype(BF16)
    pieces = back_product(grad_z, full_skip)
    if paired:
        input_grad = jnp.where(core == 0, pieces[0], pieces[1])
        skip_grad = jnp.where(core == 0, pieces[1], pieces[0])
    else:
        input_grad, skip_grad = pieces[0][:, :width], pieces[0][:, width:]

    both_cotan = right_rows(cotan)
    parts_down = summed_over_groups([(left_rows(activ), both_cotan)])
    parts_up = summed_over_groups(
        [(left_rows(n2), right_rows(gup)), (left_rows(attended), right_rows(grad_branch))]
    )
    left_n1 = left_rows(jnp.concatenate(n1_all, axis=0))
    parts_qkv = summed_over_groups(
        [(left_rows(n1), right_rows(gq)), (left_n1, right_rows(gkv))]
    )
    if paired:
        left_joined = jnp.concatenate([inputs[0], over_frames(inputs[1])], axis=0)
    else:
        left_joined = left_rows(joined[0])
    parts_skip = summed_over_groups([(left_joined, right_rows(grad_z))])
    where = jnp.stack([shard.astype(jnp.int32), plane.astype(jnp.int32)])
    hidden = w_up.shape[1]
    n_b = n_batch
    (grad_w_down,) = place(where, parts_down, ((width // n_b, 0, 0),), (width,), n_seq)
    grad_w_up, grad_w_out = place(
        where,
        parts_up,
        ((hidden // n_b, 0, 0), (width // n_b, 1, 0)),
        (hidden, width),
        n_seq,
    )
    (grad_w_qkv,) = place(
        where,
        parts_qkv,
        ((width // n_b, 0, 0), (2 * width // n_b, 0, width)),
        (3 * width,),
        n_seq,
    )
    (grad_w_skip,) = place(where, parts_skip, ((width // n_b, 0, 0),), (width,), n_seq)

    vectors = (
        jnp.sum(grad_z, axis=0, dtype=F32),
        jnp.sum(unit1 * gn1, axis=0),
        jnp.sum(gn1, axis=0),
        jnp.sum(grad_branch, axis=0, dtype=F32),
        jnp.sum(unit2 * gn2, axis=0),
        jnp.sum(gn2, axis=0),
        jnp.sum(gup, axis=0, dtype=F32),
        jnp.sum(cotan, axis=0, dtype=F32),
    )
    stacked = jnp.concatenate([v.reshape(n_frames, -1) for v in vectors], axis=1)
    if paired:
        mine = lax.dynamic_slice_in_dim(stacked, core, 1, 0)
        theirs = lax.dynamic_slice_in_dim(stacked, 1 - core, 1, 0)
        mine = mine + over_frames(theirs)
    else:
        mine = lax.psum_scatter(stacked, "frames", scatter_dimension=0, tiled=True)
    mine = mine + over_batch(mine, 1)
    mine = mine + over_batch(mine, 2)
    total = mine
    for j in range(1, n_seq):
        total = total + from_seq(mine, j)
    total = total.reshape(-1)
    vector_grads = [total[b : b + n] for b, n in zip(starts, sizes)]

    def back(array):
        return array.reshape(1, 1, 1, tok, width)

    return (
        back(output.astype(BF16)),
        back(input_grad),
        back(skip_grad),
        grad_w_skip,
        grad_w_qkv,
        grad_w_out,
        grad_w_up,
        grad_w_down,
        *vector_grads,
    )


def solution(mesh):
    rows = P("batch", "seq", "frames", None, None)
    in_specs = (
        (rows, rows, P("batch", "frames", None), rows)
        + (P("frames", None),) * 5
        + (P("frames"),) * 8
    )
    out_specs = (rows,) * 3 + (P("frames", None),) * 5 + (P("frames"),) * 8
    return jax.shard_map(body, mesh=mesh, in_specs=in_specs, out_specs=out_specs, check_vma=False)
```

```python
import functools

import jax
import jax.numpy as jnp
from jax import lax
from jax.experimental import pallas as pl
from jax.experimental.pallas import tpu as pltpu
from jax.sharding import PartitionSpec as P

HEADS = 16
HD = 64
UTTS = 3
EPS = 1e-05
MASKED = 1e12
BF16 = jnp.bfloat16
F32 = jnp.float32
INV_SQRT2 = 0.7071067811865476
INV_SQRT_2PI = 0.3989422804014327
ERFC_STEP = 0.4
ERFC_TERMS = (
    0.22567586186829244 / 2,
    0.22566960544571626 / 2,
    0.20784251123900896 / 2,
    0.16854379658168633 / 2,
    0.14142295790506823 / 2,
    -0.005586494604590357 / 2,
    0.16905696704198306 / 2,
    -0.18288169574958996 / 2,
    0.05025661354969599 / 2,
)


def contract_rows(left_side, right_side):
    return lax.dot_general(
        left_side, right_side, (((0,), (0,)), ((), ())), preferred_element_type=F32
    )


def times_transposed(left_side, right_side):
    return lax.dot_general(
        left_side, right_side, (((1,), (1,)), ((), ())), preferred_element_type=F32
    )


def times(left_side, right_side):
    return jnp.dot(left_side, right_side, preferred_element_type=F32)


def pair_rows(block, lane):
    zero = jnp.zeros_like(block)
    return jnp.concatenate(
        [jnp.where(lane < HD, block, zero), jnp.where(lane >= HD, block, zero)], axis=0
    )


def attend_forward_kernel(n_seq, meta, q_ref, k_ref, v_ref, slope_ref, out_ref, prob_ref, dist):
    tok = q_ref.shape[0]
    length = k_ref.shape[0]

    @pl.when(pl.program_id(0) == 0)
    def _():
        shard = meta[0]
        row = lax.broadcasted_iota(jnp.int32, (length, 2 * tok), 0)
        col = lax.broadcasted_iota(jnp.int32, (length, 2 * tok), 1)
        k_pos = row + shard * tok
        k_pos = jnp.where(k_pos >= length, k_pos - length, k_pos)
        q_pos = jnp.where(col >= tok, col - tok, col) + shard * tok
        k_seg = jnp.zeros_like(k_pos)
        q_seg = jnp.zeros_like(q_pos)
        for j in range(UTTS):
            k_seg = k_seg + (k_pos >= meta[1 + j]).astype(jnp.int32)
            q_seg = q_seg + (q_pos >= meta[1 + j]).astype(jnp.int32)
        allowed = (k_seg == q_seg) & (k_seg < UTTS)
        dist[...] = jnp.where(allowed, jnp.abs(k_pos - q_pos).astype(F32), MASKED)

    lane = lax.broadcasted_iota(jnp.int32, (tok, 2 * HD), 1)
    pair = pair_rows(q_ref[...] * jnp.asarray(HD**-0.5, BF16), lane)
    scores = times_transposed(k_ref[...], pair) - slope_ref[0] * dist[...]
    top = jnp.max(scores, axis=0, keepdims=True)
    exp_scores = jnp.exp(scores - top)
    total = jnp.sum(exp_scores, axis=0, keepdims=True)
    prob = (exp_scores * (1.0 / total)).astype(BF16)
    prob_ref[0] = prob
    mixed = times(v_ref[...].T, prob).T
    mixed = jnp.where(lane < HD, mixed[:tok], mixed[tok:])
    row = lax.broadcasted_iota(jnp.int32, (tok, 2 * HD), 0) + meta[0] * tok
    out_ref[...] = jnp.where(row < meta[UTTS], mixed, 0.0).astype(BF16)


def attend_backward_kernel(q_ref, k_ref, v_ref, grad_ref, prob_ref, gq_ref, gkv_ref):
    tok = q_ref.shape[0]
    lane = lax.broadcasted_iota(jnp.int32, (tok, 2 * HD), 1)
    scale = jnp.asarray(HD**-0.5, BF16)
    pair_q = pair_rows(q_ref[...] * scale, lane)
    pair_g = pair_rows(grad_ref[...], lane)
    prob_low = prob_ref[0]
    prob = prob_low.astype(F32)
    prob_grad = times_transposed(v_ref[...], pair_g)
    weighted = prob * prob_grad
    delta = jnp.sum(weighted, axis=0, keepdims=True)
    score_low = (weighted - prob * delta).astype(BF16)
    gkv_ref[1] = times(prob_low, pair_g).astype(BF16)
    gkv_ref[0] = times(score_low, pair_q).astype(BF16)
    mixed = times((k_ref[...] * scale).T, score_low).T
    gq_ref[...] = jnp.where(lane < HD, mixed[:tok], mixed[tok:]).astype(BF16)


def attend_forward(meta, queries, key_rows, value_rows, slopes, n_seq):
    tok, width = queries.shape
    length = key_rows.shape[0]
    pairs = width // (2 * HD)
    return pl.pallas_call(
        functools.partial(attend_forward_kernel, n_seq),
        grid_spec=pltpu.PrefetchScalarGridSpec(
            num_scalar_prefetch=1,
            grid=(pairs,),
            in_specs=[
                pl.BlockSpec((tok, 2 * HD), lambda g, m: (0, g)),
                pl.BlockSpec((length, 2 * HD), lambda g, m: (0, g)),
                pl.BlockSpec((length, 2 * HD), lambda g, m: (0, g)),
                pl.BlockSpec((1, 1, 2 * tok), lambda g, m: (g, 0, 0)),
            ],
            out_specs=[
                pl.BlockSpec((tok, 2 * HD), lambda g, m: (0, g)),
                pl.BlockSpec((1, length, 2 * tok), lambda g, m: (g, 0, 0)),
            ],
            scratch_shapes=[pltpu.VMEM((length, 2 * tok), F32)],
        ),
        out_shape=[
            jax.ShapeDtypeStruct((tok, width), BF16),
            jax.ShapeDtypeStruct((pairs, length, 2 * tok), BF16),
        ],
        cost_estimate=pl.CostEstimate(
            flops=8 * tok * length * width * 2,
            bytes_accessed=4 * length * width + pairs * length * tok * 4,
            transcendentals=tok * length * HEADS,
        ),
        name="attend_forward",
    )(meta, queries, key_rows, value_rows, slopes)


def attend_backward(queries, key_rows, value_rows, grad_heads, prob):
    tok, width = queries.shape
    length = key_rows.shape[0]
    pairs = width // (2 * HD)
    q_spec = pl.BlockSpec((tok, 2 * HD), lambda g: (0, g))
    k_spec = pl.BlockSpec((length, 2 * HD), lambda g: (0, g))
    return pl.pallas_call(
        attend_backward_kernel,
        grid=(pairs,),
        in_specs=[
            q_spec,
            k_spec,
            k_spec,
            q_spec,
            pl.BlockSpec((1, length, 2 * tok), lambda g: (g, 0, 0)),
        ],
        out_specs=[q_spec, pl.BlockSpec((2, length, 2 * HD), lambda g: (0, 0, g))],
        out_shape=[
            jax.ShapeDtypeStruct((tok, width), BF16),
            jax.ShapeDtypeStruct((2, length, width), BF16),
        ],
        cost_estimate=pl.CostEstimate(
            flops=16 * tok * length * width * 2,
            bytes_accessed=8 * length * width + pairs * length * tok * 4,
            transcendentals=0,
        ),
        name="attend_backward",
    )(queries, key_rows, value_rows, grad_heads, prob)


def statistics(values):
    mean = jnp.mean(values, axis=-1, keepdims=True)
    centred = values - mean
    variance = jnp.mean(centred * centred, axis=-1, keepdims=True)
    return centred, lax.rsqrt(variance + EPS)


def norm_back(unit, rstd, gain, grad):
    scaled = grad * gain
    mean_e = jnp.mean(scaled, axis=-1, keepdims=True)
    mean_eu = jnp.mean(scaled * unit, axis=-1, keepdims=True)
    return rstd * (scaled - mean_e - unit * mean_eu)


def bases(core, n_pieces, rows):
    if n_pieces == 1:
        return [0]
    return [pl.multiple_of(core * rows, 128), pl.multiple_of((1 - core) * rows, 128)]


def front_kernel(n, *refs):
    x_refs, w_refs = refs[:n], refs[n : 2 * n]
    bias, gain, shift, z_ref, n1_ref = refs[2 * n :]
    step = pl.program_id(0)
    part = times(x_refs[0][...], w_refs[0][...])
    for x_ref, w_ref in zip(x_refs[1:], w_refs[1:]):
        part = part + times(x_ref[...], w_ref[...])

    @pl.when(step == 0)
    def _():
        z_ref[...] = part + bias[...]

    @pl.when(step > 0)
    def _():
        z_ref[...] += part

    @pl.when(step == pl.num_programs(0) - 1)
    def _():
        centred, rstd = statistics(z_ref[...])
        n1_ref[...] = (centred * rstd * gain[...] + shift[...]).astype(BF16)


def front(inputs, weights, bias, gain, shift):
    tok = inputs[0].shape[0]
    rows, width = weights[0].shape
    n = len(weights)
    steps = 4
    block = rows // steps
    vector = pl.BlockSpec((1, width), lambda k: (0, 0))
    whole = pl.BlockSpec((tok, width), lambda k: (0, 0))
    return pl.pallas_call(
        functools.partial(front_kernel, n),
        grid=(steps,),
        in_specs=[pl.BlockSpec((tok, block), lambda k: (0, k))] * n
        + [pl.BlockSpec((block, width), lambda k: (k, 0))] * n
        + [vector] * 3,
        out_specs=[whole, whole],
        out_shape=[
            jax.ShapeDtypeStruct((tok, width), F32),
            jax.ShapeDtypeStruct((tok, width), BF16),
        ],
        name="front",
    )(*inputs, *weights, bias, gain, shift)


def project_kernel(n, chunks, meta, *refs):
    x_refs = refs[:chunks]
    w_refs = refs[chunks : chunks + 3 * n]
    q_ref, k_ref, v_ref = refs[chunks + 3 * n :]
    rows = w_refs[0].shape[0]
    tok = q_ref.shape[0]
    starts = bases(meta[0], n, rows)
    for c in range(chunks):
        for i, out in enumerate((q_ref, k_ref, v_ref)):
            if i == 0 and c > 0:
                continue
            total = None
            for p, start in enumerate(starts):
                term = times(x_refs[c][:, pl.ds(start, rows)], w_refs[3 * p + i][...])
                total = term if total is None else total + term
            out[c * tok : (c + 1) * tok] = total.astype(BF16)


def project(meta, chunks, weights):
    tok, width = chunks[0].shape
    rows = weights[0].shape[0]
    n = len(weights)
    tile = 256
    tiles = width // tile

    def w_spec(i):
        return pl.BlockSpec((rows, tile), lambda t, m: (0, t + i * tiles))

    length = tok * len(chunks)
    return pl.pallas_call(
        functools.partial(project_kernel, n, len(chunks)),
        grid_spec=pltpu.PrefetchScalarGridSpec(
            num_scalar_prefetch=1,
            grid=(tiles,),
            in_specs=[pl.BlockSpec((tok, width), lambda t, m: (0, 0))] * len(chunks)
            + [w_spec(i) for i in range(3)] * n,
            out_specs=[
                pl.BlockSpec((tok, tile), lambda t, m: (0, t)),
                pl.BlockSpec((length, tile), lambda t, m: (0, t)),
                pl.BlockSpec((length, tile), lambda t, m: (0, t)),
            ],
        ),
        out_shape=[
            jax.ShapeDtypeStruct((tok, width), BF16),
            jax.ShapeDtypeStruct((length, width), BF16),
            jax.ShapeDtypeStruct((length, width), BF16),
        ],
        name="project",
    )(meta, *chunks, *[w for w in weights for _ in range(3)])


def centre_kernel(n, meta, *refs):
    refs = list(refs)

    def take(count):
        taken = refs[:count]
        del refs[:count]
        return taken

    att, z_ref, cotan = take(3)
    w_out, w_up, gact = take(n), take(n), take(n)
    up_bias, out_bias, gain, shift = take(4)
    resid, n2, act, gup_ref, gres, gbranch, gatt, up_sum, sums = take(9)
    gn2, unit, rstd = refs
    core, live = meta[0], meta[1]
    step, steps = pl.program_id(0), pl.num_programs(0)
    tok = att.shape[0]
    rows = w_out[0].shape[0]
    starts = bases(core, n, rows)

    @pl.when(step == 0)
    def _():
        total = z_ref[...] + out_bias[...]
        for start, w_ref in zip(starts, w_out):
            total = total + times(att[:, pl.ds(start, rows)], w_ref[...])
        resid[...] = total
        centred, scale = statistics(total)
        unit[...] = centred * scale
        rstd[...] = scale
        n2[...] = (unit[...] * gain[...] + shift[...]).astype(BF16)
        gn2[...] = jnp.zeros_like(gn2)

    pre = up_bias[...]
    for start, w_ref in zip(starts, w_up):
        pre = pre + times(n2[:, pl.ds(start, rows)], w_ref[...])
    gauss = jnp.exp(pre * pre * (-0.5))
    t = 1.0 / (1.0 + (ERFC_STEP * INV_SQRT2) * jnp.abs(pre))
    tail = jnp.full_like(t, ERFC_TERMS[-1])
    for term in ERFC_TERMS[-2::-1]:
        tail = tail * t + term
    tail = tail * t * gauss
    cdf = jnp.where(pre < 0.0, tail, 1.0 - tail)
    act[...] = (pre * cdf).astype(BF16)
    if n == 1:
        grad = gact[0][...]
    else:
        mine = (step // (steps // 2)) == core
        grad = jnp.where(mine, gact[0][...], gact[1][...])
    gup = (grad * (cdf + pre * gauss * INV_SQRT_2PI)).astype(BF16)
    gup_ref[...] = gup
    up_sum[...] = jnp.sum(gup.astype(F32), axis=0, keepdims=True)
    for start, w_ref in zip(starts, w_up):
        gn2[:, pl.ds(start, rows)] += times_transposed(gup, w_ref[...])

    @pl.when(step == steps - 1)
    def _():
        grad_n2 = gn2[...]
        total = cotan[...].astype(F32) + norm_back(unit[...], rstd[...], gain[...], grad_n2)
        gres[...] = total
        low = total.astype(BF16)
        gbranch[...] = low
        alive = lax.broadcasted_iota(jnp.int32, (tok, 1), 0) < live
        for start, w_ref in zip(starts, w_out):
            term = times_transposed(low, w_ref[...])
            gatt[:, pl.ds(start, rows)] = jnp.where(alive, term, 0.0).astype(BF16)
        sums[0:1] = jnp.sum(low.astype(F32), axis=0, keepdims=True)
        sums[1:2] = jnp.sum(unit[...] * grad_n2, axis=0, keepdims=True)
        sums[2:3] = jnp.sum(grad_n2, axis=0, keepdims=True)


def centre(meta, att, z, cotan, w_out, w_up, gact, up_bias, out_bias, gain, shift, tile=512):
    tok, width = att.shape
    n = len(w_out)
    rows = w_out[0].shape[0]
    hidden = w_up[0].shape[1]
    steps = hidden // tile
    per = steps // n
    whole = pl.BlockSpec((tok, width), lambda t, m: (0, 0))
    vector = pl.BlockSpec((1, width), lambda t, m: (0, 0))
    tiled = pl.BlockSpec((tok, tile), lambda t, m: (0, t))

    def gact_spec(i):
        def index(t, m):
            half = m[0] if i == 0 else 1 - m[0]
            return (0, jnp.clip(t - half * per, 0, per - 1))

        return tiled if n == 1 else pl.BlockSpec((tok, tile), index)

    low = jax.ShapeDtypeStruct((tok, width), BF16)
    wide = jax.ShapeDtypeStruct((tok, width), F32)
    return pl.pallas_call(
        functools.partial(centre_kernel, n),
        grid_spec=pltpu.PrefetchScalarGridSpec(
            num_scalar_prefetch=1,
            grid=(steps,),
            in_specs=[whole, whole, whole]
            + [pl.BlockSpec((rows, width), lambda t, m: (0, 0))] * n
            + [pl.BlockSpec((rows, tile), lambda t, m: (0, t))] * n
            + [gact_spec(i) for i in range(n)]
            + [pl.BlockSpec((1, tile), lambda t, m: (0, t)), vector, vector, vector],
            out_specs=[
                whole,
                whole,
                tiled,
                tiled,
                whole,
                whole,
                whole,
                pl.BlockSpec((1, tile), lambda t, m: (0, t)),
                pl.BlockSpec((8, width), lambda t, m: (0, 0)),
            ],
            scratch_shapes=[
                pltpu.VMEM((tok, width), F32),
                pltpu.VMEM((tok, width), F32),
                pltpu.VMEM((tok, 1), F32),
            ],
        ),
        out_shape=[
            wide,
            low,
            jax.ShapeDtypeStruct((tok, hidden), BF16),
            jax.ShapeDtypeStruct((tok, hidden), BF16),
            wide,
            low,
            low,
            jax.ShapeDtypeStruct((1, hidden), F32),
            jax.ShapeDtypeStruct((8, width), F32),
        ],
        name="centre",
    )(meta, att, z, cotan, *w_out, *w_up, *gact, up_bias, out_bias, gain, shift)


def unproject_kernel(n, chunks, meta, gq_ref, gkv_ref, *refs):
    w_refs, (own_ref, rest_ref) = refs[:n], refs[n:]
    rows = w_refs[0].shape[0]
    width = gq_ref.shape[1]
    step = pl.program_id(0)
    for start, w_ref in zip(bases(meta[0], n, rows), w_refs):
        term = times_transposed(gkv_ref[0], w_ref[:, width : 2 * width])
        term = term + times_transposed(gkv_ref[1], w_ref[:, 2 * width :])

        @pl.when(step < chunks - 1)
        def _():
            rest_ref[:, pl.ds(start, rows)] = term.astype(BF16)

        @pl.when(step == chunks - 1)
        def _():
            own_ref[:, pl.ds(start, rows)] = term + times_transposed(
                gq_ref[...], w_ref[:, :width]
            )


def unproject(meta, gq, gkv, weights):
    tok, width = gq.shape
    chunks = gkv.shape[1] // tok
    rows = weights[0].shape[0]
    n = len(weights)
    return pl.pallas_call(
        functools.partial(unproject_kernel, n, chunks),
        grid_spec=pltpu.PrefetchScalarGridSpec(
            num_scalar_prefetch=1,
            grid=(chunks,),
            in_specs=[
                pl.BlockSpec((tok, width), lambda c, m: (0, 0)),
                pl.BlockSpec((2, tok, width), lambda c, m: (0, lax.rem(c + 1, chunks), 0)),
            ]
            + [pl.BlockSpec((rows, 3 * width), lambda c, m: (0, 0))] * n,
            out_specs=[
                pl.BlockSpec((tok, width), lambda c, m: (0, 0)),
                pl.BlockSpec((tok, width), lambda c, m: (jnp.minimum(c, chunks - 2), 0)),
            ],
        ),
        out_shape=[
            jax.ShapeDtypeStruct((tok, width), F32),
            jax.ShapeDtypeStruct(((chunks - 1) * tok, width), BF16),
        ],
        name="unproject",
    )(meta, gq, gkv, *weights)


def rear_kernel(others, own, *refs):
    parts = refs[:others]
    z_ref, gres, gain, gz_ref, sums = refs[others:]
    grad = own[...]
    for part in parts:
        grad = grad + part[...].astype(F32)
    centred, rstd = statistics(z_ref[...])
    unit = centred * rstd
    low = (gres[...] + norm_back(unit, rstd, gain[...], grad)).astype(BF16)
    gz_ref[...] = low
    sums[0:1] = jnp.sum(low.astype(F32), axis=0, keepdims=True)
    sums[1:2] = jnp.sum(unit * grad, axis=0, keepdims=True)
    sums[2:3] = jnp.sum(grad, axis=0, keepdims=True)


def rear(own, parts, z, gres, gain):
    tok, width = own.shape
    return pl.pallas_call(
        functools.partial(rear_kernel, len(parts)),
        out_shape=[
            jax.ShapeDtypeStruct((tok, width), BF16),
            jax.ShapeDtypeStruct((8, width), F32),
        ],
        name="rear",
    )(own, *parts, z, gres, gain)


def input_grads_kernel(n, meta, gz, first, second, input_ref, skip_ref):
    low = times_transposed(gz[...], first[...])
    high = times_transposed(gz[...], second[...])
    if n == 1:
        input_ref[...] = low
        skip_ref[...] = high
        return

    @pl.when(meta[0] == 0)
    def _():
        input_ref[...] = low
        skip_ref[...] = high

    @pl.when(meta[0] != 0)
    def _():
        input_ref[...] = high
        skip_ref[...] = low


def input_grads(meta, gz, weights):
    tok, width = gz.shape
    n = len(weights)
    steps = 4
    tile = width // steps
    if n == 1:
        weights = [weights[0], weights[0]]
    out = pl.BlockSpec((tok, tile), lambda t, m: (0, t))
    return pl.pallas_call(
        functools.partial(input_grads_kernel, n),
        grid_spec=pltpu.PrefetchScalarGridSpec(
            num_scalar_prefetch=1,
            grid=(steps,),
            in_specs=[
                pl.BlockSpec((tok, width), lambda t, m: (0, 0)),
                pl.BlockSpec((tile, width), lambda t, m: (t, 0)),
                pl.BlockSpec((tile, width), lambda t, m: (t + (steps if n == 1 else 0), 0)),
            ],
            out_specs=[out, out],
        ),
        out_shape=[jax.ShapeDtypeStruct((tok, width), F32)] * 2,
        name="input_grads",
    )(meta, gz, *weights)


def pack_kernel(*refs):
    out = refs[-1]
    start = 0
    for ref in refs[:-1]:
        size = ref.shape[1]
        out[:, start : start + size] = ref[...]
        start = start + size


def pack(vectors):
    total = sum(v.shape[0] for v in vectors)
    return pl.pallas_call(
        pack_kernel, out_shape=jax.ShapeDtypeStruct((1, total), vectors[0].dtype), name="pack"
    )(*[v.reshape(1, -1) for v in vectors])


def unpack_kernel(sizes, meta, own, other, *outs):
    start = 0
    for size, out in zip(sizes, outs):
        for ref, core in ((own, meta[0]), (other, 1 - meta[0])):
            at = pl.multiple_of(core * size, 128)
            out[:, pl.ds(at, size)] = ref[:, start : start + size].astype(F32)
        start = start + size


def unpack(meta, own, other, sizes):
    vmem = pl.BlockSpec(memory_space=pltpu.VMEM)
    return pl.pallas_call(
        functools.partial(unpack_kernel, sizes),
        in_specs=[pl.BlockSpec(memory_space=pltpu.SMEM), vmem, vmem],
        out_specs=[vmem] * len(sizes),
        out_shape=[jax.ShapeDtypeStruct((1, 2 * n), F32) for n in sizes],
        name="unpack",
    )(meta, own, other)


def place_kernel(places, meta, own, by_x, by_y, far_low, far_high, *outs):
    plane = meta[0]
    lower = pl.program_id(0) < pl.num_programs(0) // 2

    def put(ref, index):
        start = 0
        for width, out, base in places:
            at = pl.multiple_of(base + index * width, 128)
            outs[out][:, pl.ds(at, width)] = ref[:, start : start + width].astype(F32)
            start = start + width

    put(own, plane)
    put(by_x, plane ^ 1)
    put(by_y, plane ^ 2)

    @pl.when(lower)
    def _():
        put(far_low, plane ^ 3)

    @pl.when(jnp.logical_not(lower))
    def _():
        put(far_high, plane ^ 3)


def place(meta, parts, places, out_widths, n_seq):
    rows, width = parts[0].shape
    block = rows // n_seq
    half = n_seq // 2
    whole = pl.BlockSpec((block, width), lambda j, m: (j, 0))
    low = pl.BlockSpec((block, width), lambda j, m: (jnp.minimum(j, half - 1), 0))
    high = pl.BlockSpec((block, width), lambda j, m: (jnp.maximum(j - half, 0), 0))
    return pl.pallas_call(
        functools.partial(place_kernel, places),
        grid_spec=pltpu.PrefetchScalarGridSpec(
            num_scalar_prefetch=1,
            grid=(n_seq,),
            in_specs=[whole, whole, whole, low, high],
            out_specs=[
                pl.BlockSpec((block, w), lambda j, m: (j, 0))
                for w in out_widths
            ],
        ),
        out_shape=[jax.ShapeDtypeStruct((rows, w), F32) for w in out_widths],
        cost_estimate=pl.CostEstimate(
            flops=0, bytes_accessed=rows * sum(out_widths) * 6, transcendentals=0
        ),
        name="place",
    )(meta, *parts)


class Links:
    def __init__(self):
        self.last = {}

    def send(self, link, array, move, *pins):
        waits = [p for p in pins if p is not None]
        if link in self.last:
            waits.append(self.last[link])
        if waits:
            array = lax.optimization_barrier((array, *waits))[0]
        moved = move(array)
        self.last[link] = moved
        return moved


def tie(array, *others):
    return lax.optimization_barrier((array, *others))[0]


def body(
    frames_in,
    skip_in,
    lengths,
    cotangent,
    w_skip,
    w_qkv,
    w_out,
    w_up,
    w_down,
    skip_bias,
    norm1_gain,
    norm1_bias,
    out_bias,
    norm2_gain,
    norm2_bias,
    up_bias,
    down_bias,
):
    tok = frames_in.shape[3]
    width = frames_in.shape[4]
    hidden = w_up.shape[1]
    frames = frames_in.reshape(tok, width)
    skips = skip_in.reshape(tok, width)
    cotan = cotangent.reshape(tok, width)
    n_batch = lax.axis_size("batch")
    n_seq = lax.axis_size("seq")
    n_frames = lax.axis_size("frames")
    assert n_batch == 4 and n_seq % 2 == 0
    paired = n_frames == 2
    plane = lax.axis_index("batch").astype(jnp.int32)
    shard = lax.axis_index("seq").astype(jnp.int32)
    core = lax.axis_index("frames").astype(jnp.int32)
    links = Links()

    def swap_frames(array):
        return lax.ppermute(array, "frames", [(0, 1), (1, 0)])

    def over_x(array):
        return lax.ppermute(array, "batch", [(i, i ^ 1) for i in range(n_batch)])

    def over_y(array):
        return lax.ppermute(array, "batch", [(i, i ^ 2) for i in range(n_batch)])

    def to_seq(step):
        return lambda array: lax.ppermute(
            array, "seq", [(i, (i + step) % n_seq) for i in range(n_seq)]
        )

    def from_seq(step):
        return to_seq(n_seq - step)

    def exchange_seq(array):
        return lax.all_to_all(array, "seq", split_axis=0, concat_axis=0, tiled=True)

    def gather_frames(array, *pins):
        if paired:
            return [array, links.send("frames", array, swap_frames, *pins)]
        return [lax.all_gather(array, "frames", axis=0, tiled=True)]

    def split_columns(array):
        half = array.shape[1] // 2
        return (
            lax.dynamic_slice_in_dim(array, core * half, half, 1),
            lax.dynamic_slice_in_dim(array, (1 - core) * half, half, 1),
        )

    def product(array, weights):
        pieces = split_columns(array) if paired else [array]
        total = times(pieces[0], weights[0])
        for piece, weight in zip(pieces[1:], weights[1:]):
            total = total + times(piece, weight)
        return total

    def left_rows(array, *pins):
        if paired:
            own, other = split_columns(array)
            return jnp.concatenate([own, links.send("frames", other, swap_frames, *pins)], axis=0)
        split = array.reshape(array.shape[0], n_frames, array.shape[1] // n_frames)
        moved = lax.all_to_all(split, "frames", split_axis=1, concat_axis=0, tiled=True)
        return moved.reshape(array.shape[0] * n_frames, array.shape[1] // n_frames)

    def right_rows(array, *pins):
        if paired:
            return jnp.concatenate([array, links.send("frames", array, swap_frames, *pins)], axis=0)
        return lax.all_gather(array, "frames", axis=0, tiled=True)

    def by_plane(right):
        block = right.shape[1] // n_batch
        return jnp.concatenate(
            [
                lax.dynamic_slice_in_dim(right, (plane ^ bits) * block, block, 1)
                for bits in (0, 1, 3, 2)
            ],
            axis=1,
        )

    class Chain:
        def __init__(self, terms):
            self.terms = [(left, by_plane(right)) for left, right in terms]
            self.rows = terms[0][0].shape[1]

        def gemm(self, low, high, first, last):
            outs = []
            for left, right in self.terms:
                block = right.shape[1] // n_batch
                outs.append(
                    contract_rows(left[:, low:high], right[:, first * block : last * block])
                )
            return outs

        def send(self, link, arrays, move, *pins):
            sizes = [a.shape[1] for a in arrays]
            arrays = [a.astype(BF16) for a in arrays]
            joined = jnp.concatenate(arrays, axis=1) if len(arrays) > 1 else arrays[0]
            moved = links.send(link, joined, move, *pins)
            ends = [sum(sizes[: i + 1]) for i in range(len(sizes))]
            return [moved[:, e - s : e] for e, s in zip(ends, sizes)]

        def first(self, *pins):
            half, rows = self.rows // 2, self.rows
            self.from_x = self.send("x", self.gemm(0, half, 1, 3), over_x, *pins)
            self.from_y = self.send("y", self.gemm(half, rows, 2, 4), over_y, *pins)

        def second(self, *pins):
            half, rows = self.rows // 2, self.rows
            low = [
                g + r[:, g.shape[1] :].astype(F32)
                for g, r in zip(self.gemm(0, half, 3, 4), self.from_x)
            ]
            high = [
                g + r[:, : g.shape[1]].astype(F32)
                for g, r in zip(self.gemm(half, rows, 1, 2), self.from_y)
            ]
            self.then_y = self.send("y", low, over_y, *pins)
            self.then_x = self.send("x", high, over_x, *pins)

        def across(self, *pins):
            own = []
            for g, fx, fy, ty, tx in zip(
                self.gemm(0, self.rows, 0, 1), self.from_x, self.from_y, self.then_y, self.then_x
            ):
                n = g.shape[1]
                low = fx[:, :n].astype(F32) + ty.astype(F32)
                high = fy[:, n:].astype(F32) + tx.astype(F32)
                own.append((g + jnp.concatenate([low, high], axis=0)).astype(BF16))
            own = jnp.concatenate(own, axis=1) if len(own) > 1 else own[0]
            own = own.reshape(n_seq, self.rows // n_seq, own.shape[1])
            self.terms_seq = links.send("z", own, exchange_seq, *pins)

        def along(self, *pins):
            total = jnp.sum(self.terms_seq.astype(F32), axis=0).astype(BF16)
            copies = jnp.broadcast_to(total[None], self.terms_seq.shape)
            whole = links.send("z", copies, exchange_seq, *pins)
            self.whole = whole.reshape(self.rows, whole.shape[2])

        def spread(self, *pins):
            self.by_x = links.send("x", self.whole, over_x, *pins)
            self.by_y = links.send("y", self.whole, over_y, *pins)

        def finish(self, *pins):
            half = self.rows // 2
            self.far_low = links.send("x", self.by_y[:half], over_x, *pins)
            self.far_high = links.send("y", self.by_x[half:], over_y, *pins)

        def parts(self):
            return self.whole, self.by_x, self.by_y, self.far_low, self.far_high

    vectors_in = (
        skip_bias,
        norm1_gain,
        norm1_bias,
        out_bias,
        norm2_gain,
        norm2_bias,
        up_bias,
        down_bias,
    )
    sizes = [v.shape[0] for v in vectors_in]
    starts = [sum(sizes[:i]) for i in range(len(sizes))]
    packed = pack(vectors_in)
    bounds = jnp.cumsum(lengths.reshape(-1), dtype=jnp.int32)
    core_meta = core.reshape(1)
    if paired:
        full_skip = [w_skip, swap_frames(w_skip)]
        links.last["frames"] = full_skip[1]
        vectors = unpack(core_meta, packed, swap_frames(packed), sizes)
        inputs = [jnp.where(core == 0, frames, skips), jnp.where(core == 0, skips, frames)]
    else:
        full_skip = gather_frames(w_skip)
        packed = lax.all_gather(packed, "frames", axis=0, tiled=True).astype(F32)
        vectors = [packed[:, b : b + n].reshape(1, -1) for b, n in zip(starts, sizes)]
        inputs = [jnp.concatenate([frames, skips], axis=1)]
    sbias, gain1, bias1, obias, gain2, bias2, ubias, dbias = vectors
    full_qkv = gather_frames(w_qkv)

    hidden_z, n1 = front(inputs, full_skip, sbias, gain1, bias1)
    n1_all = [n1] + [from_seq(j)(n1) for j in range(1, n_seq)]
    full_down = gather_frames(w_down, n1)
    full_out = gather_frames(w_out)
    full_up = gather_frames(w_up)
    gact = [times_transposed(cotan, weight) for weight in full_down]
    n1_all[-1] = tie(n1_all[-1], *gact)
    queries, key_rows, value_rows = project(core_meta, n1_all, full_qkv)
    attend_meta = jnp.concatenate([shard.reshape(1), bounds])
    slopes = 2.0 ** (-8.0 * jnp.arange(1, HEADS + 1, dtype=F32) / HEADS)
    slopes = jnp.repeat(slopes, tok).reshape(HEADS // 2, 1, 2 * tok)
    attended, prob = attend_forward(attend_meta, queries, key_rows, value_rows, slopes, n_seq)
    both_cotan = right_rows(cotan, queries)
    left_n1 = left_rows(jnp.concatenate(n1_all, axis=0), queries)
    left_att = left_rows(attended)
    centre_meta = jnp.stack([core, bounds[UTTS - 1] - shard * tok])
    resid, n2, activ, gup, grad_resid, grad_branch, grad_heads, up_sum, sums2 = centre(
        centre_meta, attended, hidden_z, cotan, full_out, full_up, gact, ubias, obias, gain2, bias2
    )

    down = Chain([(left_rows(activ), both_cotan)])
    down.first()
    gq, gkv = attend_backward(queries, key_rows, value_rows, grad_heads, prob)
    up = Chain(
        [
            (left_rows(n2, gq), right_rows(gup, gq)),
            (left_att, right_rows(grad_branch, gq)),
        ]
    )
    gn1_own, gn1_rest = unproject(core_meta, gq, gkv, full_qkv)
    gn1_parts = [
        to_seq(j)(gn1_rest[(j - 1) * tok : j * tok]) for j in range(1, n_seq)
    ]
    down.second(gn1_rest)
    up.first()
    grad_z, sums1 = rear(gn1_own, gn1_parts, hidden_z, grad_resid, gain1)
    if paired:
        both_gkv = links.send("frames", gkv, swap_frames, gn1_rest)
        left_q = left_n1.reshape(2, n_seq * tok, -1)[:, :tok].reshape(2 * tok, -1)
        both_k = jnp.concatenate([gkv[0], both_gkv[0]], axis=0)
        both_v = jnp.concatenate([gkv[1], both_gkv[1]], axis=0)
    else:
        left_q = left_rows(n1)
        both_k, both_v = right_rows(gkv[0]), right_rows(gkv[1])
    qkv = Chain([(left_q, right_rows(gq)), (left_n1, both_k), (left_n1, both_v)])
    links.last["z"] = grad_z
    down.across()
    up.second(grad_z)
    qkv.first()
    down.along()
    if paired:
        left_joined = jnp.concatenate(
            [inputs[0], links.send("frames", inputs[1], swap_frames)], axis=0
        )
    else:
        left_joined = left_rows(inputs[0])
    skip = Chain([(left_joined, right_rows(grad_z))])
    up.across()
    qkv.second()
    skip.first()
    up.along()
    skip.second()
    output = (resid + product(activ, full_down) + dbias).astype(BF16)
    down.spread(output)
    qkv.across()
    down.finish()
    qkv.along()
    place_meta = plane.reshape(1)
    quarter = width // n_batch
    (grad_w_down,) = place(place_meta, down.parts(), ((quarter, 0, 0),), (width,), n_seq)
    input_grad, skip_grad = input_grads(core_meta, grad_z, full_skip)
    up.spread(input_grad)
    skip.across()
    up.finish(grad_w_down)
    skip.along()
    grad_w_up, grad_w_out = place(
        place_meta,
        up.parts(),
        ((hidden // n_batch, 0, 0), (quarter, 1, 0)),
        (hidden, width),
        n_seq,
    )

    vector_sums = (
        sums1[0],
        sums1[1],
        sums1[2],
        sums2[0],
        sums2[1],
        sums2[2],
        up_sum[0],
        jnp.sum(cotan, axis=0, dtype=F32),
    )
    stacked = jnp.concatenate([v.reshape(n_frames, -1) for v in vector_sums], axis=1)
    if paired:
        mine = lax.dynamic_slice_in_dim(stacked, core, 1, 0)
        theirs = lax.dynamic_slice_in_dim(stacked, 1 - core, 1, 0)
        mine = mine + links.send("frames", theirs, swap_frames)
    else:
        mine = lax.psum_scatter(stacked, "frames", scatter_dimension=0, tiled=True)
    mine = mine + links.send("x", mine, over_x)
    mine = mine + links.send("y", mine, over_y)
    copies = jnp.broadcast_to(mine[None], (n_seq,) + mine.shape)
    total = jnp.sum(links.send("z", copies, exchange_seq), axis=0).reshape(-1)
    vector_grads = [total[b : b + n] for b, n in zip(starts, sizes)]

    qkv.spread(grad_w_up, grad_w_out)
    qkv.finish()
    (grad_w_qkv,) = place(
        place_meta,
        qkv.parts(),
        ((quarter, 0, 0), (quarter, 0, width), (quarter, 0, 2 * width)),
        (3 * width,),
        n_seq,
    )
    skip.spread()
    skip.finish(grad_w_qkv)
    (grad_w_skip,) = place(place_meta, skip.parts(), ((quarter, 0, 0),), (width,), n_seq)

    def back(array):
        return array.reshape(1, 1, 1, tok, width)

    return (
        back(output),
        back(input_grad),
        back(skip_grad),
        grad_w_skip,
        grad_w_qkv,
        grad_w_out,
        grad_w_up,
        grad_w_down,
        *vector_grads,
    )


def solution(mesh):
    rows = P("batch", "seq", "frames", None, None)
    in_specs = (
        (rows, rows, P("batch", "frames", None), rows)
        + (P("frames", None),) * 5
        + (P("frames"),) * 8
    )
    out_specs = (rows,) * 3 + (P("frames", None),) * 5 + (P("frames"),) * 8
    return jax.shard_map(body, mesh=mesh, in_specs=in_specs, out_specs=out_specs, check_vma=False)
```

```python
import functools

import jax
import jax.numpy as jnp
from jax import lax
from jax.experimental import pallas as pl
from jax.experimental.pallas import tpu as pltpu
from jax.sharding import PartitionSpec as P

HEADS = 16
HD = 64
UTTS = 3
EPS = 1e-05
MASKED = 1e12
BF16 = jnp.bfloat16
F32 = jnp.float32
INV_SQRT2 = 0.7071067811865476
INV_SQRT_2PI = 0.3989422804014327
ERFC_STEP = 0.4
ERFC_TERMS = (
    0.22567586186829244 / 2,
    0.22566960544571626 / 2,
    0.20784251123900896 / 2,
    0.16854379658168633 / 2,
    0.14142295790506823 / 2,
    -0.005586494604590357 / 2,
    0.16905696704198306 / 2,
    -0.18288169574958996 / 2,
    0.05025661354969599 / 2,
)


def contract_rows(left_side, right_side):
    return lax.dot_general(
        left_side, right_side, (((0,), (0,)), ((), ())), preferred_element_type=F32
    )


def times_transposed(left_side, right_side):
    return lax.dot_general(
        left_side, right_side, (((1,), (1,)), ((), ())), preferred_element_type=F32
    )


def times(left_side, right_side):
    return jnp.dot(left_side, right_side, preferred_element_type=F32)


def ordered(kernel, count, after):
    n = len(after)

    def run(*refs):
        kernel(*refs[:count], *refs[count + n :])

    return run, [pl.BlockSpec(memory_space=pl.ANY)] * n


TURNS = (0, 1, 3, 2)


def turn(block, plane):
    bits = block ^ plane
    return bits ^ (bits >> 1)


def put_turned(part, read, plane):
    block = part.shape[-1] // len(TURNS)
    for i, bits in enumerate(TURNS):
        at = pl.multiple_of((plane ^ bits) * block, 128)
        part[:, i * block : (i + 1) * block] = read(at, block)


def pair_rows(block, lane):
    zero = jnp.zeros_like(block)
    return jnp.concatenate(
        [jnp.where(lane < HD, block, zero), jnp.where(lane >= HD, block, zero)], axis=0
    )


def utterance_ends(meta):
    ends = [meta[3]]
    for j in range(1, UTTS):
        ends.append(ends[-1] + meta[3 + j])
    return ends


def attend_forward_kernel(meta, q_ref, k_ref, v_ref, out_ref, prob_ref, dist):
    tok = q_ref.shape[0]
    length = k_ref.shape[0]
    shard = meta[1]
    ends = utterance_ends(meta)

    @pl.when(pl.program_id(0) == 0)
    def _():
        row = lax.broadcasted_iota(jnp.int32, (length, 2 * tok), 0)
        col = lax.broadcasted_iota(jnp.int32, (length, 2 * tok), 1)
        k_pos = row + shard * tok
        k_pos = jnp.where(k_pos >= length, k_pos - length, k_pos)
        q_pos = jnp.where(col >= tok, col - tok, col) + shard * tok
        k_seg = jnp.zeros_like(k_pos)
        q_seg = jnp.zeros_like(q_pos)
        for j in range(UTTS):
            k_seg = k_seg + (k_pos >= ends[j]).astype(jnp.int32)
            q_seg = q_seg + (q_pos >= ends[j]).astype(jnp.int32)
        allowed = (k_seg == q_seg) & (k_seg < UTTS)
        dist[...] = jnp.where(allowed, jnp.abs(k_pos - q_pos).astype(F32), MASKED)

    lane = lax.broadcasted_iota(jnp.int32, (tok, 2 * HD), 1)
    pair = pair_rows(q_ref[...] * jnp.asarray(HD**-0.5, BF16), lane)
    head = 2 * pl.program_id(0) + 1 + (lax.broadcasted_iota(jnp.int32, (1, 2 * tok), 1) >= tok)
    slope = jnp.exp2(head.astype(F32) * (-8.0 / HEADS))
    scores = times_transposed(k_ref[...], pair) - slope * dist[...]
    top = jnp.max(scores, axis=0, keepdims=True)
    exp_scores = jnp.exp(scores - top)
    total = jnp.sum(exp_scores, axis=0, keepdims=True)
    prob = (exp_scores * (1.0 / total)).astype(BF16)
    prob_ref[0] = prob
    mixed = times(v_ref[...].T, prob).T
    mixed = jnp.where(lane < HD, mixed[:tok], mixed[tok:])
    row = lax.broadcasted_iota(jnp.int32, (tok, 2 * HD), 0) + shard * tok
    out_ref[...] = jnp.where(row < ends[UTTS - 1], mixed, 0.0).astype(BF16)


def attend_backward_kernel(q_ref, k_ref, v_ref, grad_ref, prob_ref, out_ref):
    tok = q_ref.shape[0]
    lane = lax.broadcasted_iota(jnp.int32, (tok, 2 * HD), 1)
    scale = jnp.asarray(HD**-0.5, BF16)
    pair_q = pair_rows(q_ref[...] * scale, lane)
    pair_g = pair_rows(grad_ref[...], lane)
    prob_low = prob_ref[0]
    prob = prob_low.astype(F32)
    prob_grad = times_transposed(v_ref[...], pair_g)
    weighted = prob * prob_grad
    delta = jnp.sum(weighted, axis=0, keepdims=True)
    score_low = (weighted - prob * delta).astype(BF16)
    out_ref[2] = times(prob_low, pair_g).astype(BF16)
    out_ref[1] = times(score_low, pair_q).astype(BF16)
    mixed = times((k_ref[...] * scale).T, score_low).T
    out_ref[0, :tok] = jnp.where(lane < HD, mixed[:tok], mixed[tok:]).astype(BF16)
    out_ref[0, tok:] = jnp.zeros_like(out_ref[0, tok:])


def attend_forward(meta, queries, key_rows, value_rows, after=()):
    tok, width = queries.shape
    length = key_rows.shape[0]
    pairs = width // (2 * HD)
    kernel, waits = ordered(attend_forward_kernel, 4, after)
    return pl.pallas_call(
        kernel,
        grid_spec=pltpu.PrefetchScalarGridSpec(
            num_scalar_prefetch=1,
            grid=(pairs,),
            in_specs=[
                pl.BlockSpec((tok, 2 * HD), lambda g, m: (0, g)),
                pl.BlockSpec((length, 2 * HD), lambda g, m: (0, g)),
                pl.BlockSpec((length, 2 * HD), lambda g, m: (0, g)),
            ]
            + waits,
            out_specs=[
                pl.BlockSpec((tok, 2 * HD), lambda g, m: (0, g)),
                pl.BlockSpec((1, length, 2 * tok), lambda g, m: (g, 0, 0)),
            ],
            scratch_shapes=[pltpu.VMEM((length, 2 * tok), F32)],
        ),
        out_shape=[
            jax.ShapeDtypeStruct((tok, width), BF16),
            jax.ShapeDtypeStruct((pairs, length, 2 * tok), BF16),
        ],
        name="attend_forward",
    )(meta, queries, key_rows, value_rows, *after)


def attend_backward(queries, key_rows, value_rows, grad_heads, prob, after=()):
    tok, width = queries.shape
    length = key_rows.shape[0]
    pairs = width // (2 * HD)
    q_spec = pl.BlockSpec((tok, 2 * HD), lambda g: (0, g))
    k_spec = pl.BlockSpec((length, 2 * HD), lambda g: (0, g))
    kernel, waits = ordered(attend_backward_kernel, 5, after)
    return pl.pallas_call(
        kernel,
        grid=(pairs,),
        in_specs=[
            q_spec,
            k_spec,
            k_spec,
            q_spec,
            pl.BlockSpec((1, length, 2 * tok), lambda g: (g, 0, 0)),
        ]
        + waits,
        out_specs=pl.BlockSpec((3, length, 2 * HD), lambda g: (0, 0, g)),
        out_shape=jax.ShapeDtypeStruct((3, length, width), BF16),
        name="attend_backward",
    )(queries, key_rows, value_rows, grad_heads, prob, *after)


def statistics(values):
    mean = jnp.mean(values, axis=-1, keepdims=True)
    centred = values - mean
    variance = jnp.mean(centred * centred, axis=-1, keepdims=True)
    return centred, lax.rsqrt(variance + EPS)


def norm_back(unit, rstd, gain, grad):
    scaled = grad * gain
    mean_e = jnp.mean(scaled, axis=-1, keepdims=True)
    mean_eu = jnp.mean(scaled * unit, axis=-1, keepdims=True)
    return rstd * (scaled - mean_e - unit * mean_eu)


def bases(core, n_pieces, rows):
    if n_pieces == 1:
        return [0]
    return [pl.multiple_of(core * rows, 128), pl.multiple_of((1 - core) * rows, 128)]


def front_kernel(n, sizes, meta, *refs):
    x_refs, refs = refs[:2], refs[2:]
    w_refs, packs, outs = refs[:n], refs[n : 2 * n], refs[2 * n :]
    z_ref, n1_ref, own_ref, other_ref = outs
    step = pl.program_id(0)
    first = meta[0] == 0

    def vector(i):
        start = sum(sizes[:i])
        parts = [ref[:, start : start + sizes[i]].astype(F32) for ref in packs]
        low = jnp.where(first, parts[0], parts[1])
        high = jnp.where(first, parts[1], parts[0])
        return jnp.concatenate([low, high], axis=1)

    x, s = x_refs[0][...], x_refs[1][...]
    own = jnp.where(first, x, s)
    other = jnp.where(first, s, x)
    own_ref[...] = own
    other_ref[...] = other
    part = times(own, w_refs[0][...]) + times(other, w_refs[1][...])

    @pl.when(step == 0)
    def _():
        z_ref[...] = part + vector(0)

    @pl.when(step > 0)
    def _():
        z_ref[...] += part

    @pl.when(step == pl.num_programs(0) - 1)
    def _():
        centred, rstd = statistics(z_ref[...])
        n1_ref[...] = (centred * rstd * vector(1) + vector(2)).astype(BF16)


def front(meta, frames, skips, weights, packs, sizes, after=()):
    tok = frames.shape[0]
    rows, width = weights[0].shape
    n = len(weights)
    steps = 4
    block = rows // steps
    packed = pl.BlockSpec(packs[0].shape, lambda k, m: (0, 0))
    whole = pl.BlockSpec((tok, width), lambda k, m: (0, 0))
    columns = pl.BlockSpec((tok, block), lambda k, m: (0, k))
    turned = pl.BlockSpec((tok, block), lambda k, m: (0, turn(k, m[2])))
    kernel, waits = ordered(functools.partial(front_kernel, n, sizes), 3 + 2 * n, after)
    return pl.pallas_call(
        kernel,
        grid_spec=pltpu.PrefetchScalarGridSpec(
            num_scalar_prefetch=1,
            grid=(steps,),
            in_specs=[columns] * 2
            + [pl.BlockSpec((block, width), lambda k, m: (k, 0))] * n
            + [packed] * n
            + waits,
            out_specs=[whole, whole, turned, turned],
        ),
        out_shape=[
            jax.ShapeDtypeStruct((tok, width), F32),
            jax.ShapeDtypeStruct((tok, width), BF16),
            jax.ShapeDtypeStruct((tok, rows), BF16),
            jax.ShapeDtypeStruct((tok, rows), BF16),
        ],
        name="front",
    )(meta, frames, skips, *weights, *packs, *after)


def front_whole_kernel(x_ref, s_ref, first_ref, second_ref, bias, gain, shift, z_ref, n1_ref):
    step = pl.program_id(0)
    part = times(x_ref[...], first_ref[...]) + times(s_ref[...], second_ref[...])

    @pl.when(step == 0)
    def _():
        z_ref[...] = part + bias[...]

    @pl.when(step > 0)
    def _():
        z_ref[...] += part

    @pl.when(step == pl.num_programs(0) - 1)
    def _():
        centred, rstd = statistics(z_ref[...])
        n1_ref[...] = (centred * rstd * gain[...] + shift[...]).astype(BF16)


def front_whole(frames, skips, weight, bias, gain, shift):
    tok, width = frames.shape
    steps = 4
    block = width // steps
    vector = pl.BlockSpec((1, width), lambda k: (0, 0))
    whole = pl.BlockSpec((tok, width), lambda k: (0, 0))
    return pl.pallas_call(
        front_whole_kernel,
        grid=(steps,),
        in_specs=[pl.BlockSpec((tok, block), lambda k: (0, k))] * 2
        + [
            pl.BlockSpec((block, width), lambda k: (k, 0)),
            pl.BlockSpec((block, width), lambda k: (k + steps, 0)),
        ]
        + [vector] * 3,
        out_specs=[whole, whole],
        out_shape=[
            jax.ShapeDtypeStruct((tok, width), F32),
            jax.ShapeDtypeStruct((tok, width), BF16),
        ],
        name="front",
    )(frames, skips, weight, weight, bias, gain, shift)


def project_kernel(n, chunks, meta, *refs):
    x_refs = refs[:chunks]
    w_refs = refs[chunks : chunks + 3 * n]
    q_ref, k_ref, v_ref = refs[chunks + 3 * n : chunks + 3 * n + 3]
    parts = refs[chunks + 3 * n + 3 :]
    rows = w_refs[0].shape[0]
    tok = q_ref.shape[0]
    starts = bases(meta[0], n, rows)

    @pl.when(pl.program_id(0) == 0)
    def _():
        for start, part in zip(starts, parts):
            for c in range(chunks):
                if n == 1:
                    part[c * tok : (c + 1) * tok] = x_refs[c][...]
                    continue
                put_turned(
                    part.at[c * tok : (c + 1) * tok],
                    lambda at, block: x_refs[c][:, pl.ds(pl.multiple_of(start + at, 128), block)],
                    meta[2],
                )

    for c in range(chunks):
        for i, out in enumerate((q_ref, k_ref, v_ref)):
            if i == 0 and c > 0:
                continue
            total = None
            for p, start in enumerate(starts):
                term = times(x_refs[c][:, pl.ds(start, rows)], w_refs[3 * p + i][...])
                total = term if total is None else total + term
            out[c * tok : (c + 1) * tok] = total.astype(BF16)


def project(meta, chunks, weights, after=()):
    tok, width = chunks[0].shape
    rows = weights[0].shape[0]
    n = len(weights)
    tile = 256
    tiles = width // tile

    def w_spec(i):
        return pl.BlockSpec((rows, tile), lambda t, m: (0, t + i * tiles))

    length = tok * len(chunks)
    kernel, waits = ordered(
        functools.partial(project_kernel, n, len(chunks)), 1 + len(chunks) + 3 * n, after
    )
    return pl.pallas_call(
        kernel,
        grid_spec=pltpu.PrefetchScalarGridSpec(
            num_scalar_prefetch=1,
            grid=(tiles,),
            in_specs=[pl.BlockSpec((tok, width), lambda t, m: (0, 0))] * len(chunks)
            + [w_spec(i) for i in range(3)] * n
            + waits,
            out_specs=[
                pl.BlockSpec((tok, tile), lambda t, m: (0, t)),
                pl.BlockSpec((length, tile), lambda t, m: (0, t)),
                pl.BlockSpec((length, tile), lambda t, m: (0, t)),
            ]
            + [pl.BlockSpec((length, rows), lambda t, m: (0, 0))] * n,
        ),
        out_shape=[
            jax.ShapeDtypeStruct((tok, width), BF16),
            jax.ShapeDtypeStruct((length, width), BF16),
            jax.ShapeDtypeStruct((length, width), BF16),
        ]
        + [jax.ShapeDtypeStruct((length, rows), BF16)] * n,
        name="project",
    )(meta, *chunks, *[w for w in weights for _ in range(3)], *after)


def centre_kernel(n, meta, *refs):
    refs = list(refs)

    def take(count):
        taken = refs[:count]
        del refs[:count]
        return taken

    att, z_ref, cotan = take(3)
    w_out, w_up, gact = take(n), take(n), take(n)
    up_bias, out_bias, gain, shift = take(4)
    resid, gup_ref, gres, gbranch, gatt, up_sum, sums = take(7)
    acts, n2_parts, att_parts = take(n), take(n), take(n)
    n2, gn2, unit, rstd = refs
    step, steps = pl.program_id(0), pl.num_programs(0)
    tok = att.shape[0]
    core, live = meta[0], utterance_ends(meta)[-1] - meta[1] * tok
    rows = w_out[0].shape[0]
    starts = bases(core, n, rows)

    @pl.when(step == 0)
    def _():
        total = z_ref[...] + out_bias[...]
        for start, w_ref, part in zip(starts, w_out, att_parts):
            total = total + times(att[:, pl.ds(start, rows)], w_ref[...])
        resid[...] = total
        centred, scale = statistics(total)
        unit[...] = centred * scale
        rstd[...] = scale
        n2[...] = (unit[...] * gain[...] + shift[...]).astype(BF16)
        for start, n2_part, att_part in zip(starts, n2_parts, att_parts):
            for part, source in ((n2_part, n2), (att_part, att)):
                if n == 1:
                    part[...] = source[...]
                    continue
                put_turned(
                    part,
                    lambda at, block: source[:, pl.ds(pl.multiple_of(start + at, 128), block)],
                    meta[2],
                )
        gn2[...] = jnp.zeros_like(gn2)

    pre = up_bias[...]
    for start, w_ref in zip(starts, w_up):
        pre = pre + times(n2[:, pl.ds(start, rows)], w_ref[...])
    gauss = jnp.exp(pre * pre * (-0.5))
    t = 1.0 / (1.0 + (ERFC_STEP * INV_SQRT2) * jnp.abs(pre))
    tail = jnp.full_like(t, ERFC_TERMS[-1])
    for term in ERFC_TERMS[-2::-1]:
        tail = tail * t + term
    tail = tail * t * gauss
    cdf = jnp.where(pre < 0.0, tail, 1.0 - tail)
    act = (pre * cdf).astype(BF16)
    if n == 1:
        acts[0][...] = act
        grad = gact[0][...]
    else:
        mine = (step // (steps // 2)) == core

        @pl.when(mine)
        def _():
            acts[0][...] = act

        @pl.when(jnp.logical_not(mine))
        def _():
            acts[1][...] = act

        grad = jnp.where(mine, gact[0][...], gact[1][...])
    gup = (grad * (cdf + pre * gauss * INV_SQRT_2PI)).astype(BF16)
    gup_ref[...] = gup
    up_sum[...] = jnp.sum(gup.astype(F32), axis=0, keepdims=True)
    for start, w_ref in zip(starts, w_up):
        gn2[:, pl.ds(start, rows)] += times_transposed(gup, w_ref[...])

    @pl.when(step == steps - 1)
    def _():
        grad_n2 = gn2[...]
        total = cotan[...].astype(F32) + norm_back(unit[...], rstd[...], gain[...], grad_n2)
        gres[...] = total
        low = total.astype(BF16)
        gbranch[...] = low
        alive = lax.broadcasted_iota(jnp.int32, (tok, 1), 0) < live
        for start, w_ref in zip(starts, w_out):
            term = times_transposed(low, w_ref[...])
            gatt[:, pl.ds(start, rows)] = jnp.where(alive, term, 0.0).astype(BF16)
        sums[0:1] = jnp.sum(low.astype(F32), axis=0, keepdims=True)
        sums[1:2] = jnp.sum(unit[...] * grad_n2, axis=0, keepdims=True)
        sums[2:3] = jnp.sum(grad_n2, axis=0, keepdims=True)
        sums[3:4] = jnp.sum(cotan[...].astype(F32), axis=0, keepdims=True)


def centre(meta, att, z, cotan, w_out, w_up, gact, up_bias, out_bias, gain, shift, after=(), tile=512):
    tok, width = att.shape
    n = len(w_out)
    rows = w_out[0].shape[0]
    hidden = w_up[0].shape[1]
    steps = hidden // tile
    per = steps // n
    assert n == 1 or per == len(TURNS)
    whole = pl.BlockSpec((tok, width), lambda t, m: (0, 0))
    vector = pl.BlockSpec((1, width), lambda t, m: (0, 0))
    tiled = pl.BlockSpec((tok, tile), lambda t, m: (0, t))

    def gact_spec(i, by_plane=False):
        def index(t, m):
            half = m[0] if i == 0 else 1 - m[0]
            at = jnp.clip(t - half * per, 0, per - 1)
            return (0, turn(at, m[2]) if by_plane else at)

        return tiled if n == 1 else pl.BlockSpec((tok, tile), index)

    low = jax.ShapeDtypeStruct((tok, width), BF16)
    wide = jax.ShapeDtypeStruct((tok, width), F32)
    part = pl.BlockSpec((tok, rows), lambda t, m: (0, 0))
    kernel, waits = ordered(functools.partial(centre_kernel, n), 8 + 3 * n, after)
    return pl.pallas_call(
        kernel,
        grid_spec=pltpu.PrefetchScalarGridSpec(
            num_scalar_prefetch=1,
            grid=(steps,),
            in_specs=[whole, whole, whole]
            + [pl.BlockSpec((rows, width), lambda t, m: (0, 0))] * n
            + [pl.BlockSpec((rows, tile), lambda t, m: (0, t))] * n
            + [gact_spec(i) for i in range(n)]
            + [pl.BlockSpec((1, tile), lambda t, m: (0, t)), vector, vector, vector]
            + waits,
            out_specs=[
                whole,
                tiled,
                whole,
                whole,
                whole,
                pl.BlockSpec((1, tile), lambda t, m: (0, t)),
                pl.BlockSpec((8, width), lambda t, m: (0, 0)),
            ]
            + [gact_spec(i, True) for i in range(n)]
            + [part] * (2 * n),
            scratch_shapes=[
                pltpu.VMEM((tok, width), BF16),
                pltpu.VMEM((tok, width), F32),
                pltpu.VMEM((tok, width), F32),
                pltpu.VMEM((tok, 1), F32),
            ],
        ),
        out_shape=[
            wide,
            jax.ShapeDtypeStruct((tok, hidden), BF16),
            wide,
            low,
            low,
            jax.ShapeDtypeStruct((1, hidden), F32),
            jax.ShapeDtypeStruct((8, width), F32),
        ]
        + [jax.ShapeDtypeStruct((tok, hidden // n), BF16)] * n
        + [jax.ShapeDtypeStruct((tok, rows), BF16)] * (2 * n),
        name="centre",
    )(meta, att, z, cotan, *w_out, *w_up, *gact, up_bias, out_bias, gain, shift, *after)


def unproject_kernel(n, meta, grads, *refs):
    w_refs, out, flat = refs[:n], refs[n], refs[n + 1]
    rows = w_refs[0].shape[0]
    width = grads.shape[2]
    for i in range(3):
        flat[:, i * width : (i + 1) * width] = grads[i]
    for start, w_ref in zip(bases(meta[0], n, rows), w_refs):
        term = times_transposed(grads[1], w_ref[:, width : 2 * width])
        term = term + times_transposed(grads[2], w_ref[:, 2 * width :])

        @pl.when(pl.program_id(0) == 0)
        def _():
            own = term + times_transposed(grads[0], w_ref[:, :width])
            out[0, :, pl.ds(start, rows)] = own.astype(BF16)

        @pl.when(pl.program_id(0) > 0)
        def _():
            out[0, :, pl.ds(start, rows)] = term.astype(BF16)


def unproject(meta, grads, weights, chunks, after=()):
    length, width = grads.shape[1:]
    tok = length // chunks
    rows = weights[0].shape[0]
    n = len(weights)
    kernel, waits = ordered(functools.partial(unproject_kernel, n), 2 + n, after)
    return pl.pallas_call(
        kernel,
        grid_spec=pltpu.PrefetchScalarGridSpec(
            num_scalar_prefetch=1,
            grid=(chunks,),
            in_specs=[pl.BlockSpec((3, tok, width), lambda c, m: (0, c, 0))]
            + [pl.BlockSpec((rows, 3 * width), lambda c, m: (0, 0))] * n
            + waits,
            out_specs=[
                pl.BlockSpec((1, tok, width), lambda c, m: (lax.rem(c + m[1], chunks), 0, 0)),
                pl.BlockSpec((tok, 3 * width), lambda c, m: (c, 0)),
            ],
        ),
        out_shape=[
            jax.ShapeDtypeStruct((chunks, tok, width), BF16),
            jax.ShapeDtypeStruct((length, 3 * width), BF16),
        ],
        name="unproject",
    )(meta, grads, *weights, *after)


def rear_kernel(parts, z_ref, gres, gain, gz_ref, sums):
    grad = parts[0].astype(F32)
    for i in range(1, parts.shape[0]):
        grad = grad + parts[i].astype(F32)
    centred, rstd = statistics(z_ref[...])
    unit = centred * rstd
    low = (gres[...] + norm_back(unit, rstd, gain[...], grad)).astype(BF16)
    gz_ref[...] = low
    sums[0:1] = jnp.sum(low.astype(F32), axis=0, keepdims=True)
    sums[1:2] = jnp.sum(unit * grad, axis=0, keepdims=True)
    sums[2:3] = jnp.sum(grad, axis=0, keepdims=True)


def rear(parts, z, gres, gain, after=()):
    tok, width = z.shape
    count = 4
    kernel, waits = ordered(rear_kernel, count, after)
    vmem = pl.BlockSpec(memory_space=pltpu.VMEM)
    return pl.pallas_call(
        kernel,
        in_specs=[vmem] * count + waits,
        out_specs=[vmem] * 2,
        out_shape=[
            jax.ShapeDtypeStruct((tok, width), BF16),
            jax.ShapeDtypeStruct((8, width), F32),
        ],
        name="rear",
    )(parts, z, gres, gain, *after)


def forward_kernel(resid, bias, own, other, w_own, w_other, out, total):
    step = pl.program_id(0)
    part = times(own[...], w_own[...]) + times(other[...], w_other[...])

    @pl.when(step == 0)
    def _():
        total[...] = resid[...] + bias[...] + part

    @pl.when(step > 0)
    def _():
        total[...] += part

    @pl.when(step == pl.num_programs(0) - 1)
    def _():
        out[...] = total[...].astype(BF16)


def forward(meta, resid, bias, acts, weights, after=()):
    tok, width = resid.shape
    steps = len(TURNS)
    rows = weights[0].shape[0] // steps
    whole = pl.BlockSpec((tok, width), lambda k, m: (0, 0))
    kernel, waits = ordered(
        lambda meta, *refs: forward_kernel(*refs), 7, after
    )
    return pl.pallas_call(
        kernel,
        grid_spec=pltpu.PrefetchScalarGridSpec(
            num_scalar_prefetch=1,
            grid=(steps,),
            in_specs=[whole, pl.BlockSpec((1, width), lambda k, m: (0, 0))]
            + [pl.BlockSpec((tok, rows), lambda k, m: (0, k))] * 2
            + [pl.BlockSpec((rows, width), lambda k, m: (m[2] ^ k ^ (k >> 1), 0))] * 2
            + waits,
            out_specs=whole,
            scratch_shapes=[pltpu.VMEM((tok, width), F32)],
        ),
        out_shape=jax.ShapeDtypeStruct((tok, width), BF16),
        name="forward",
    )(meta, resid, bias, *acts, *weights, *after)


def sort_sums_kernel(meta, late, early, wide, mine, theirs):
    rows = [late[i : i + 1] for i in range(3)] + [early[i : i + 1] for i in range(3)]
    rows = rows + [wide[...], early[3:4]]
    first = meta[0] == 0
    start = 0
    for row in rows:
        half = row.shape[1] // 2
        low, high = row[:, :half], row[:, half:]
        mine[:, start : start + half] = jnp.where(first, low, high)
        theirs[:, start : start + half] = jnp.where(first, high, low)
        start = start + half


def sort_sums(meta, late, early, wide, after=()):
    size = (7 * late.shape[1] + wide.shape[1]) // 2
    vmem = pl.BlockSpec(memory_space=pltpu.VMEM)
    kernel, waits = ordered(sort_sums_kernel, 4, after)
    return pl.pallas_call(
        kernel,
        in_specs=[pl.BlockSpec(memory_space=pltpu.SMEM), vmem, vmem, vmem] + waits,
        out_specs=[vmem] * 2,
        out_shape=[jax.ShapeDtypeStruct((1, size), F32)] * 2,
        name="sort_sums",
    )(meta, late, early, wide, *after)


def input_grads_kernel(n, meta, gz, first, second, input_ref, skip_ref):
    low = times_transposed(gz[...], first[...])
    high = times_transposed(gz[...], second[...])
    if n == 1:
        input_ref[...] = low
        skip_ref[...] = high
        return

    @pl.when(meta[0] == 0)
    def _():
        input_ref[...] = low
        skip_ref[...] = high

    @pl.when(meta[0] != 0)
    def _():
        input_ref[...] = high
        skip_ref[...] = low


def input_grads(meta, gz, weights, after=()):
    tok, width = gz.shape
    n = len(weights)
    steps = 4
    tile = width // steps
    if n == 1:
        weights = [weights[0], weights[0]]
    out = pl.BlockSpec((tok, tile), lambda t, m: (0, t))
    kernel, waits = ordered(functools.partial(input_grads_kernel, n), 4, after)
    return pl.pallas_call(
        kernel,
        grid_spec=pltpu.PrefetchScalarGridSpec(
            num_scalar_prefetch=1,
            grid=(steps,),
            in_specs=[
                pl.BlockSpec((tok, width), lambda t, m: (0, 0)),
                pl.BlockSpec((tile, width), lambda t, m: (t, 0)),
                pl.BlockSpec((tile, width), lambda t, m: (t + (steps if n == 1 else 0), 0)),
            ]
            + waits,
            out_specs=[out, out],
        ),
        out_shape=[jax.ShapeDtypeStruct((tok, width), F32)] * 2,
        name="input_grads",
    )(meta, gz, *weights, *after)


def pack_kernel(*refs):
    out = refs[-1]
    start = 0
    for ref in refs[:-1]:
        size = ref.shape[0]
        out[0, start : start + size] = ref[...]
        start = start + size


def pack(vectors):
    total = sum(v.shape[0] for v in vectors)
    return pl.pallas_call(
        pack_kernel, out_shape=jax.ShapeDtypeStruct((1, total), vectors[0].dtype), name="pack"
    )(*vectors)


def unpack_kernel(sizes, meta, own, other, *outs):
    start = 0
    for size, out in zip(sizes, outs):
        for ref, core in ((own, meta[0]), (other, 1 - meta[0])):
            at = pl.multiple_of(core * size, 128)
            out[:, pl.ds(at, size)] = ref[:, start : start + size].astype(F32)
        start = start + size


def unpack(meta, own, other, sizes, after=()):
    vmem = pl.BlockSpec(memory_space=pltpu.VMEM)
    kernel, waits = ordered(functools.partial(unpack_kernel, sizes), 3, after)
    return pl.pallas_call(
        kernel,
        in_specs=[pl.BlockSpec(memory_space=pltpu.SMEM), vmem, vmem] + waits,
        out_specs=[vmem] * len(sizes),
        out_shape=[jax.ShapeDtypeStruct((1, 2 * n), F32) for n in sizes],
        name="unpack",
    )(meta, own, other, *after)


def fold_kernel(terms, out):
    total = terms[0].astype(F32)
    for i in range(1, terms.shape[0]):
        total = total + terms[i].astype(F32)
    total = total.astype(BF16)
    for i in range(out.shape[0]):
        out[i] = total


def fold(terms, copies, after=()):
    n, rows, width = terms.shape
    tile = width
    while tile % 256 == 0 and tile > 1024:
        tile //= 2
    kernel, waits = ordered(fold_kernel, 1, after)
    return pl.pallas_call(
        kernel,
        grid=(width // tile,),
        in_specs=[pl.BlockSpec((n, rows, tile), lambda c: (0, 0, c))] + waits,
        out_specs=pl.BlockSpec((copies, rows, tile), lambda c: (0, 0, c)),
        out_shape=jax.ShapeDtypeStruct((copies, rows, width), BF16),
        name="fold",
    )(terms, *after)


def place_kernel(meta, own, by_x, by_y, far_low, far_high, out):
    part = pl.program_id(0)
    for i, ref in enumerate((own, by_x, by_y)):

        @pl.when(part == i)
        def _(ref=ref):
            out[...] = ref[...].astype(F32)

    @pl.when(part == 3)
    def _():
        half = far_low.shape[1]
        out[:, :half] = far_low[...].astype(F32)
        out[:, half:] = far_high[...].astype(F32)


def place(meta, parts, start, rows, after=()):
    width = parts[0].shape[1]
    tile = rows
    while start % tile or tile * width > 262144:
        tile //= 2
    base, steps = start // tile, rows // tile

    def spec(i, columns):
        def index(q, c, m):
            return (base + jnp.where(q == i, c, jnp.where(q < i, 0, steps - 1)), 0)

        return pl.BlockSpec((tile, columns), index)

    kernel, waits = ordered(place_kernel, 6, after)
    return pl.pallas_call(
        kernel,
        grid_spec=pltpu.PrefetchScalarGridSpec(
            num_scalar_prefetch=1,
            grid=(4, steps),
            in_specs=[spec(i, width) for i in range(3)] + [spec(3, width // 2)] * 2 + waits,
            out_specs=pl.BlockSpec((tile, width), lambda q, c, m: ((m[0] ^ q) * steps + c, 0)),
        ),
        out_shape=jax.ShapeDtypeStruct((4 * rows, width), F32),
        name="place",
    )(meta, *parts, *after)


class Links:
    def __init__(self):
        self.sent = {"x": [], "y": [], "z": [], "frames": []}

    def send(self, link, array, move, *pins):
        waits = [p for p in pins if p is not None]
        earlier = self.sent[link]
        depth = 2 if link in ("x", "y") else 1
        if len(earlier) >= depth:
            waits.append(earlier[-depth])
        if waits:
            array = tie(array, *waits)
        moved = move(array)
        earlier.append(moved)
        return moved


def tie(array, *others):
    return lax.optimization_barrier((array, *others))[0]


def body(
    frames_in,
    skip_in,
    lengths,
    cotangent,
    w_skip,
    w_qkv,
    w_out,
    w_up,
    w_down,
    skip_bias,
    norm1_gain,
    norm1_bias,
    out_bias,
    norm2_gain,
    norm2_bias,
    up_bias,
    down_bias,
):
    tok = frames_in.shape[3]
    width = frames_in.shape[4]
    frames = frames_in.reshape(tok, width)
    skips = skip_in.reshape(tok, width)
    cotan = cotangent.reshape(tok, width)
    n_batch = lax.axis_size("batch")
    n_seq = lax.axis_size("seq")
    n_frames = lax.axis_size("frames")
    assert n_batch == 4 and n_seq % 2 == 0
    paired = n_frames == 2
    plane = lax.axis_index("batch").astype(jnp.int32)
    shard = lax.axis_index("seq").astype(jnp.int32)
    core = lax.axis_index("frames").astype(jnp.int32)
    links = Links()

    def swap_frames(array):
        return lax.ppermute(array, "frames", [(0, 1), (1, 0)])

    def over_x(array):
        return lax.ppermute(array, "batch", [(i, i ^ 1) for i in range(n_batch)])

    def over_y(array):
        return lax.ppermute(array, "batch", [(i, i ^ 2) for i in range(n_batch)])

    def from_seq(step):
        return lambda array: lax.ppermute(
            array, "seq", [((i + step) % n_seq, i) for i in range(n_seq)]
        )

    def to_seq(step):
        return from_seq(n_seq - step)

    def exchange_seq(array):
        return lax.all_to_all(array, "seq", split_axis=0, concat_axis=0, tiled=True)

    def send_rows(array, *pins):
        if paired:
            return swap_frames(tie(array, *pins) if pins else array)
        return lax.all_gather(array, "frames", axis=0, tiled=True)

    def gather_frames(array, *pins):
        moved = send_rows(array, *pins)
        return [array, moved] if paired else [moved]

    def send_left(parts, *pins):
        if paired:
            return [parts[0], swap_frames(tie(parts[1], *pins) if pins else parts[1])]
        array = parts[0]
        split = array.reshape(array.shape[0], n_frames, array.shape[1] // n_frames)
        moved = lax.all_to_all(split, "frames", split_axis=1, concat_axis=0, tiled=True)
        return [moved.reshape(array.shape[0] * n_frames, array.shape[1] // n_frames)]

    def by_plane(source):
        block = source.shape[1] // n_batch
        return jnp.concatenate(
            [
                lax.dynamic_slice_in_dim(source, (plane ^ bits) * block, block, 1)
                for bits in TURNS
            ],
            axis=1,
        )

    def turned(sources):
        return stack(sources if paired else [by_plane(source) for source in sources])

    def stack(arrays):
        return arrays[0] if len(arrays) == 1 else jnp.concatenate(arrays, axis=0)

    class Chain:
        def __init__(self, terms):
            self.terms = terms
            self.half = terms[0][1][0].shape[1] // 2
            self.blocks = [lefts[0].shape[1] // n_batch for lefts, _ in terms]
            self.block = sum(self.blocks)

        def gemm(self, plane_blocks, low, high):
            whole = len(self.terms) == 1
            first, last = plane_blocks[0], plane_blocks[-1] + 1
            spans = [(first, last)] if whole else [(p, p + 1) for p in plane_blocks]
            outs = []
            for p, q in spans:
                for (lefts, rights), block in zip(self.terms, self.blocks):
                    total = None
                    for left, right in zip(lefts, rights):
                        term = contract_rows(
                            left[:, p * block : q * block], right[:, low:high]
                        )
                        total = term if total is None else total + term
                    outs.append(total)
            return stack(outs)

        def begin(self, *pins):
            half = self.half
            if pins:
                lefts, rights = self.terms[0]
                self.terms[0] = ([tie(lefts[0], *pins), *lefts[1:]], rights)
            self.to_x = self.gemm((1, 2), 0, half).astype(BF16)
            self.to_y = self.gemm((2, 3), half, 2 * half).astype(BF16)
            return self.to_x, self.to_y

        def first(self, *pins):
            self.from_x = links.send("x", self.to_x, over_x, *pins)
            self.from_y = links.send("y", self.to_y, over_y, *pins)

        def between(self, *pins):
            half, block = self.half, self.block
            from_x, from_y = self.from_x, self.from_y
            if pins:
                from_x, from_y = tie(from_x, *pins), tie(from_y, *pins)
            low = self.gemm((3,), 0, half) + from_x[block:].astype(F32)
            high = self.gemm((1,), half, 2 * half) + from_y[:block].astype(F32)
            self.next_y, self.next_x = low.astype(BF16), high.astype(BF16)
            return self.next_x, self.next_y

        def second(self, *pins):
            self.then_y = links.send("y", self.next_y, over_y, *pins)
            self.then_x = links.send("x", self.next_x, over_x, *pins)

        def own_sum(self, *pins):
            block, half = self.block, self.half
            then_x, then_y = self.then_x, self.then_y
            if pins:
                then_x, then_y = tie(then_x, *pins), tie(then_y, *pins)
            low = self.from_x[:block].astype(F32) + then_y.astype(F32)
            high = self.from_y[block:].astype(F32) + then_x.astype(F32)
            own = self.gemm((0,), 0, 2 * half) + jnp.concatenate([low, high], axis=1)
            self.own = own.astype(BF16).reshape(n_seq, block // n_seq, 2 * half)
            return self.own

        def across(self, *pins):
            self.terms_seq = links.send("z", self.own, exchange_seq, *pins)

        def along(self, after=(), *pins):
            self.folded = fold(self.terms_seq, n_seq, after)
            whole = links.send("z", self.folded, exchange_seq, *pins)
            self.whole = whole.reshape(self.block, 2 * self.half)
            return self.folded

        def spread(self, *pins):
            self.by_x = links.send("x", self.whole, over_x, *pins)
            self.by_y = links.send("y", self.whole, over_y, *pins)

        def finish(self, *pins):
            half = self.half
            self.far_low = links.send("x", self.by_y[:, :half], over_x, *pins)
            self.far_high = links.send("y", self.by_x[:, half:], over_y, *pins)

        def place(self, after=()):
            parts = (self.whole, self.by_x, self.by_y, self.far_low, self.far_high)
            starts = [sum(self.blocks[:i]) for i in range(len(self.blocks))]
            return [
                place(plane.reshape(1), parts, start, rows, after)
                for start, rows in zip(starts, self.blocks)
            ]

    vectors_in = (
        skip_bias,
        norm1_gain,
        norm1_bias,
        out_bias,
        norm2_gain,
        norm2_bias,
        up_bias,
        down_bias,
    )
    sizes = [v.shape[0] for v in vectors_in]
    starts = [sum(sizes[:i]) for i in range(len(sizes))]
    packed = pack(vectors_in)
    meta = jnp.concatenate([jnp.stack([core, shard, plane]), lengths.reshape(-1)])
    full_skip = gather_frames(w_skip, packed)

    if paired:
        packs = [packed, swap_frames(packed)]
        full_qkv = gather_frames(w_qkv, full_skip[1])
        full_down = gather_frames(w_down, full_skip[1])
        hidden_z, n1, own_in, other_in = front(
            meta, frames, skips, full_skip, packs, tuple(sizes)
        )
        vectors = unpack(meta, *packs, sizes, after=(n1,))
        inputs = [own_in, other_in]
    else:
        packed = lax.all_gather(packed, "frames", axis=0, tiled=True).astype(F32)
        vectors = [packed[:, b : b + n].reshape(1, -1) for b, n in zip(starts, sizes)]
        hidden_z, n1 = front_whole(frames, skips, full_skip[0], *vectors[:3])
        inputs = [jnp.concatenate([frames, skips], axis=1)]
        full_qkv, full_down = gather_frames(w_qkv), gather_frames(w_down)
    obias, gain2, bias2, ubias, dbias = vectors[3:]
    gain1 = vectors[1]
    n1_all = [n1] + [from_seq(j)(n1) for j in range(1, n_seq)]
    full_up = gather_frames(w_up, full_down[-1], n1)
    gact = [times_transposed(tie(cotan, n1), full_down[0])]
    if paired:
        gact.append(times_transposed(tie(cotan, gact[0]), full_down[1]))
    queries, key_rows, value_rows, *n1_parts = project(
        meta, n1_all, full_qkv, after=(*gact, gain1)
    )
    full_out = gather_frames(w_out, queries)
    both_cotan = [cotan, swap_frames(tie(cotan, queries))] if paired else None
    if not paired:
        both_cotan = [lax.all_gather(cotan, "frames", axis=0, tiled=True)]
    left_n1 = send_left(n1_parts)
    attended, prob = attend_forward(meta, queries, key_rows, value_rows)
    both_cotan = stack(both_cotan)
    left_n1 = left_n1 if paired else [by_plane(a) for a in left_n1]
    (
        resid,
        gup,
        grad_resid,
        grad_branch,
        grad_heads,
        up_sum,
        sums2,
        *parts,
    ) = centre(
        meta,
        attended,
        hidden_z,
        cotan,
        full_out,
        full_up,
        gact,
        ubias,
        obias,
        gain2,
        bias2,
        after=(both_cotan, *left_n1),
    )
    n = len(full_out)
    acts, n2_parts, att_parts = parts[:n], parts[n : 2 * n], parts[2 * n :]

    def right_rows(array, *pins):
        moved = send_rows(array, *pins)
        return stack([array, moved] if paired else [moved])

    down = Chain([([turned(send_left(acts))], [both_cotan])])
    down_first = down.begin()
    down.first()
    both_up = right_rows(gup)
    left_n2 = turned(send_left(n2_parts))
    grads = attend_backward(queries, key_rows, value_rows, grad_heads, prob, after=down_first)
    up = Chain([([left_n2], [both_up])])
    terms_n1, flat = unproject(meta, grads, full_qkv, n_seq, after=down_first)
    down_second = down.between(flat)
    down.second()
    up_first = up.begin(*down_second)
    up.first()
    terms_n1 = links.send("z", terms_n1, exchange_seq)
    both_flat = gather_frames(flat, *up_first)
    qkv = Chain([(left_n1, both_flat)])
    down_own = down.own_sum(*up_first)
    grad_z, sums1 = rear(
        terms_n1, hidden_z, grad_resid, gain1, after=(down_own, both_flat[-1])
    )
    up.between()
    up.second()
    down.across()
    left_joined = turned(send_left(inputs, grad_z))
    left_att = turned(send_left(att_parts, grad_z))
    both_branch = right_rows(grad_branch, left_joined)
    rest = Chain([([left_joined], [right_rows(grad_z, left_att)]), ([left_att], [both_branch])])
    qkv_first = qkv.begin(up.next_x, up.next_y)
    qkv.first()
    up_own = up.own_sum(*qkv_first)
    up.across()
    rest_first = rest.begin(up_own)
    rest.first()
    qkv_second = qkv.between(*rest_first)
    qkv.second()
    down_fold = down.along(qkv_second)
    rest_second = rest.between(down_fold)
    rest.second()
    up_fold = up.along(rest_second, rest.from_x, rest.from_y, qkv.then_x, qkv.then_y)
    qkv_own = qkv.own_sum(up_fold)
    down.spread()
    if paired:
        output = forward(meta, resid, dbias, acts, full_down, after=(qkv_own,))
        mine, theirs = sort_sums(meta, sums1, sums2, up_sum, after=rest_first)
        mine = mine + swap_frames(theirs)
    else:
        output = (resid + times(acts[0], full_down[0]) + dbias).astype(BF16)
        summed = (
            *(sums1[i] for i in range(3)),
            *(sums2[i] for i in range(3)),
            up_sum[0],
            sums2[3],
        )
        summed = jnp.concatenate([v.reshape(n_frames, -1) for v in summed], axis=1)
        mine = lax.psum_scatter(summed, "frames", scatter_dimension=0, tiled=True)
    rest_own = rest.own_sum(output)
    qkv.across(rest.then_x, rest.then_y)
    up.spread()
    input_grad, skip_grad = input_grads(meta, grad_z, full_skip, after=(rest_own,))
    down.finish()
    qkv.along((input_grad,), down.by_x, down.by_y)
    rest.across(up.by_x, up.by_y)
    qkv.spread()
    (grad_w_down,) = down.place()
    up.finish(grad_w_down)
    rest.along((mine,), down.far_low, down.far_high)
    copies = jnp.broadcast_to(mine[None], (n_batch * n_seq,) + mine.shape)

    def exchange_all(array):
        return lax.all_to_all(array, ("batch", "seq"), split_axis=0, concat_axis=0, tiled=True)

    qkv.finish()
    total = links.send("z", copies, exchange_all, qkv.far_low, qkv.far_high)
    total = jnp.sum(total, axis=0).reshape(-1)
    vector_grads = [total[b : b + n] for b, n in zip(starts, sizes)]
    (grad_w_up,) = up.place()
    rest.spread(grad_w_up)
    (grad_w_qkv,) = qkv.place()
    rest.finish(grad_w_qkv, *vector_grads[:1])
    grad_w_skip, grad_w_out = rest.place(after=(grad_w_qkv,))

    def back(array):
        return array.reshape(1, 1, 1, tok, width)

    return (
        back(output),
        back(input_grad),
        back(skip_grad),
        grad_w_skip,
        grad_w_qkv,
        grad_w_out,
        grad_w_up,
        grad_w_down,
        *vector_grads,
    )


def solution(mesh):
    rows = P("batch", "seq", "frames", None, None)
    in_specs = (
        (rows, rows, P("batch", "frames", None), rows)
        + (P("frames", None),) * 5
        + (P("frames"),) * 8
    )
    out_specs = (rows,) * 3 + (P("frames", None),) * 5 + (P("frames"),) * 8
    return jax.shard_map(body, mesh=mesh, in_specs=in_specs, out_specs=out_specs, check_vma=False)
```

```python
import functools

import jax
import jax.numpy as jnp
from jax import lax
from jax.experimental import pallas as pl
from jax.experimental.pallas import tpu as pltpu
from jax.sharding import PartitionSpec as P

HEADS = 16
HD = 64
UTTS = 3
EPS = 1e-05
MASKED = 1e12
BF16 = jnp.bfloat16
F32 = jnp.float32
INV_SQRT2 = 0.7071067811865476
INV_SQRT_2PI = 0.3989422804014327
ERFC_STEP = 0.4
ERFC_TERMS = (
    0.22567586186829244 / 2,
    0.22566960544571626 / 2,
    0.20784251123900896 / 2,
    0.16854379658168633 / 2,
    0.14142295790506823 / 2,
    -0.005586494604590357 / 2,
    0.16905696704198306 / 2,
    -0.18288169574958996 / 2,
    0.05025661354969599 / 2,
)


def contract_rows(left_side, right_side):
    return lax.dot_general(
        left_side, right_side, (((0,), (0,)), ((), ())), preferred_element_type=F32
    )


def times_transposed(left_side, right_side):
    return lax.dot_general(
        left_side, right_side, (((1,), (1,)), ((), ())), preferred_element_type=F32
    )


def times(left_side, right_side):
    return jnp.dot(left_side, right_side, preferred_element_type=F32)


def ordered(kernel, count, after):
    n = len(after)

    def run(*refs):
        kernel(*refs[:count], *refs[count + n :])

    return run, [pl.BlockSpec(memory_space=pl.ANY)] * n


TURNS = (0, 1, 3, 2)


def turn(block, plane):
    bits = block ^ plane
    return bits ^ (bits >> 1)


def put_turned(part, read, plane):
    block = part.shape[-1] // len(TURNS)
    for i, bits in enumerate(TURNS):
        at = pl.multiple_of((plane ^ bits) * block, 128)
        part[:, i * block : (i + 1) * block] = read(at, block)


def pair_rows(block, lane):
    zero = jnp.zeros_like(block)
    return jnp.concatenate(
        [jnp.where(lane < HD, block, zero), jnp.where(lane >= HD, block, zero)], axis=0
    )


def utterance_ends(meta):
    ends = [meta[3]]
    for j in range(1, UTTS):
        ends.append(ends[-1] + meta[3 + j])
    return ends


def attend_forward_kernel(meta, q_ref, k_ref, v_ref, out_ref, prob_ref, dist):
    tok = q_ref.shape[0]
    length = k_ref.shape[0]
    shard = meta[1]
    ends = utterance_ends(meta)

    @pl.when(pl.program_id(0) == 0)
    def _():
        row = lax.broadcasted_iota(jnp.int32, (length, 2 * tok), 0)
        col = lax.broadcasted_iota(jnp.int32, (length, 2 * tok), 1)
        k_pos = row + shard * tok
        k_pos = jnp.where(k_pos >= length, k_pos - length, k_pos)
        q_pos = jnp.where(col >= tok, col - tok, col) + shard * tok
        k_seg = jnp.zeros_like(k_pos)
        q_seg = jnp.zeros_like(q_pos)
        for j in range(UTTS):
            k_seg = k_seg + (k_pos >= ends[j]).astype(jnp.int32)
            q_seg = q_seg + (q_pos >= ends[j]).astype(jnp.int32)
        allowed = (k_seg == q_seg) & (k_seg < UTTS)
        dist[...] = jnp.where(allowed, jnp.abs(k_pos - q_pos).astype(F32), MASKED)

    lane = lax.broadcasted_iota(jnp.int32, (tok, 2 * HD), 1)
    pair = pair_rows(q_ref[...] * jnp.asarray(HD**-0.5, BF16), lane)
    head = 2 * pl.program_id(0) + 1 + (lax.broadcasted_iota(jnp.int32, (1, 2 * tok), 1) >= tok)
    slope = jnp.exp2(head.astype(F32) * (-8.0 / HEADS))
    scores = times_transposed(k_ref[...], pair) - slope * dist[...]
    top = jnp.max(scores, axis=0, keepdims=True)
    exp_scores = jnp.exp(scores - top)
    total = jnp.sum(exp_scores, axis=0, keepdims=True)
    prob = (exp_scores * (1.0 / total)).astype(BF16)
    prob_ref[0] = prob
    mixed = times(v_ref[...].T, prob).T
    mixed = jnp.where(lane < HD, mixed[:tok], mixed[tok:])
    row = lax.broadcasted_iota(jnp.int32, (tok, 2 * HD), 0) + shard * tok
    out_ref[...] = jnp.where(row < ends[UTTS - 1], mixed, 0.0).astype(BF16)


def attend_backward_kernel(q_ref, k_ref, v_ref, grad_ref, prob_ref, out_ref):
    tok = q_ref.shape[0]
    lane = lax.broadcasted_iota(jnp.int32, (tok, 2 * HD), 1)
    scale = jnp.asarray(HD**-0.5, BF16)
    pair_q = pair_rows(q_ref[...] * scale, lane)
    pair_g = pair_rows(grad_ref[...], lane)
    prob_low = prob_ref[0]
    prob = prob_low.astype(F32)
    prob_grad = times_transposed(v_ref[...], pair_g)
    weighted = prob * prob_grad
    delta = jnp.sum(weighted, axis=0, keepdims=True)
    score_low = (weighted - prob * delta).astype(BF16)
    out_ref[2] = times(prob_low, pair_g).astype(BF16)
    out_ref[1] = times(score_low, pair_q).astype(BF16)
    mixed = times((k_ref[...] * scale).T, score_low).T
    out_ref[0, :tok] = jnp.where(lane < HD, mixed[:tok], mixed[tok:]).astype(BF16)
    out_ref[0, tok:] = jnp.zeros_like(out_ref[0, tok:])


def attend_forward(meta, queries, key_rows, value_rows, after=()):
    tok, width = queries.shape
    length = key_rows.shape[0]
    pairs = width // (2 * HD)
    kernel, waits = ordered(attend_forward_kernel, 4, after)
    return pl.pallas_call(
        kernel,
        grid_spec=pltpu.PrefetchScalarGridSpec(
            num_scalar_prefetch=1,
            grid=(pairs,),
            in_specs=[
                pl.BlockSpec((tok, 2 * HD), lambda g, m: (0, g)),
                pl.BlockSpec((length, 2 * HD), lambda g, m: (0, g)),
                pl.BlockSpec((length, 2 * HD), lambda g, m: (0, g)),
            ]
            + waits,
            out_specs=[
                pl.BlockSpec((tok, 2 * HD), lambda g, m: (0, g)),
                pl.BlockSpec((1, length, 2 * tok), lambda g, m: (g, 0, 0)),
            ],
            scratch_shapes=[pltpu.VMEM((length, 2 * tok), F32)],
        ),
        out_shape=[
            jax.ShapeDtypeStruct((tok, width), BF16),
            jax.ShapeDtypeStruct((pairs, length, 2 * tok), BF16),
        ],
        name="attend_forward",
    )(meta, queries, key_rows, value_rows, *after)


def attend_backward(queries, key_rows, value_rows, grad_heads, prob, after=()):
    tok, width = queries.shape
    length = key_rows.shape[0]
    pairs = width // (2 * HD)
    q_spec = pl.BlockSpec((tok, 2 * HD), lambda g: (0, g))
    k_spec = pl.BlockSpec((length, 2 * HD), lambda g: (0, g))
    kernel, waits = ordered(attend_backward_kernel, 5, after)
    return pl.pallas_call(
        kernel,
        grid=(pairs,),
        in_specs=[
            q_spec,
            k_spec,
            k_spec,
            q_spec,
            pl.BlockSpec((1, length, 2 * tok), lambda g: (g, 0, 0)),
        ]
        + waits,
        out_specs=pl.BlockSpec((3, length, 2 * HD), lambda g: (0, 0, g)),
        out_shape=jax.ShapeDtypeStruct((3, length, width), BF16),
        name="attend_backward",
    )(queries, key_rows, value_rows, grad_heads, prob, *after)


def statistics(values):
    mean = jnp.mean(values, axis=-1, keepdims=True)
    centred = values - mean
    variance = jnp.mean(centred * centred, axis=-1, keepdims=True)
    return centred, lax.rsqrt(variance + EPS)


def norm_back(unit, rstd, gain, grad):
    scaled = grad * gain
    mean_e = jnp.mean(scaled, axis=-1, keepdims=True)
    mean_eu = jnp.mean(scaled * unit, axis=-1, keepdims=True)
    return rstd * (scaled - mean_e - unit * mean_eu)


def bases(core, n_pieces, rows):
    if n_pieces == 1:
        return [0]
    return [pl.multiple_of(core * rows, 128), pl.multiple_of((1 - core) * rows, 128)]


def front_kernel(n, sizes, meta, *refs):
    x_refs, refs = refs[:2], refs[2:]
    w_refs, packs, outs = refs[:n], refs[n : 2 * n], refs[2 * n :]
    z_ref, n1_ref, own_ref, other_ref = outs
    step = pl.program_id(0)
    first = meta[0] == 0

    def vector(i):
        start = sum(sizes[:i])
        parts = [ref[:, start : start + sizes[i]].astype(F32) for ref in packs]
        low = jnp.where(first, parts[0], parts[1])
        high = jnp.where(first, parts[1], parts[0])
        return jnp.concatenate([low, high], axis=1)

    x, s = x_refs[0][...], x_refs[1][...]
    own = jnp.where(first, x, s)
    other = jnp.where(first, s, x)
    own_ref[...] = own
    other_ref[...] = other
    part = times(own, w_refs[0][...]) + times(other, w_refs[1][...])

    @pl.when(step == 0)
    def _():
        z_ref[...] = part + vector(0)

    @pl.when(step > 0)
    def _():
        z_ref[...] += part

    @pl.when(step == pl.num_programs(0) - 1)
    def _():
        centred, rstd = statistics(z_ref[...])
        n1_ref[...] = (centred * rstd * vector(1) + vector(2)).astype(BF16)


def front(meta, frames, skips, weights, packs, sizes, after=()):
    tok = frames.shape[0]
    rows, width = weights[0].shape
    n = len(weights)
    steps = 4
    block = rows // steps
    packed = pl.BlockSpec(packs[0].shape, lambda k, m: (0, 0))
    whole = pl.BlockSpec((tok, width), lambda k, m: (0, 0))
    columns = pl.BlockSpec((tok, block), lambda k, m: (0, k))
    turned = pl.BlockSpec((tok, block), lambda k, m: (0, turn(k, m[2])))
    kernel, waits = ordered(functools.partial(front_kernel, n, sizes), 3 + 2 * n, after)
    return pl.pallas_call(
        kernel,
        grid_spec=pltpu.PrefetchScalarGridSpec(
            num_scalar_prefetch=1,
            grid=(steps,),
            in_specs=[columns] * 2
            + [pl.BlockSpec((block, width), lambda k, m: (k, 0))] * n
            + [packed] * n
            + waits,
            out_specs=[whole, whole, turned, turned],
        ),
        out_shape=[
            jax.ShapeDtypeStruct((tok, width), F32),
            jax.ShapeDtypeStruct((tok, width), BF16),
            jax.ShapeDtypeStruct((tok, rows), BF16),
            jax.ShapeDtypeStruct((tok, rows), BF16),
        ],
        name="front",
    )(meta, frames, skips, *weights, *packs, *after)


def front_whole_kernel(x_ref, s_ref, first_ref, second_ref, bias, gain, shift, z_ref, n1_ref):
    step = pl.program_id(0)
    part = times(x_ref[...], first_ref[...]) + times(s_ref[...], second_ref[...])

    @pl.when(step == 0)
    def _():
        z_ref[...] = part + bias[...]

    @pl.when(step > 0)
    def _():
        z_ref[...] += part

    @pl.when(step == pl.num_programs(0) - 1)
    def _():
        centred, rstd = statistics(z_ref[...])
        n1_ref[...] = (centred * rstd * gain[...] + shift[...]).astype(BF16)


def front_whole(frames, skips, weight, bias, gain, shift):
    tok, width = frames.shape
    steps = 4
    block = width // steps
    vector = pl.BlockSpec((1, width), lambda k: (0, 0))
    whole = pl.BlockSpec((tok, width), lambda k: (0, 0))
    return pl.pallas_call(
        front_whole_kernel,
        grid=(steps,),
        in_specs=[pl.BlockSpec((tok, block), lambda k: (0, k))] * 2
        + [
            pl.BlockSpec((block, width), lambda k: (k, 0)),
            pl.BlockSpec((block, width), lambda k: (k + steps, 0)),
        ]
        + [vector] * 3,
        out_specs=[whole, whole],
        out_shape=[
            jax.ShapeDtypeStruct((tok, width), F32),
            jax.ShapeDtypeStruct((tok, width), BF16),
        ],
        name="front",
    )(frames, skips, weight, weight, bias, gain, shift)


def project_kernel(n, chunks, meta, *refs):
    x_refs = refs[:chunks]
    w_refs = refs[chunks : chunks + 3 * n]
    q_ref, k_ref, v_ref = refs[chunks + 3 * n : chunks + 3 * n + 3]
    parts = refs[chunks + 3 * n + 3 :]
    rows = w_refs[0].shape[0]
    tok = q_ref.shape[0]
    starts = bases(meta[0], n, rows)

    @pl.when(pl.program_id(0) == 0)
    def _():
        for start, part in zip(starts, parts):
            for c in range(chunks):
                if n == 1:
                    part[c * tok : (c + 1) * tok] = x_refs[c][...]
                    continue
                put_turned(
                    part.at[c * tok : (c + 1) * tok],
                    lambda at, block: x_refs[c][:, pl.ds(pl.multiple_of(start + at, 128), block)],
                    meta[2],
                )

    for c in range(chunks):
        for i, out in enumerate((q_ref, k_ref, v_ref)):
            if i == 0 and c > 0:
                continue
            total = None
            for p, start in enumerate(starts):
                term = times(x_refs[c][:, pl.ds(start, rows)], w_refs[3 * p + i][...])
                total = term if total is None else total + term
            out[c * tok : (c + 1) * tok] = total.astype(BF16)


def project(meta, chunks, weights, after=()):
    tok, width = chunks[0].shape
    rows = weights[0].shape[0]
    n = len(weights)
    tile = 256
    tiles = width // tile

    def w_spec(i):
        return pl.BlockSpec((rows, tile), lambda t, m: (0, t + i * tiles))

    length = tok * len(chunks)
    kernel, waits = ordered(
        functools.partial(project_kernel, n, len(chunks)), 1 + len(chunks) + 3 * n, after
    )
    return pl.pallas_call(
        kernel,
        grid_spec=pltpu.PrefetchScalarGridSpec(
            num_scalar_prefetch=1,
            grid=(tiles,),
            in_specs=[pl.BlockSpec((tok, width), lambda t, m: (0, 0))] * len(chunks)
            + [w_spec(i) for i in range(3)] * n
            + waits,
            out_specs=[
                pl.BlockSpec((tok, tile), lambda t, m: (0, t)),
                pl.BlockSpec((length, tile), lambda t, m: (0, t)),
                pl.BlockSpec((length, tile), lambda t, m: (0, t)),
            ]
            + [pl.BlockSpec((length, rows), lambda t, m: (0, 0))] * n,
        ),
        out_shape=[
            jax.ShapeDtypeStruct((tok, width), BF16),
            jax.ShapeDtypeStruct((length, width), BF16),
            jax.ShapeDtypeStruct((length, width), BF16),
        ]
        + [jax.ShapeDtypeStruct((length, rows), BF16)] * n,
        name="project",
    )(meta, *chunks, *[w for w in weights for _ in range(3)], *after)


def centre_kernel(n, meta, *refs):
    refs = list(refs)

    def take(count):
        taken = refs[:count]
        del refs[:count]
        return taken

    att, z_ref, cotan = take(3)
    w_out, w_up, gact = take(n), take(n), take(n)
    up_bias, out_bias, gain, shift = take(4)
    resid, gup_ref, gres, gbranch, gatt, up_sum, sums = take(7)
    acts, n2_parts, att_parts = take(n), take(n), take(n)
    n2, gn2, unit, rstd = refs
    step, steps = pl.program_id(0), pl.num_programs(0)
    tok = att.shape[0]
    core, live = meta[0], utterance_ends(meta)[-1] - meta[1] * tok
    rows = w_out[0].shape[0]
    starts = bases(core, n, rows)

    @pl.when(step == 0)
    def _():
        total = z_ref[...] + out_bias[...]
        for start, w_ref, part in zip(starts, w_out, att_parts):
            total = total + times(att[:, pl.ds(start, rows)], w_ref[...])
        resid[...] = total
        centred, scale = statistics(total)
        unit[...] = centred * scale
        rstd[...] = scale
        n2[...] = (unit[...] * gain[...] + shift[...]).astype(BF16)
        for start, n2_part, att_part in zip(starts, n2_parts, att_parts):
            for part, source in ((n2_part, n2), (att_part, att)):
                if n == 1:
                    part[...] = source[...]
                    continue
                put_turned(
                    part,
                    lambda at, block: source[:, pl.ds(pl.multiple_of(start + at, 128), block)],
                    meta[2],
                )
        gn2[...] = jnp.zeros_like(gn2)

    pre = up_bias[...]
    for start, w_ref in zip(starts, w_up):
        pre = pre + times(n2[:, pl.ds(start, rows)], w_ref[...])
    gauss = jnp.exp(pre * pre * (-0.5))
    t = 1.0 / (1.0 + (ERFC_STEP * INV_SQRT2) * jnp.abs(pre))
    tail = jnp.full_like(t, ERFC_TERMS[-1])
    for term in ERFC_TERMS[-2::-1]:
        tail = tail * t + term
    tail = tail * t * gauss
    cdf = jnp.where(pre < 0.0, tail, 1.0 - tail)
    act = (pre * cdf).astype(BF16)
    if n == 1:
        acts[0][...] = act
        grad = gact[0][...]
    else:
        mine = (step // (steps // 2)) == core

        @pl.when(mine)
        def _():
            acts[0][...] = act

        @pl.when(jnp.logical_not(mine))
        def _():
            acts[1][...] = act

        grad = jnp.where(mine, gact[0][...], gact[1][...])
    gup = (grad * (cdf + pre * gauss * INV_SQRT_2PI)).astype(BF16)
    gup_ref[...] = gup
    up_sum[...] = jnp.sum(gup.astype(F32), axis=0, keepdims=True)
    for start, w_ref in zip(starts, w_up):
        gn2[:, pl.ds(start, rows)] += times_transposed(gup, w_ref[...])

    @pl.when(step == steps - 1)
    def _():
        grad_n2 = gn2[...]
        total = cotan[...].astype(F32) + norm_back(unit[...], rstd[...], gain[...], grad_n2)
        gres[...] = total
        low = total.astype(BF16)
        gbranch[...] = low
        alive = lax.broadcasted_iota(jnp.int32, (tok, 1), 0) < live
        for start, w_ref in zip(starts, w_out):
            term = times_transposed(low, w_ref[...])
            gatt[:, pl.ds(start, rows)] = jnp.where(alive, term, 0.0).astype(BF16)
        sums[0:1] = jnp.sum(low.astype(F32), axis=0, keepdims=True)
        sums[1:2] = jnp.sum(unit[...] * grad_n2, axis=0, keepdims=True)
        sums[2:3] = jnp.sum(grad_n2, axis=0, keepdims=True)
        sums[3:4] = jnp.sum(cotan[...].astype(F32), axis=0, keepdims=True)


def centre(meta, att, z, cotan, w_out, w_up, gact, up_bias, out_bias, gain, shift, after=(), tile=512):
    tok, width = att.shape
    n = len(w_out)
    rows = w_out[0].shape[0]
    hidden = w_up[0].shape[1]
    steps = hidden // tile
    per = steps // n
    assert n == 1 or per == len(TURNS)
    whole = pl.BlockSpec((tok, width), lambda t, m: (0, 0))
    vector = pl.BlockSpec((1, width), lambda t, m: (0, 0))
    tiled = pl.BlockSpec((tok, tile), lambda t, m: (0, t))

    def gact_spec(i, by_plane=False):
        def index(t, m):
            half = m[0] if i == 0 else 1 - m[0]
            at = jnp.clip(t - half * per, 0, per - 1)
            return (0, turn(at, m[2]) if by_plane else at)

        return tiled if n == 1 else pl.BlockSpec((tok, tile), index)

    low = jax.ShapeDtypeStruct((tok, width), BF16)
    wide = jax.ShapeDtypeStruct((tok, width), F32)
    part = pl.BlockSpec((tok, rows), lambda t, m: (0, 0))
    kernel, waits = ordered(functools.partial(centre_kernel, n), 8 + 3 * n, after)
    return pl.pallas_call(
        kernel,
        grid_spec=pltpu.PrefetchScalarGridSpec(
            num_scalar_prefetch=1,
            grid=(steps,),
            in_specs=[whole, whole, whole]
            + [pl.BlockSpec((rows, width), lambda t, m: (0, 0))] * n
            + [pl.BlockSpec((rows, tile), lambda t, m: (0, t))] * n
            + [gact_spec(i) for i in range(n)]
            + [pl.BlockSpec((1, tile), lambda t, m: (0, t)), vector, vector, vector]
            + waits,
            out_specs=[
                whole,
                tiled,
                whole,
                whole,
                whole,
                pl.BlockSpec((1, tile), lambda t, m: (0, t)),
                pl.BlockSpec((8, width), lambda t, m: (0, 0)),
            ]
            + [gact_spec(i, True) for i in range(n)]
            + [part] * (2 * n),
            scratch_shapes=[
                pltpu.VMEM((tok, width), BF16),
                pltpu.VMEM((tok, width), F32),
                pltpu.VMEM((tok, width), F32),
                pltpu.VMEM((tok, 1), F32),
            ],
        ),
        out_shape=[
            wide,
            jax.ShapeDtypeStruct((tok, hidden), BF16),
            wide,
            low,
            low,
            jax.ShapeDtypeStruct((1, hidden), F32),
            jax.ShapeDtypeStruct((8, width), F32),
        ]
        + [jax.ShapeDtypeStruct((tok, hidden // n), BF16)] * n
        + [jax.ShapeDtypeStruct((tok, rows), BF16)] * (2 * n),
        name="centre",
    )(meta, att, z, cotan, *w_out, *w_up, *gact, up_bias, out_bias, gain, shift, *after)


def unproject_kernel(n, meta, grads, *refs):
    w_refs, out, flat = refs[:n], refs[n], refs[n + 1]
    rows = w_refs[0].shape[0]
    width = grads.shape[2]
    for i in range(3):
        flat[:, i * width : (i + 1) * width] = grads[i]
    for start, w_ref in zip(bases(meta[0], n, rows), w_refs):
        term = times_transposed(grads[1], w_ref[:, width : 2 * width])
        term = term + times_transposed(grads[2], w_ref[:, 2 * width :])

        @pl.when(pl.program_id(0) == 0)
        def _():
            own = term + times_transposed(grads[0], w_ref[:, :width])
            out[0, :, pl.ds(start, rows)] = own.astype(BF16)

        @pl.when(pl.program_id(0) > 0)
        def _():
            out[0, :, pl.ds(start, rows)] = term.astype(BF16)


def unproject(meta, grads, weights, chunks, after=()):
    length, width = grads.shape[1:]
    tok = length // chunks
    rows = weights[0].shape[0]
    n = len(weights)
    kernel, waits = ordered(functools.partial(unproject_kernel, n), 2 + n, after)
    return pl.pallas_call(
        kernel,
        grid_spec=pltpu.PrefetchScalarGridSpec(
            num_scalar_prefetch=1,
            grid=(chunks,),
            in_specs=[pl.BlockSpec((3, tok, width), lambda c, m: (0, c, 0))]
            + [pl.BlockSpec((rows, 3 * width), lambda c, m: (0, 0))] * n
            + waits,
            out_specs=[
                pl.BlockSpec((1, tok, width), lambda c, m: (lax.rem(c + m[1], chunks), 0, 0)),
                pl.BlockSpec((tok, 3 * width), lambda c, m: (c, 0)),
            ],
        ),
        out_shape=[
            jax.ShapeDtypeStruct((chunks, tok, width), BF16),
            jax.ShapeDtypeStruct((length, 3 * width), BF16),
        ],
        name="unproject",
    )(meta, grads, *weights, *after)


def rear_kernel(parts, z_ref, gres, gain, gz_ref, sums):
    grad = parts[0].astype(F32)
    for i in range(1, parts.shape[0]):
        grad = grad + parts[i].astype(F32)
    centred, rstd = statistics(z_ref[...])
    unit = centred * rstd
    low = (gres[...] + norm_back(unit, rstd, gain[...], grad)).astype(BF16)
    gz_ref[...] = low
    sums[0:1] = jnp.sum(low.astype(F32), axis=0, keepdims=True)
    sums[1:2] = jnp.sum(unit * grad, axis=0, keepdims=True)
    sums[2:3] = jnp.sum(grad, axis=0, keepdims=True)


def rear(parts, z, gres, gain, after=()):
    tok, width = z.shape
    count = 4
    kernel, waits = ordered(rear_kernel, count, after)
    vmem = pl.BlockSpec(memory_space=pltpu.VMEM)
    return pl.pallas_call(
        kernel,
        in_specs=[vmem] * count + waits,
        out_specs=[vmem] * 2,
        out_shape=[
            jax.ShapeDtypeStruct((tok, width), BF16),
            jax.ShapeDtypeStruct((8, width), F32),
        ],
        name="rear",
    )(parts, z, gres, gain, *after)


def forward_kernel(resid, bias, own, other, w_own, w_other, out, total):
    step = pl.program_id(0)
    part = times(own[...], w_own[...]) + times(other[...], w_other[...])

    @pl.when(step == 0)
    def _():
        total[...] = resid[...] + bias[...] + part

    @pl.when(step > 0)
    def _():
        total[...] += part

    @pl.when(step == pl.num_programs(0) - 1)
    def _():
        out[...] = total[...].astype(BF16)


def forward(meta, resid, bias, acts, weights, after=()):
    tok, width = resid.shape
    steps = len(TURNS)
    rows = weights[0].shape[0] // steps
    whole = pl.BlockSpec((tok, width), lambda k, m: (0, 0))
    kernel, waits = ordered(
        lambda meta, *refs: forward_kernel(*refs), 7, after
    )
    return pl.pallas_call(
        kernel,
        grid_spec=pltpu.PrefetchScalarGridSpec(
            num_scalar_prefetch=1,
            grid=(steps,),
            in_specs=[whole, pl.BlockSpec((1, width), lambda k, m: (0, 0))]
            + [pl.BlockSpec((tok, rows), lambda k, m: (0, k))] * 2
            + [pl.BlockSpec((rows, width), lambda k, m: (m[2] ^ k ^ (k >> 1), 0))] * 2
            + waits,
            out_specs=whole,
            scratch_shapes=[pltpu.VMEM((tok, width), F32)],
        ),
        out_shape=jax.ShapeDtypeStruct((tok, width), BF16),
        name="forward",
    )(meta, resid, bias, *acts, *weights, *after)


def sort_sums_kernel(meta, late, early, wide, mine, theirs):
    rows = [late[i : i + 1] for i in range(3)] + [early[i : i + 1] for i in range(3)]
    rows = rows + [wide[...], early[3:4]]
    first = meta[0] == 0
    start = 0
    for row in rows:
        half = row.shape[1] // 2
        low, high = row[:, :half], row[:, half:]
        mine[:, start : start + half] = jnp.where(first, low, high)
        theirs[:, start : start + half] = jnp.where(first, high, low)
        start = start + half


def sort_sums(meta, late, early, wide, after=()):
    size = (7 * late.shape[1] + wide.shape[1]) // 2
    vmem = pl.BlockSpec(memory_space=pltpu.VMEM)
    kernel, waits = ordered(sort_sums_kernel, 4, after)
    return pl.pallas_call(
        kernel,
        in_specs=[pl.BlockSpec(memory_space=pltpu.SMEM), vmem, vmem, vmem] + waits,
        out_specs=[vmem] * 2,
        out_shape=[jax.ShapeDtypeStruct((1, size), F32)] * 2,
        name="sort_sums",
    )(meta, late, early, wide, *after)


def input_grads_kernel(n, meta, gz, first, second, input_ref, skip_ref):
    low = times_transposed(gz[...], first[...])
    high = times_transposed(gz[...], second[...])
    if n == 1:
        input_ref[...] = low
        skip_ref[...] = high
        return

    @pl.when(meta[0] == 0)
    def _():
        input_ref[...] = low
        skip_ref[...] = high

    @pl.when(meta[0] != 0)
    def _():
        input_ref[...] = high
        skip_ref[...] = low


def input_grads(meta, gz, weights, after=()):
    tok, width = gz.shape
    n = len(weights)
    steps = 4
    tile = width // steps
    if n == 1:
        weights = [weights[0], weights[0]]
    out = pl.BlockSpec((tok, tile), lambda t, m: (0, t))
    kernel, waits = ordered(functools.partial(input_grads_kernel, n), 4, after)
    return pl.pallas_call(
        kernel,
        grid_spec=pltpu.PrefetchScalarGridSpec(
            num_scalar_prefetch=1,
            grid=(steps,),
            in_specs=[
                pl.BlockSpec((tok, width), lambda t, m: (0, 0)),
                pl.BlockSpec((tile, width), lambda t, m: (t, 0)),
                pl.BlockSpec((tile, width), lambda t, m: (t + (steps if n == 1 else 0), 0)),
            ]
            + waits,
            out_specs=[out, out],
        ),
        out_shape=[jax.ShapeDtypeStruct((tok, width), F32)] * 2,
        name="input_grads",
    )(meta, gz, *weights, *after)


def pack_kernel(*refs):
    out = refs[-1]
    start = 0
    for ref in refs[:-1]:
        size = ref.shape[0]
        out[0, start : start + size] = ref[...]
        start = start + size


def pack(vectors):
    total = sum(v.shape[0] for v in vectors)
    return pl.pallas_call(
        pack_kernel, out_shape=jax.ShapeDtypeStruct((1, total), vectors[0].dtype), name="pack"
    )(*vectors)


def unpack_kernel(sizes, meta, own, other, *outs):
    start = 0
    for size, out in zip(sizes, outs):
        for ref, core in ((own, meta[0]), (other, 1 - meta[0])):
            at = pl.multiple_of(core * size, 128)
            out[:, pl.ds(at, size)] = ref[:, start : start + size].astype(F32)
        start = start + size


def unpack(meta, own, other, sizes, after=()):
    vmem = pl.BlockSpec(memory_space=pltpu.VMEM)
    kernel, waits = ordered(functools.partial(unpack_kernel, sizes), 3, after)
    return pl.pallas_call(
        kernel,
        in_specs=[pl.BlockSpec(memory_space=pltpu.SMEM), vmem, vmem] + waits,
        out_specs=[vmem] * len(sizes),
        out_shape=[jax.ShapeDtypeStruct((1, 2 * n), F32) for n in sizes],
        name="unpack",
    )(meta, own, other, *after)


def fold_kernel(terms, out):
    total = terms[0].astype(F32)
    for i in range(1, terms.shape[0]):
        total = total + terms[i].astype(F32)
    total = total.astype(BF16)
    for i in range(out.shape[0]):
        out[i] = total


def fold(terms, copies, after=()):
    n, rows, width = terms.shape
    tile = width
    while tile % 256 == 0 and tile > 1024:
        tile //= 2
    kernel, waits = ordered(fold_kernel, 1, after)
    return pl.pallas_call(
        kernel,
        grid=(width // tile,),
        in_specs=[pl.BlockSpec((n, rows, tile), lambda c: (0, 0, c))] + waits,
        out_specs=pl.BlockSpec((copies, rows, tile), lambda c: (0, 0, c)),
        out_shape=jax.ShapeDtypeStruct((copies, rows, width), BF16),
        name="fold",
    )(terms, *after)


def place_kernel(meta, own, by_x, by_y, far_low, far_high, out):
    part = pl.program_id(0)
    for i, ref in enumerate((own, by_x, by_y)):

        @pl.when(part == i)
        def _(ref=ref):
            out[...] = ref[...].astype(F32)

    @pl.when(part == 3)
    def _():
        half = far_low.shape[1]
        out[:, :half] = far_low[...].astype(F32)
        out[:, half:] = far_high[...].astype(F32)


def place(meta, parts, start, rows, after=()):
    width = parts[0].shape[1]
    tile = rows
    while start % tile or tile * width > 262144:
        tile //= 2
    base, steps = start // tile, rows // tile

    def spec(i, columns):
        def index(q, c, m):
            return (base + jnp.where(q == i, c, jnp.where(q < i, 0, steps - 1)), 0)

        return pl.BlockSpec((tile, columns), index)

    kernel, waits = ordered(place_kernel, 6, after)
    return pl.pallas_call(
        kernel,
        grid_spec=pltpu.PrefetchScalarGridSpec(
            num_scalar_prefetch=1,
            grid=(4, steps),
            in_specs=[spec(i, width) for i in range(3)] + [spec(3, width // 2)] * 2 + waits,
            out_specs=pl.BlockSpec((tile, width), lambda q, c, m: ((m[0] ^ q) * steps + c, 0)),
        ),
        out_shape=jax.ShapeDtypeStruct((4 * rows, width), F32),
        name="place",
    )(meta, *parts, *after)


class Links:
    def __init__(self):
        self.sent = {"x": [], "y": [], "z": [], "frames": []}

    def send(self, link, array, move, *pins):
        waits = [p for p in pins if p is not None]
        earlier = self.sent[link]
        depth = 2 if link in ("x", "y") else 1
        if len(earlier) >= depth:
            waits.append(earlier[-depth])
        if waits:
            array = tie(array, *waits)
        moved = move(array)
        earlier.append(moved)
        return moved


def tie(array, *others):
    return lax.optimization_barrier((array, *others))[0]


def body(
    frames_in,
    skip_in,
    lengths,
    cotangent,
    w_skip,
    w_qkv,
    w_out,
    w_up,
    w_down,
    skip_bias,
    norm1_gain,
    norm1_bias,
    out_bias,
    norm2_gain,
    norm2_bias,
    up_bias,
    down_bias,
):
    tok = frames_in.shape[3]
    width = frames_in.shape[4]
    frames = frames_in.reshape(tok, width)
    skips = skip_in.reshape(tok, width)
    cotan = cotangent.reshape(tok, width)
    n_batch = lax.axis_size("batch")
    n_seq = lax.axis_size("seq")
    n_frames = lax.axis_size("frames")
    assert n_batch == 4 and n_seq % 2 == 0
    paired = n_frames == 2
    plane = lax.axis_index("batch").astype(jnp.int32)
    shard = lax.axis_index("seq").astype(jnp.int32)
    core = lax.axis_index("frames").astype(jnp.int32)
    links = Links()

    def swap_frames(array):
        return lax.ppermute(array, "frames", [(0, 1), (1, 0)])

    def over_x(array):
        return lax.ppermute(array, "batch", [(i, i ^ 1) for i in range(n_batch)])

    def over_y(array):
        return lax.ppermute(array, "batch", [(i, i ^ 2) for i in range(n_batch)])

    def from_seq(step):
        return lambda array: lax.ppermute(
            array, "seq", [((i + step) % n_seq, i) for i in range(n_seq)]
        )

    def to_seq(step):
        return from_seq(n_seq - step)

    def exchange_seq(array):
        return lax.all_to_all(array, "seq", split_axis=0, concat_axis=0, tiled=True)

    def send_rows(array, *pins):
        if paired:
            return swap_frames(tie(array, *pins) if pins else array)
        return lax.all_gather(array, "frames", axis=0, tiled=True)

    def gather_frames(array, *pins):
        moved = send_rows(array, *pins)
        return [array, moved] if paired else [moved]

    def send_left(parts, *pins):
        if paired:
            return [parts[0], swap_frames(tie(parts[1], *pins) if pins else parts[1])]
        array = parts[0]
        split = array.reshape(array.shape[0], n_frames, array.shape[1] // n_frames)
        moved = lax.all_to_all(split, "frames", split_axis=1, concat_axis=0, tiled=True)
        return [moved.reshape(array.shape[0] * n_frames, array.shape[1] // n_frames)]

    def by_plane(source):
        block = source.shape[1] // n_batch
        return jnp.concatenate(
            [
                lax.dynamic_slice_in_dim(source, (plane ^ bits) * block, block, 1)
                for bits in TURNS
            ],
            axis=1,
        )

    def turned(sources):
        return stack(sources if paired else [by_plane(source) for source in sources])

    def stack(arrays):
        return arrays[0] if len(arrays) == 1 else jnp.concatenate(arrays, axis=0)

    class Chain:
        def __init__(self, terms):
            self.terms = terms
            self.half = terms[0][1][0].shape[1] // 2
            self.blocks = [lefts[0].shape[1] // n_batch for lefts, _ in terms]
            self.block = sum(self.blocks)

        def gemm(self, plane_blocks, low, high):
            whole = len(self.terms) == 1
            first, last = plane_blocks[0], plane_blocks[-1] + 1
            spans = [(first, last)] if whole else [(p, p + 1) for p in plane_blocks]
            outs = []
            for p, q in spans:
                for (lefts, rights), block in zip(self.terms, self.blocks):
                    total = None
                    for left, right in zip(lefts, rights):
                        term = contract_rows(
                            left[:, p * block : q * block], right[:, low:high]
                        )
                        total = term if total is None else total + term
                    outs.append(total)
            return stack(outs)

        def begin(self, *pins):
            half = self.half
            if pins:
                lefts, rights = self.terms[0]
                self.terms[0] = ([tie(lefts[0], *pins), *lefts[1:]], rights)
            self.to_x = self.gemm((1, 2), 0, half).astype(BF16)
            self.to_y = self.gemm((2, 3), half, 2 * half).astype(BF16)
            return self.to_x, self.to_y

        def first(self, *pins):
            self.from_x = links.send("x", self.to_x, over_x, *pins)
            self.from_y = links.send("y", self.to_y, over_y, *pins)

        def between(self, *pins):
            half, block = self.half, self.block
            from_x, from_y = self.from_x, self.from_y
            if pins:
                from_x, from_y = tie(from_x, *pins), tie(from_y, *pins)
            low = self.gemm((3,), 0, half) + from_x[block:].astype(F32)
            high = self.gemm((1,), half, 2 * half) + from_y[:block].astype(F32)
            self.next_y, self.next_x = low.astype(BF16), high.astype(BF16)
            return self.next_x, self.next_y

        def second(self, *pins):
            self.then_y = links.send("y", self.next_y, over_y, *pins)
            self.then_x = links.send("x", self.next_x, over_x, *pins)

        def own_sum(self, *pins):
            block, half = self.block, self.half
            then_x, then_y = self.then_x, self.then_y
            if pins:
                then_x, then_y = tie(then_x, *pins), tie(then_y, *pins)
            low = self.from_x[:block].astype(F32) + then_y.astype(F32)
            high = self.from_y[block:].astype(F32) + then_x.astype(F32)
            own = self.gemm((0,), 0, 2 * half) + jnp.concatenate([low, high], axis=1)
            self.own = own.astype(BF16).reshape(n_seq, block // n_seq, 2 * half)
            return self.own

        def across(self, *pins):
            self.terms_seq = links.send("z", self.own, exchange_seq, *pins)

        def along(self, after=(), *pins):
            self.folded = fold(self.terms_seq, n_seq, after)
            whole = links.send("z", self.folded, exchange_seq, *pins)
            self.whole = whole.reshape(self.block, 2 * self.half)
            return self.folded

        def spread(self, *pins):
            self.by_x = links.send("x", self.whole, over_x, *pins)
            self.by_y = links.send("y", self.whole, over_y, *pins)

        def finish(self, *pins):
            half = self.half
            self.far_low = links.send("x", self.by_y[:, :half], over_x, *pins)
            self.far_high = links.send("y", self.by_x[:, half:], over_y, *pins)

        def place(self, after=()):
            parts = (self.whole, self.by_x, self.by_y, self.far_low, self.far_high)
            starts = [sum(self.blocks[:i]) for i in range(len(self.blocks))]
            return [
                place(plane.reshape(1), parts, start, rows, after)
                for start, rows in zip(starts, self.blocks)
            ]

    vectors_in = (
        skip_bias,
        norm1_gain,
        norm1_bias,
        out_bias,
        norm2_gain,
        norm2_bias,
        up_bias,
        down_bias,
    )
    sizes = [v.shape[0] for v in vectors_in]
    starts = [sum(sizes[:i]) for i in range(len(sizes))]
    packed = pack(vectors_in)
    meta = jnp.concatenate([jnp.stack([core, shard, plane]), lengths.reshape(-1)])
    full_skip = gather_frames(w_skip, packed)

    if paired:
        packs = [packed, swap_frames(packed)]
        full_qkv = gather_frames(w_qkv, full_skip[1], packs[1])
        full_down = gather_frames(w_down, full_skip[1], packs[1])
        hidden_z, n1, own_in, other_in = front(
            meta, frames, skips, full_skip, packs, tuple(sizes)
        )
        vectors = unpack(meta, *packs, sizes, after=(n1,))
        inputs = [own_in, other_in]
    else:
        packed = lax.all_gather(packed, "frames", axis=0, tiled=True).astype(F32)
        vectors = [packed[:, b : b + n].reshape(1, -1) for b, n in zip(starts, sizes)]
        hidden_z, n1 = front_whole(frames, skips, full_skip[0], *vectors[:3])
        inputs = [jnp.concatenate([frames, skips], axis=1)]
        full_qkv, full_down = gather_frames(w_qkv), gather_frames(w_down)
    obias, gain2, bias2, ubias, dbias = vectors[3:]
    gain1 = vectors[1]
    n1_all = [n1] + [from_seq(j)(n1) for j in range(1, n_seq)]
    full_up = gather_frames(w_up, full_down[-1], n1)
    gact = [times_transposed(tie(cotan, n1), full_down[0])]
    if paired:
        gact.append(times_transposed(tie(cotan, gact[0]), full_down[1]))
    queries, key_rows, value_rows, *n1_parts = project(
        meta, n1_all, full_qkv, after=(*gact, gain1)
    )
    full_out = gather_frames(w_out, queries)
    both_cotan = [cotan, swap_frames(tie(cotan, queries))] if paired else None
    if not paired:
        both_cotan = [lax.all_gather(cotan, "frames", axis=0, tiled=True)]
    left_n1 = send_left(n1_parts)
    attended, prob = attend_forward(meta, queries, key_rows, value_rows)
    both_cotan = stack(both_cotan)
    left_n1 = left_n1 if paired else [by_plane(a) for a in left_n1]
    (
        resid,
        gup,
        grad_resid,
        grad_branch,
        grad_heads,
        up_sum,
        sums2,
        *parts,
    ) = centre(
        meta,
        attended,
        hidden_z,
        cotan,
        full_out,
        full_up,
        gact,
        ubias,
        obias,
        gain2,
        bias2,
        after=(both_cotan, *left_n1),
    )
    n = len(full_out)
    acts, n2_parts, att_parts = parts[:n], parts[n : 2 * n], parts[2 * n :]

    def right_rows(array, *pins):
        moved = send_rows(array, *pins)
        return stack([array, moved] if paired else [moved])

    down = Chain([([turned(send_left(acts))], [both_cotan])])
    down_first = down.begin()
    down.first()
    both_up = right_rows(gup)
    left_n2 = turned(send_left(n2_parts))
    grads = attend_backward(queries, key_rows, value_rows, grad_heads, prob, after=down_first)
    up = Chain([([left_n2], [both_up])])
    terms_n1, flat = unproject(meta, grads, full_qkv, n_seq, after=down_first)
    down_second = down.between(flat)
    down.second()
    up_first = up.begin(*down_second)
    up.first()
    terms_n1 = links.send("z", terms_n1, exchange_seq)
    both_flat = gather_frames(flat, *up_first)
    qkv = Chain([(left_n1, both_flat)])
    down_own = down.own_sum(*up_first)
    grad_z, sums1 = rear(
        terms_n1, hidden_z, grad_resid, gain1, after=(down_own, both_flat[-1])
    )
    up.between(grad_z)
    up.second()
    down.across()
    left_joined = turned(send_left(inputs, grad_z))
    left_att = turned(send_left(att_parts, grad_z))
    both_branch = right_rows(grad_branch, left_joined)
    rest = Chain([([left_joined], [right_rows(grad_z, left_att)]), ([left_att], [both_branch])])
    qkv_first = qkv.begin(up.next_x, up.next_y)
    qkv.first()
    up_own = up.own_sum(*qkv_first)
    up.across()
    rest_first = rest.begin(up_own)
    rest.first()
    qkv_second = qkv.between(*rest_first)
    qkv.second()
    down_fold = down.along(qkv_second, rest.from_x, rest.from_y)
    rest_second = rest.between(down_fold)
    rest.second()
    up_fold = up.along(rest_second, qkv.then_x, qkv.then_y)
    qkv_own = qkv.own_sum(up_fold)
    down.spread()
    if paired:
        output = forward(meta, resid, dbias, acts, full_down, after=(qkv_own,))
        mine, theirs = sort_sums(meta, sums1, sums2, up_sum, after=rest_first)
        mine = mine + swap_frames(theirs)
    else:
        output = (resid + times(acts[0], full_down[0]) + dbias).astype(BF16)
        summed = (
            *(sums1[i] for i in range(3)),
            *(sums2[i] for i in range(3)),
            up_sum[0],
            sums2[3],
        )
        summed = jnp.concatenate([v.reshape(n_frames, -1) for v in summed], axis=1)
        mine = lax.psum_scatter(summed, "frames", scatter_dimension=0, tiled=True)
    rest_own = rest.own_sum(output)
    qkv.across(rest.then_x, rest.then_y)
    up.spread()
    input_grad, skip_grad = input_grads(meta, grad_z, full_skip, after=(rest_own,))
    down.finish()
    qkv.along((input_grad,), down.by_x, down.by_y, up.by_x, up.by_y)
    rest.across(down.far_low, down.far_high)
    qkv.spread()
    (grad_w_down,) = down.place()
    up.finish()
    rest.along((mine, grad_w_down), qkv.by_x, qkv.by_y)
    copies = jnp.broadcast_to(mine[None], (n_batch * n_seq,) + mine.shape)

    def exchange_all(array):
        return lax.all_to_all(array, ("batch", "seq"), split_axis=0, concat_axis=0, tiled=True)

    qkv.finish()
    (grad_w_up,) = up.place()
    total = exchange_all(tie(copies, qkv.far_low, qkv.far_high))
    rest.spread(grad_w_up)
    (grad_w_qkv,) = qkv.place(after=(grad_w_up,))
    rest.finish(grad_w_qkv)
    total = jnp.sum(total, axis=0).reshape(-1)
    vector_grads = [total[b : b + n] for b, n in zip(starts, sizes)]
    grad_w_skip, grad_w_out = rest.place(after=(grad_w_qkv,))

    def back(array):
        return array.reshape(1, 1, 1, tok, width)

    return (
        back(output),
        back(input_grad),
        back(skip_grad),
        grad_w_skip,
        grad_w_qkv,
        grad_w_out,
        grad_w_up,
        grad_w_down,
        *vector_grads,
    )


def solution(mesh):
    rows = P("batch", "seq", "frames", None, None)
    in_specs = (
        (rows, rows, P("batch", "frames", None), rows)
        + (P("frames", None),) * 5
        + (P("frames"),) * 8
    )
    out_specs = (rows,) * 3 + (P("frames", None),) * 5 + (P("frames"),) * 8
    return jax.shard_map(body, mesh=mesh, in_specs=in_specs, out_specs=out_specs, check_vma=False)
```

```python
import functools

import jax
import jax.numpy as jnp
from jax import lax
from jax.experimental import pallas as pl
from jax.experimental.pallas import tpu as pltpu
from jax.sharding import PartitionSpec as P

HEADS = 16
HD = 64
UTTS = 3
EPS = 1e-05
MASKED = 1e12
BF16 = jnp.bfloat16
F32 = jnp.float32
INV_SQRT2 = 0.7071067811865476
INV_SQRT_2PI = 0.3989422804014327
ERFC_STEP = 0.4
ERFC_TERMS = (
    0.22567586186829244 / 2,
    0.22566960544571626 / 2,
    0.20784251123900896 / 2,
    0.16854379658168633 / 2,
    0.14142295790506823 / 2,
    -0.005586494604590357 / 2,
    0.16905696704198306 / 2,
    -0.18288169574958996 / 2,
    0.05025661354969599 / 2,
)


def contract_rows(left_side, right_side):
    return lax.dot_general(
        left_side, right_side, (((0,), (0,)), ((), ())), preferred_element_type=F32
    )


def times_transposed(left_side, right_side):
    return lax.dot_general(
        left_side, right_side, (((1,), (1,)), ((), ())), preferred_element_type=F32
    )


def times(left_side, right_side):
    return jnp.dot(left_side, right_side, preferred_element_type=F32)


def ordered(kernel, count, after):
    n = len(after)

    def run(*refs):
        kernel(*refs[:count], *refs[count + n :])

    return run, [pl.BlockSpec(memory_space=pl.ANY)] * n


TURNS = (0, 1, 3, 2)


def turn(block, plane):
    bits = block ^ plane
    return bits ^ (bits >> 1)


def put_turned(part, read, plane):
    block = part.shape[-1] // len(TURNS)
    for i, bits in enumerate(TURNS):
        at = pl.multiple_of((plane ^ bits) * block, 128)
        part[:, i * block : (i + 1) * block] = read(at, block)


def pair_rows(block, lane):
    zero = jnp.zeros_like(block)
    return jnp.concatenate(
        [jnp.where(lane < HD, block, zero), jnp.where(lane >= HD, block, zero)], axis=0
    )


def utterance_ends(meta):
    ends = [meta[3]]
    for j in range(1, UTTS):
        ends.append(ends[-1] + meta[3 + j])
    return ends


def attend_forward_kernel(meta, q_ref, k_ref, v_ref, out_ref, prob_ref, dist):
    tok = q_ref.shape[0]
    length = k_ref.shape[0]
    shard = meta[1]
    ends = utterance_ends(meta)

    @pl.when(pl.program_id(0) == 0)
    def _():
        row = lax.broadcasted_iota(jnp.int32, (length, 2 * tok), 0)
        col = lax.broadcasted_iota(jnp.int32, (length, 2 * tok), 1)
        k_pos = row + shard * tok
        k_pos = jnp.where(k_pos >= length, k_pos - length, k_pos)
        q_pos = jnp.where(col >= tok, col - tok, col) + shard * tok
        k_seg = jnp.zeros_like(k_pos)
        q_seg = jnp.zeros_like(q_pos)
        for j in range(UTTS):
            k_seg = k_seg + (k_pos >= ends[j]).astype(jnp.int32)
            q_seg = q_seg + (q_pos >= ends[j]).astype(jnp.int32)
        allowed = (k_seg == q_seg) & (k_seg < UTTS)
        dist[...] = jnp.where(allowed, jnp.abs(k_pos - q_pos).astype(F32), MASKED)

    lane = lax.broadcasted_iota(jnp.int32, (tok, 2 * HD), 1)
    pair = pair_rows(q_ref[...] * jnp.asarray(HD**-0.5, BF16), lane)
    head = 2 * pl.program_id(0) + 1 + (lax.broadcasted_iota(jnp.int32, (1, 2 * tok), 1) >= tok)
    slope = jnp.exp2(head.astype(F32) * (-8.0 / HEADS))
    scores = times_transposed(k_ref[...], pair) - slope * dist[...]
    top = jnp.max(scores, axis=0, keepdims=True)
    exp_scores = jnp.exp(scores - top)
    total = jnp.sum(exp_scores, axis=0, keepdims=True)
    prob = (exp_scores * (1.0 / total)).astype(BF16)
    prob_ref[0] = prob
    mixed = times(v_ref[...].T, prob).T
    mixed = jnp.where(lane < HD, mixed[:tok], mixed[tok:])
    row = lax.broadcasted_iota(jnp.int32, (tok, 2 * HD), 0) + shard * tok
    out_ref[...] = jnp.where(row < ends[UTTS - 1], mixed, 0.0).astype(BF16)


def attend_backward_kernel(q_ref, k_ref, v_ref, grad_ref, prob_ref, out_ref):
    tok = q_ref.shape[0]
    lane = lax.broadcasted_iota(jnp.int32, (tok, 2 * HD), 1)
    scale = jnp.asarray(HD**-0.5, BF16)
    pair_q = pair_rows(q_ref[...] * scale, lane)
    pair_g = pair_rows(grad_ref[...], lane)
    prob_low = prob_ref[0]
    prob = prob_low.astype(F32)
    prob_grad = times_transposed(v_ref[...], pair_g)
    weighted = prob * prob_grad
    delta = jnp.sum(weighted, axis=0, keepdims=True)
    score_low = (weighted - prob * delta).astype(BF16)
    out_ref[2] = times(prob_low, pair_g).astype(BF16)
    out_ref[1] = times(score_low, pair_q).astype(BF16)
    mixed = times((k_ref[...] * scale).T, score_low).T
    out_ref[0, :tok] = jnp.where(lane < HD, mixed[:tok], mixed[tok:]).astype(BF16)
    out_ref[0, tok:] = jnp.zeros_like(out_ref[0, tok:])


def attend_forward(meta, queries, key_rows, value_rows, after=()):
    tok, width = queries.shape
    length = key_rows.shape[0]
    pairs = width // (2 * HD)
    kernel, waits = ordered(attend_forward_kernel, 4, after)
    return pl.pallas_call(
        kernel,
        grid_spec=pltpu.PrefetchScalarGridSpec(
            num_scalar_prefetch=1,
            grid=(pairs,),
            in_specs=[
                pl.BlockSpec((tok, 2 * HD), lambda g, m: (0, g)),
                pl.BlockSpec((length, 2 * HD), lambda g, m: (0, g)),
                pl.BlockSpec((length, 2 * HD), lambda g, m: (0, g)),
            ]
            + waits,
            out_specs=[
                pl.BlockSpec((tok, 2 * HD), lambda g, m: (0, g)),
                pl.BlockSpec((1, length, 2 * tok), lambda g, m: (g, 0, 0)),
            ],
            scratch_shapes=[pltpu.VMEM((length, 2 * tok), F32)],
        ),
        out_shape=[
            jax.ShapeDtypeStruct((tok, width), BF16),
            jax.ShapeDtypeStruct((pairs, length, 2 * tok), BF16),
        ],
        name="attend_forward",
    )(meta, queries, key_rows, value_rows, *after)


def attend_backward(queries, key_rows, value_rows, grad_heads, prob, after=()):
    tok, width = queries.shape
    length = key_rows.shape[0]
    pairs = width // (2 * HD)
    q_spec = pl.BlockSpec((tok, 2 * HD), lambda g: (0, g))
    k_spec = pl.BlockSpec((length, 2 * HD), lambda g: (0, g))
    kernel, waits = ordered(attend_backward_kernel, 5, after)
    return pl.pallas_call(
        kernel,
        grid=(pairs,),
        in_specs=[
            q_spec,
            k_spec,
            k_spec,
            q_spec,
            pl.BlockSpec((1, length, 2 * tok), lambda g: (g, 0, 0)),
        ]
        + waits,
        out_specs=pl.BlockSpec((3, length, 2 * HD), lambda g: (0, 0, g)),
        out_shape=jax.ShapeDtypeStruct((3, length, width), BF16),
        name="attend_backward",
    )(queries, key_rows, value_rows, grad_heads, prob, *after)


def statistics(values):
    mean = jnp.mean(values, axis=-1, keepdims=True)
    centred = values - mean
    variance = jnp.mean(centred * centred, axis=-1, keepdims=True)
    return centred, lax.rsqrt(variance + EPS)


def norm_back(unit, rstd, gain, grad):
    scaled = grad * gain
    mean_e = jnp.mean(scaled, axis=-1, keepdims=True)
    mean_eu = jnp.mean(scaled * unit, axis=-1, keepdims=True)
    return rstd * (scaled - mean_e - unit * mean_eu)


def bases(core, n_pieces, rows):
    if n_pieces == 1:
        return [0]
    return [pl.multiple_of(core * rows, 128), pl.multiple_of((1 - core) * rows, 128)]


def front_kernel(n, sizes, meta, *refs):
    x_refs, refs = refs[:2], refs[2:]
    w_refs, packs, outs = refs[:n], refs[n : 2 * n], refs[2 * n :]
    z_ref, n1_ref, own_ref, other_ref = outs
    step = pl.program_id(0)
    first = meta[0] == 0

    def vector(i):
        start = sum(sizes[:i])
        parts = [ref[:, start : start + sizes[i]].astype(F32) for ref in packs]
        low = jnp.where(first, parts[0], parts[1])
        high = jnp.where(first, parts[1], parts[0])
        return jnp.concatenate([low, high], axis=1)

    x, s = x_refs[0][...], x_refs[1][...]
    own = jnp.where(first, x, s)
    other = jnp.where(first, s, x)
    own_ref[...] = own
    other_ref[...] = other
    part = times(own, w_refs[0][...]) + times(other, w_refs[1][...])

    @pl.when(step == 0)
    def _():
        z_ref[...] = part + vector(0)

    @pl.when(step > 0)
    def _():
        z_ref[...] += part

    @pl.when(step == pl.num_programs(0) - 1)
    def _():
        centred, rstd = statistics(z_ref[...])
        n1_ref[...] = (centred * rstd * vector(1) + vector(2)).astype(BF16)


def front(meta, frames, skips, weights, packs, sizes, after=()):
    tok = frames.shape[0]
    rows, width = weights[0].shape
    n = len(weights)
    steps = 4
    block = rows // steps
    packed = pl.BlockSpec(packs[0].shape, lambda k, m: (0, 0))
    whole = pl.BlockSpec((tok, width), lambda k, m: (0, 0))
    columns = pl.BlockSpec((tok, block), lambda k, m: (0, k))
    turned = pl.BlockSpec((tok, block), lambda k, m: (0, turn(k, m[2])))
    kernel, waits = ordered(functools.partial(front_kernel, n, sizes), 3 + 2 * n, after)
    return pl.pallas_call(
        kernel,
        grid_spec=pltpu.PrefetchScalarGridSpec(
            num_scalar_prefetch=1,
            grid=(steps,),
            in_specs=[columns] * 2
            + [pl.BlockSpec((block, width), lambda k, m: (k, 0))] * n
            + [packed] * n
            + waits,
            out_specs=[whole, whole, turned, turned],
        ),
        out_shape=[
            jax.ShapeDtypeStruct((tok, width), F32),
            jax.ShapeDtypeStruct((tok, width), BF16),
            jax.ShapeDtypeStruct((tok, rows), BF16),
            jax.ShapeDtypeStruct((tok, rows), BF16),
        ],
        name="front",
    )(meta, frames, skips, *weights, *packs, *after)


def front_whole_kernel(x_ref, s_ref, first_ref, second_ref, bias, gain, shift, z_ref, n1_ref):
    step = pl.program_id(0)
    part = times(x_ref[...], first_ref[...]) + times(s_ref[...], second_ref[...])

    @pl.when(step == 0)
    def _():
        z_ref[...] = part + bias[...]

    @pl.when(step > 0)
    def _():
        z_ref[...] += part

    @pl.when(step == pl.num_programs(0) - 1)
    def _():
        centred, rstd = statistics(z_ref[...])
        n1_ref[...] = (centred * rstd * gain[...] + shift[...]).astype(BF16)


def front_whole(frames, skips, weight, bias, gain, shift):
    tok, width = frames.shape
    steps = 4
    block = width // steps
    vector = pl.BlockSpec((1, width), lambda k: (0, 0))
    whole = pl.BlockSpec((tok, width), lambda k: (0, 0))
    return pl.pallas_call(
        front_whole_kernel,
        grid=(steps,),
        in_specs=[pl.BlockSpec((tok, block), lambda k: (0, k))] * 2
        + [
            pl.BlockSpec((block, width), lambda k: (k, 0)),
            pl.BlockSpec((block, width), lambda k: (k + steps, 0)),
        ]
        + [vector] * 3,
        out_specs=[whole, whole],
        out_shape=[
            jax.ShapeDtypeStruct((tok, width), F32),
            jax.ShapeDtypeStruct((tok, width), BF16),
        ],
        name="front",
    )(frames, skips, weight, weight, bias, gain, shift)


def project_kernel(n, chunks, meta, *refs):
    x_refs = refs[:chunks]
    w_refs = refs[chunks : chunks + 3 * n]
    q_ref, k_ref, v_ref = refs[chunks + 3 * n : chunks + 3 * n + 3]
    parts = refs[chunks + 3 * n + 3 :]
    rows = w_refs[0].shape[0]
    tok = q_ref.shape[0]
    starts = bases(meta[0], n, rows)

    @pl.when(pl.program_id(0) == 0)
    def _():
        for start, part in zip(starts, parts):
            for c in range(chunks):
                if n == 1:
                    part[c * tok : (c + 1) * tok] = x_refs[c][...]
                    continue
                put_turned(
                    part.at[c * tok : (c + 1) * tok],
                    lambda at, block: x_refs[c][:, pl.ds(pl.multiple_of(start + at, 128), block)],
                    meta[2],
                )

    for c in range(chunks):
        for i, out in enumerate((q_ref, k_ref, v_ref)):
            if i == 0 and c > 0:
                continue
            total = None
            for p, start in enumerate(starts):
                term = times(x_refs[c][:, pl.ds(start, rows)], w_refs[3 * p + i][...])
                total = term if total is None else total + term
            out[c * tok : (c + 1) * tok] = total.astype(BF16)


def project(meta, chunks, weights, after=()):
    tok, width = chunks[0].shape
    rows = weights[0].shape[0]
    n = len(weights)
    tile = 256
    tiles = width // tile

    def w_spec(i):
        return pl.BlockSpec((rows, tile), lambda t, m: (0, t + i * tiles))

    length = tok * len(chunks)
    kernel, waits = ordered(
        functools.partial(project_kernel, n, len(chunks)), 1 + len(chunks) + 3 * n, after
    )
    return pl.pallas_call(
        kernel,
        grid_spec=pltpu.PrefetchScalarGridSpec(
            num_scalar_prefetch=1,
            grid=(tiles,),
            in_specs=[pl.BlockSpec((tok, width), lambda t, m: (0, 0))] * len(chunks)
            + [w_spec(i) for i in range(3)] * n
            + waits,
            out_specs=[
                pl.BlockSpec((tok, tile), lambda t, m: (0, t)),
                pl.BlockSpec((length, tile), lambda t, m: (0, t)),
                pl.BlockSpec((length, tile), lambda t, m: (0, t)),
            ]
            + [pl.BlockSpec((length, rows), lambda t, m: (0, 0))] * n,
        ),
        out_shape=[
            jax.ShapeDtypeStruct((tok, width), BF16),
            jax.ShapeDtypeStruct((length, width), BF16),
            jax.ShapeDtypeStruct((length, width), BF16),
        ]
        + [jax.ShapeDtypeStruct((length, rows), BF16)] * n,
        name="project",
    )(meta, *chunks, *[w for w in weights for _ in range(3)], *after)


def centre_kernel(n, meta, *refs):
    refs = list(refs)

    def take(count):
        taken = refs[:count]
        del refs[:count]
        return taken

    att, z_ref, cotan = take(3)
    w_out, w_up, gact = take(n), take(n), take(n)
    up_bias, out_bias, gain, shift = take(4)
    resid, gup_ref, gres, gbranch, gatt, up_sum, sums = take(7)
    acts, n2_parts, att_parts = take(n), take(n), take(n)
    n2, gn2, unit, rstd = refs
    step, steps = pl.program_id(0), pl.num_programs(0)
    tok = att.shape[0]
    core, live = meta[0], utterance_ends(meta)[-1] - meta[1] * tok
    rows = w_out[0].shape[0]
    starts = bases(core, n, rows)

    @pl.when(step == 0)
    def _():
        total = z_ref[...] + out_bias[...]
        for start, w_ref, part in zip(starts, w_out, att_parts):
            total = total + times(att[:, pl.ds(start, rows)], w_ref[...])
        resid[...] = total
        centred, scale = statistics(total)
        unit[...] = centred * scale
        rstd[...] = scale
        n2[...] = (unit[...] * gain[...] + shift[...]).astype(BF16)
        for start, n2_part, att_part in zip(starts, n2_parts, att_parts):
            for part, source in ((n2_part, n2), (att_part, att)):
                if n == 1:
                    part[...] = source[...]
                    continue
                put_turned(
                    part,
                    lambda at, block: source[:, pl.ds(pl.multiple_of(start + at, 128), block)],
                    meta[2],
                )
        gn2[...] = jnp.zeros_like(gn2)

    pre = up_bias[...]
    for start, w_ref in zip(starts, w_up):
        pre = pre + times(n2[:, pl.ds(start, rows)], w_ref[...])
    gauss = jnp.exp(pre * pre * (-0.5))
    t = 1.0 / (1.0 + (ERFC_STEP * INV_SQRT2) * jnp.abs(pre))
    tail = jnp.full_like(t, ERFC_TERMS[-1])
    for term in ERFC_TERMS[-2::-1]:
        tail = tail * t + term
    tail = tail * t * gauss
    cdf = jnp.where(pre < 0.0, tail, 1.0 - tail)
    act = (pre * cdf).astype(BF16)
    if n == 1:
        acts[0][...] = act
        grad = gact[0][...]
    else:
        mine = (step // (steps // 2)) == core

        @pl.when(mine)
        def _():
            acts[0][...] = act

        @pl.when(jnp.logical_not(mine))
        def _():
            acts[1][...] = act

        grad = jnp.where(mine, gact[0][...], gact[1][...])
    gup = (grad * (cdf + pre * gauss * INV_SQRT_2PI)).astype(BF16)
    gup_ref[...] = gup
    up_sum[...] = jnp.sum(gup.astype(F32), axis=0, keepdims=True)
    for start, w_ref in zip(starts, w_up):
        gn2[:, pl.ds(start, rows)] += times_transposed(gup, w_ref[...])

    @pl.when(step == steps - 1)
    def _():
        grad_n2 = gn2[...]
        total = cotan[...].astype(F32) + norm_back(unit[...], rstd[...], gain[...], grad_n2)
        gres[...] = total
        low = total.astype(BF16)
        gbranch[...] = low
        alive = lax.broadcasted_iota(jnp.int32, (tok, 1), 0) < live
        for start, w_ref in zip(starts, w_out):
            term = times_transposed(low, w_ref[...])
            gatt[:, pl.ds(start, rows)] = jnp.where(alive, term, 0.0).astype(BF16)
        sums[0:1] = jnp.sum(low.astype(F32), axis=0, keepdims=True)
        sums[1:2] = jnp.sum(unit[...] * grad_n2, axis=0, keepdims=True)
        sums[2:3] = jnp.sum(grad_n2, axis=0, keepdims=True)
        sums[3:4] = jnp.sum(cotan[...].astype(F32), axis=0, keepdims=True)


def centre(meta, att, z, cotan, w_out, w_up, gact, up_bias, out_bias, gain, shift, after=(), tile=512):
    tok, width = att.shape
    n = len(w_out)
    rows = w_out[0].shape[0]
    hidden = w_up[0].shape[1]
    steps = hidden // tile
    per = steps // n
    assert n == 1 or per == len(TURNS)
    whole = pl.BlockSpec((tok, width), lambda t, m: (0, 0))
    vector = pl.BlockSpec((1, width), lambda t, m: (0, 0))
    tiled = pl.BlockSpec((tok, tile), lambda t, m: (0, t))

    def gact_spec(i, by_plane=False):
        def index(t, m):
            half = m[0] if i == 0 else 1 - m[0]
            at = jnp.clip(t - half * per, 0, per - 1)
            return (0, turn(at, m[2]) if by_plane else at)

        return tiled if n == 1 else pl.BlockSpec((tok, tile), index)

    low = jax.ShapeDtypeStruct((tok, width), BF16)
    wide = jax.ShapeDtypeStruct((tok, width), F32)
    part = pl.BlockSpec((tok, rows), lambda t, m: (0, 0))
    kernel, waits = ordered(functools.partial(centre_kernel, n), 8 + 3 * n, after)
    return pl.pallas_call(
        kernel,
        grid_spec=pltpu.PrefetchScalarGridSpec(
            num_scalar_prefetch=1,
            grid=(steps,),
            in_specs=[whole, whole, whole]
            + [pl.BlockSpec((rows, width), lambda t, m: (0, 0))] * n
            + [pl.BlockSpec((rows, tile), lambda t, m: (0, t))] * n
            + [gact_spec(i) for i in range(n)]
            + [pl.BlockSpec((1, tile), lambda t, m: (0, t)), vector, vector, vector]
            + waits,
            out_specs=[
                whole,
                tiled,
                whole,
                whole,
                whole,
                pl.BlockSpec((1, tile), lambda t, m: (0, t)),
                pl.BlockSpec((8, width), lambda t, m: (0, 0)),
            ]
            + [gact_spec(i, True) for i in range(n)]
            + [part] * (2 * n),
            scratch_shapes=[
                pltpu.VMEM((tok, width), BF16),
                pltpu.VMEM((tok, width), F32),
                pltpu.VMEM((tok, width), F32),
                pltpu.VMEM((tok, 1), F32),
            ],
        ),
        out_shape=[
            wide,
            jax.ShapeDtypeStruct((tok, hidden), BF16),
            wide,
            low,
            low,
            jax.ShapeDtypeStruct((1, hidden), F32),
            jax.ShapeDtypeStruct((8, width), F32),
        ]
        + [jax.ShapeDtypeStruct((tok, hidden // n), BF16)] * n
        + [jax.ShapeDtypeStruct((tok, rows), BF16)] * (2 * n),
        name="centre",
    )(meta, att, z, cotan, *w_out, *w_up, *gact, up_bias, out_bias, gain, shift, *after)


def unproject_kernel(n, meta, grads, *refs):
    w_refs, out, flat = refs[:n], refs[n], refs[n + 1]
    rows = w_refs[0].shape[0]
    width = grads.shape[2]
    for i in range(3):
        flat[:, i * width : (i + 1) * width] = grads[i]
    for start, w_ref in zip(bases(meta[0], n, rows), w_refs):
        term = times_transposed(grads[1], w_ref[:, width : 2 * width])
        term = term + times_transposed(grads[2], w_ref[:, 2 * width :])

        @pl.when(pl.program_id(0) == 0)
        def _():
            own = term + times_transposed(grads[0], w_ref[:, :width])
            out[0, :, pl.ds(start, rows)] = own.astype(BF16)

        @pl.when(pl.program_id(0) > 0)
        def _():
            out[0, :, pl.ds(start, rows)] = term.astype(BF16)


def unproject(meta, grads, weights, chunks, after=()):
    length, width = grads.shape[1:]
    tok = length // chunks
    rows = weights[0].shape[0]
    n = len(weights)
    kernel, waits = ordered(functools.partial(unproject_kernel, n), 2 + n, after)
    return pl.pallas_call(
        kernel,
        grid_spec=pltpu.PrefetchScalarGridSpec(
            num_scalar_prefetch=1,
            grid=(chunks,),
            in_specs=[pl.BlockSpec((3, tok, width), lambda c, m: (0, c, 0))]
            + [pl.BlockSpec((rows, 3 * width), lambda c, m: (0, 0))] * n
            + waits,
            out_specs=[
                pl.BlockSpec((1, tok, width), lambda c, m: (lax.rem(c + m[1], chunks), 0, 0)),
                pl.BlockSpec((tok, 3 * width), lambda c, m: (c, 0)),
            ],
        ),
        out_shape=[
            jax.ShapeDtypeStruct((chunks, tok, width), BF16),
            jax.ShapeDtypeStruct((length, 3 * width), BF16),
        ],
        name="unproject",
    )(meta, grads, *weights, *after)


def rear_kernel(parts, z_ref, gres, gain, gz_ref, sums):
    grad = parts[0].astype(F32)
    for i in range(1, parts.shape[0]):
        grad = grad + parts[i].astype(F32)
    centred, rstd = statistics(z_ref[...])
    unit = centred * rstd
    low = (gres[...] + norm_back(unit, rstd, gain[...], grad)).astype(BF16)
    gz_ref[...] = low
    sums[0:1] = jnp.sum(low.astype(F32), axis=0, keepdims=True)
    sums[1:2] = jnp.sum(unit * grad, axis=0, keepdims=True)
    sums[2:3] = jnp.sum(grad, axis=0, keepdims=True)


def rear(parts, z, gres, gain, after=()):
    tok, width = z.shape
    count = 4
    kernel, waits = ordered(rear_kernel, count, after)
    vmem = pl.BlockSpec(memory_space=pltpu.VMEM)
    return pl.pallas_call(
        kernel,
        in_specs=[vmem] * count + waits,
        out_specs=[vmem] * 2,
        out_shape=[
            jax.ShapeDtypeStruct((tok, width), BF16),
            jax.ShapeDtypeStruct((8, width), F32),
        ],
        name="rear",
    )(parts, z, gres, gain, *after)


def forward_kernel(resid, bias, own, other, w_own, w_other, out, total):
    step = pl.program_id(0)
    part = times(own[...], w_own[...]) + times(other[...], w_other[...])

    @pl.when(step == 0)
    def _():
        total[...] = resid[...] + bias[...] + part

    @pl.when(step > 0)
    def _():
        total[...] += part

    @pl.when(step == pl.num_programs(0) - 1)
    def _():
        out[...] = total[...].astype(BF16)


def forward(meta, resid, bias, acts, weights, after=()):
    tok, width = resid.shape
    steps = len(TURNS)
    rows = weights[0].shape[0] // steps
    whole = pl.BlockSpec((tok, width), lambda k, m: (0, 0))
    kernel, waits = ordered(
        lambda meta, *refs: forward_kernel(*refs), 7, after
    )
    return pl.pallas_call(
        kernel,
        grid_spec=pltpu.PrefetchScalarGridSpec(
            num_scalar_prefetch=1,
            grid=(steps,),
            in_specs=[whole, pl.BlockSpec((1, width), lambda k, m: (0, 0))]
            + [pl.BlockSpec((tok, rows), lambda k, m: (0, k))] * 2
            + [pl.BlockSpec((rows, width), lambda k, m: (m[2] ^ k ^ (k >> 1), 0))] * 2
            + waits,
            out_specs=whole,
            scratch_shapes=[pltpu.VMEM((tok, width), F32)],
        ),
        out_shape=jax.ShapeDtypeStruct((tok, width), BF16),
        name="forward",
    )(meta, resid, bias, *acts, *weights, *after)


def sort_sums_kernel(meta, late, early, wide, mine, theirs):
    rows = [late[i : i + 1] for i in range(3)] + [early[i : i + 1] for i in range(3)]
    rows = rows + [wide[...], early[3:4]]
    first = meta[0] == 0
    start = 0
    for row in rows:
        half = row.shape[1] // 2
        low, high = row[:, :half], row[:, half:]
        mine[:, start : start + half] = jnp.where(first, low, high)
        theirs[:, start : start + half] = jnp.where(first, high, low)
        start = start + half


def sort_sums(meta, late, early, wide, after=()):
    size = (7 * late.shape[1] + wide.shape[1]) // 2
    vmem = pl.BlockSpec(memory_space=pltpu.VMEM)
    kernel, waits = ordered(sort_sums_kernel, 4, after)
    return pl.pallas_call(
        kernel,
        in_specs=[pl.BlockSpec(memory_space=pltpu.SMEM), vmem, vmem, vmem] + waits,
        out_specs=[vmem] * 2,
        out_shape=[jax.ShapeDtypeStruct((1, size), F32)] * 2,
        name="sort_sums",
    )(meta, late, early, wide, *after)


def input_grads_kernel(n, meta, gz, first, second, input_ref, skip_ref):
    low = times_transposed(gz[...], first[...])
    high = times_transposed(gz[...], second[...])
    if n == 1:
        input_ref[...] = low
        skip_ref[...] = high
        return

    @pl.when(meta[0] == 0)
    def _():
        input_ref[...] = low
        skip_ref[...] = high

    @pl.when(meta[0] != 0)
    def _():
        input_ref[...] = high
        skip_ref[...] = low


def input_grads(meta, gz, weights, after=()):
    tok, width = gz.shape
    n = len(weights)
    steps = 4
    tile = width // steps
    if n == 1:
        weights = [weights[0], weights[0]]
    out = pl.BlockSpec((tok, tile), lambda t, m: (0, t))
    kernel, waits = ordered(functools.partial(input_grads_kernel, n), 4, after)
    return pl.pallas_call(
        kernel,
        grid_spec=pltpu.PrefetchScalarGridSpec(
            num_scalar_prefetch=1,
            grid=(steps,),
            in_specs=[
                pl.BlockSpec((tok, width), lambda t, m: (0, 0)),
                pl.BlockSpec((tile, width), lambda t, m: (t, 0)),
                pl.BlockSpec((tile, width), lambda t, m: (t + (steps if n == 1 else 0), 0)),
            ]
            + waits,
            out_specs=[out, out],
        ),
        out_shape=[jax.ShapeDtypeStruct((tok, width), F32)] * 2,
        name="input_grads",
    )(meta, gz, *weights, *after)


def pack_kernel(*refs):
    out = refs[-1]
    start = 0
    for ref in refs[:-1]:
        size = ref.shape[0]
        out[0, start : start + size] = ref[...]
        start = start + size


def pack(vectors):
    total = sum(v.shape[0] for v in vectors)
    return pl.pallas_call(
        pack_kernel, out_shape=jax.ShapeDtypeStruct((1, total), vectors[0].dtype), name="pack"
    )(*vectors)


def unpack_kernel(sizes, meta, own, other, *outs):
    start = 0
    for size, out in zip(sizes, outs):
        for ref, core in ((own, meta[0]), (other, 1 - meta[0])):
            at = pl.multiple_of(core * size, 128)
            out[:, pl.ds(at, size)] = ref[:, start : start + size].astype(F32)
        start = start + size


def unpack(meta, own, other, sizes, after=()):
    vmem = pl.BlockSpec(memory_space=pltpu.VMEM)
    kernel, waits = ordered(functools.partial(unpack_kernel, sizes), 3, after)
    return pl.pallas_call(
        kernel,
        in_specs=[pl.BlockSpec(memory_space=pltpu.SMEM), vmem, vmem] + waits,
        out_specs=[vmem] * len(sizes),
        out_shape=[jax.ShapeDtypeStruct((1, 2 * n), F32) for n in sizes],
        name="unpack",
    )(meta, own, other, *after)


def fold_kernel(terms, out):
    total = terms[0].astype(F32)
    for i in range(1, terms.shape[0]):
        total = total + terms[i].astype(F32)
    total = total.astype(BF16)
    for i in range(out.shape[0]):
        out[i] = total


def fold(terms, copies, after=()):
    n, rows, width = terms.shape
    tile = width
    while tile % 256 == 0 and tile > 1024:
        tile //= 2
    kernel, waits = ordered(fold_kernel, 1, after)
    return pl.pallas_call(
        kernel,
        grid=(width // tile,),
        in_specs=[pl.BlockSpec((n, rows, tile), lambda c: (0, 0, c))] + waits,
        out_specs=pl.BlockSpec((copies, rows, tile), lambda c: (0, 0, c)),
        out_shape=jax.ShapeDtypeStruct((copies, rows, width), BF16),
        name="fold",
    )(terms, *after)


def place_kernel(meta, own, by_x, by_y, far_low, far_high, out):
    part = pl.program_id(0)
    for i, ref in enumerate((own, by_x, by_y)):

        @pl.when(part == i)
        def _(ref=ref):
            out[...] = ref[...].astype(F32)

    @pl.when(part == 3)
    def _():
        half = far_low.shape[1]
        out[:, :half] = far_low[...].astype(F32)
        out[:, half:] = far_high[...].astype(F32)


def place(meta, parts, start, rows, after=()):
    width = parts[0].shape[1]
    tile = rows
    while start % tile or tile * width > 262144:
        tile //= 2
    base, steps = start // tile, rows // tile

    def spec(i, columns):
        def index(q, c, m):
            return (base + jnp.where(q == i, c, jnp.where(q < i, 0, steps - 1)), 0)

        return pl.BlockSpec((tile, columns), index)

    kernel, waits = ordered(place_kernel, 6, after)
    return pl.pallas_call(
        kernel,
        grid_spec=pltpu.PrefetchScalarGridSpec(
            num_scalar_prefetch=1,
            grid=(4, steps),
            in_specs=[spec(i, width) for i in range(3)] + [spec(3, width // 2)] * 2 + waits,
            out_specs=pl.BlockSpec((tile, width), lambda q, c, m: ((m[0] ^ q) * steps + c, 0)),
        ),
        out_shape=jax.ShapeDtypeStruct((4 * rows, width), F32),
        name="place",
    )(meta, *parts, *after)


class Links:
    def __init__(self):
        self.sent = {"x": [], "y": [], "z": [], "frames": []}

    def send(self, link, array, move, *pins):
        waits = [p for p in pins if p is not None]
        earlier = self.sent[link]
        depth = 2 if link in ("x", "y") else 1
        if len(earlier) >= depth:
            waits.append(earlier[-depth])
        if waits:
            array = tie(array, *waits)
        moved = move(array)
        earlier.append(moved)
        return moved


def tie(array, *others):
    return lax.optimization_barrier((array, *others))[0]


def body(
    frames_in,
    skip_in,
    lengths,
    cotangent,
    w_skip,
    w_qkv,
    w_out,
    w_up,
    w_down,
    skip_bias,
    norm1_gain,
    norm1_bias,
    out_bias,
    norm2_gain,
    norm2_bias,
    up_bias,
    down_bias,
):
    tok = frames_in.shape[3]
    width = frames_in.shape[4]
    frames = frames_in.reshape(tok, width)
    skips = skip_in.reshape(tok, width)
    cotan = cotangent.reshape(tok, width)
    n_batch = lax.axis_size("batch")
    n_seq = lax.axis_size("seq")
    n_frames = lax.axis_size("frames")
    assert n_batch == 4 and n_seq % 2 == 0
    paired = n_frames == 2
    plane = lax.axis_index("batch").astype(jnp.int32)
    shard = lax.axis_index("seq").astype(jnp.int32)
    core = lax.axis_index("frames").astype(jnp.int32)
    links = Links()

    def swap_frames(array):
        return lax.ppermute(array, "frames", [(0, 1), (1, 0)])

    def over_x(array):
        return lax.ppermute(array, "batch", [(i, i ^ 1) for i in range(n_batch)])

    def over_y(array):
        return lax.ppermute(array, "batch", [(i, i ^ 2) for i in range(n_batch)])

    def from_seq(step):
        return lambda array: lax.ppermute(
            array, "seq", [((i + step) % n_seq, i) for i in range(n_seq)]
        )

    def to_seq(step):
        return from_seq(n_seq - step)

    def exchange_seq(array):
        return lax.all_to_all(array, "seq", split_axis=0, concat_axis=0, tiled=True)

    def send_rows(array, *pins):
        if paired:
            return swap_frames(tie(array, *pins) if pins else array)
        return lax.all_gather(array, "frames", axis=0, tiled=True)

    def gather_frames(array, *pins):
        moved = send_rows(array, *pins)
        return [array, moved] if paired else [moved]

    def send_left(parts, *pins):
        if paired:
            return [parts[0], swap_frames(tie(parts[1], *pins) if pins else parts[1])]
        array = parts[0]
        split = array.reshape(array.shape[0], n_frames, array.shape[1] // n_frames)
        moved = lax.all_to_all(split, "frames", split_axis=1, concat_axis=0, tiled=True)
        return [moved.reshape(array.shape[0] * n_frames, array.shape[1] // n_frames)]

    def by_plane(source):
        block = source.shape[1] // n_batch
        return jnp.concatenate(
            [
                lax.dynamic_slice_in_dim(source, (plane ^ bits) * block, block, 1)
                for bits in TURNS
            ],
            axis=1,
        )

    def turned(sources):
        return stack(sources if paired else [by_plane(source) for source in sources])

    def stack(arrays):
        return arrays[0] if len(arrays) == 1 else jnp.concatenate(arrays, axis=0)

    class Chain:
        def __init__(self, terms):
            self.terms = terms
            self.half = terms[0][1][0].shape[1] // 2
            self.blocks = [lefts[0].shape[1] // n_batch for lefts, _ in terms]
            self.block = sum(self.blocks)

        def gemm(self, plane_blocks, low, high):
            whole = len(self.terms) == 1
            first, last = plane_blocks[0], plane_blocks[-1] + 1
            spans = [(first, last)] if whole else [(p, p + 1) for p in plane_blocks]
            outs = []
            for p, q in spans:
                for (lefts, rights), block in zip(self.terms, self.blocks):
                    total = None
                    for left, right in zip(lefts, rights):
                        term = contract_rows(
                            left[:, p * block : q * block], right[:, low:high]
                        )
                        total = term if total is None else total + term
                    outs.append(total)
            return stack(outs)

        def begin(self, *pins):
            half = self.half
            if pins:
                lefts, rights = self.terms[0]
                self.terms[0] = ([tie(lefts[0], *pins), *lefts[1:]], rights)
            self.to_x = self.gemm((1, 2), 0, half).astype(BF16)
            self.to_y = self.gemm((2, 3), half, 2 * half).astype(BF16)
            return self.to_x, self.to_y

        def first(self, *pins):
            self.from_x = links.send("x", self.to_x, over_x, *pins)
            self.from_y = links.send("y", self.to_y, over_y, *pins)

        def between(self, *pins):
            half, block = self.half, self.block
            from_x, from_y = self.from_x, self.from_y
            if pins:
                from_x, from_y = tie(from_x, *pins), tie(from_y, *pins)
            low = self.gemm((3,), 0, half) + from_x[block:].astype(F32)
            high = self.gemm((1,), half, 2 * half) + from_y[:block].astype(F32)
            self.next_y, self.next_x = low.astype(BF16), high.astype(BF16)
            return self.next_x, self.next_y

        def second(self, *pins):
            self.then_y = links.send("y", self.next_y, over_y, *pins)
            self.then_x = links.send("x", self.next_x, over_x, *pins)

        def own_sum(self, *pins):
            block, half = self.block, self.half
            then_x, then_y = self.then_x, self.then_y
            if pins:
                then_x, then_y = tie(then_x, *pins), tie(then_y, *pins)
            low = self.from_x[:block].astype(F32) + then_y.astype(F32)
            high = self.from_y[block:].astype(F32) + then_x.astype(F32)
            own = self.gemm((0,), 0, 2 * half) + jnp.concatenate([low, high], axis=1)
            self.own = own.astype(BF16).reshape(n_seq, block // n_seq, 2 * half)
            return self.own

        def across(self, *pins):
            self.terms_seq = links.send("z", self.own, exchange_seq, *pins)

        def along(self, after=(), *pins):
            self.folded = fold(self.terms_seq, n_seq, after)
            whole = links.send("z", self.folded, exchange_seq, *pins)
            self.whole = whole.reshape(self.block, 2 * self.half)
            return self.folded

        def spread(self, *pins):
            self.by_x = links.send("x", self.whole, over_x, *pins)
            self.by_y = links.send("y", self.whole, over_y, *pins)

        def finish(self, *pins):
            half = self.half
            self.far_low = links.send("x", self.by_y[:, :half], over_x, *pins)
            self.far_high = links.send("y", self.by_x[:, half:], over_y, *pins)

        def place(self, after=()):
            parts = (self.whole, self.by_x, self.by_y, self.far_low, self.far_high)
            starts = [sum(self.blocks[:i]) for i in range(len(self.blocks))]
            return [
                place(plane.reshape(1), parts, start, rows, after)
                for start, rows in zip(starts, self.blocks)
            ]

    vectors_in = (
        skip_bias,
        norm1_gain,
        norm1_bias,
        out_bias,
        norm2_gain,
        norm2_bias,
        up_bias,
        down_bias,
    )
    sizes = [v.shape[0] for v in vectors_in]
    starts = [sum(sizes[:i]) for i in range(len(sizes))]
    packed = pack(vectors_in)
    meta = jnp.concatenate([jnp.stack([core, shard, plane]), lengths.reshape(-1)])
    full_skip = gather_frames(w_skip, packed)

    if paired:
        packs = [packed, swap_frames(packed)]
        full_qkv = gather_frames(w_qkv, full_skip[1], packs[1])
        full_down = gather_frames(w_down, full_skip[1], packs[1])
        hidden_z, n1, own_in, other_in = front(
            meta, frames, skips, full_skip, packs, tuple(sizes)
        )
        vectors = unpack(meta, *packs, sizes, after=(n1,))
        inputs = [own_in, other_in]
    else:
        packed = lax.all_gather(packed, "frames", axis=0, tiled=True).astype(F32)
        vectors = [packed[:, b : b + n].reshape(1, -1) for b, n in zip(starts, sizes)]
        hidden_z, n1 = front_whole(frames, skips, full_skip[0], *vectors[:3])
        inputs = [jnp.concatenate([frames, skips], axis=1)]
        full_qkv, full_down = gather_frames(w_qkv), gather_frames(w_down)
    obias, gain2, bias2, ubias, dbias = vectors[3:]
    gain1 = vectors[1]
    n1_all = [n1] + [from_seq(j)(n1) for j in range(1, n_seq)]
    full_up = gather_frames(w_up, full_down[-1], n1)
    gact = [times_transposed(tie(cotan, n1), full_down[0])]
    if paired:
        gact.append(times_transposed(tie(cotan, gact[0]), full_down[1]))
    queries, key_rows, value_rows, *n1_parts = project(
        meta, n1_all, full_qkv, after=(*gact, gain1)
    )
    full_out = gather_frames(w_out, queries)
    both_cotan = [cotan, swap_frames(tie(cotan, queries))] if paired else None
    if not paired:
        both_cotan = [lax.all_gather(cotan, "frames", axis=0, tiled=True)]
    left_n1 = send_left(n1_parts)
    attended, prob = attend_forward(meta, queries, key_rows, value_rows)
    both_cotan = stack(both_cotan)
    left_n1 = left_n1 if paired else [by_plane(a) for a in left_n1]
    (
        resid,
        gup,
        grad_resid,
        grad_branch,
        grad_heads,
        up_sum,
        sums2,
        *parts,
    ) = centre(
        meta,
        attended,
        hidden_z,
        cotan,
        full_out,
        full_up,
        gact,
        ubias,
        obias,
        gain2,
        bias2,
        after=(both_cotan, *left_n1),
    )
    n = len(full_out)
    acts, n2_parts, att_parts = parts[:n], parts[n : 2 * n], parts[2 * n :]

    def right_rows(array, *pins):
        moved = send_rows(array, *pins)
        return stack([array, moved] if paired else [moved])

    down = Chain([([turned(send_left(acts))], [both_cotan])])
    down_first = down.begin()
    down.first()
    both_up = right_rows(gup)
    left_n2 = turned(send_left(n2_parts))
    grads = attend_backward(queries, key_rows, value_rows, grad_heads, prob, after=down_first)
    up = Chain([([left_n2], [both_up])])
    terms_n1, flat = unproject(meta, grads, full_qkv, n_seq, after=down_first)
    down_second = down.between(flat)
    down.second()
    up_first = up.begin(*down_second)
    up.first()
    terms_n1 = links.send("z", terms_n1, exchange_seq)
    both_flat = gather_frames(flat, *up_first)
    qkv = Chain([(left_n1, both_flat)])
    down_own = down.own_sum(*up_first)
    grad_z, sums1 = rear(
        terms_n1, hidden_z, grad_resid, gain1, after=(down_own, both_flat[-1])
    )
    up.between(grad_z)
    up.second()
    down.across()
    left_joined = turned(send_left(inputs, grad_z))
    left_att = turned(send_left(att_parts, grad_z))
    both_branch = right_rows(grad_branch, left_joined)
    rest = Chain([([left_joined], [right_rows(grad_z, left_att)]), ([left_att], [both_branch])])
    qkv_first = qkv.begin(up.next_x, up.next_y)
    qkv.first(up.then_x, up.then_y)
    up_own = up.own_sum(*qkv_first)
    up.across()
    rest_first = rest.begin(up_own)
    rest.first()
    qkv_second = qkv.between(*rest_first)
    qkv.second()
    down_fold = down.along(qkv_second, rest.from_x, rest.from_y)
    rest_second = rest.between(down_fold)
    rest.second()
    up_fold = up.along(rest_second, qkv.then_x, qkv.then_y)
    qkv_own = qkv.own_sum(up_fold)
    down.spread()
    if paired:
        output = forward(meta, resid, dbias, acts, full_down, after=(qkv_own,))
        mine, theirs = sort_sums(meta, sums1, sums2, up_sum, after=rest_first)
        mine = mine + swap_frames(theirs)
    else:
        output = (resid + times(acts[0], full_down[0]) + dbias).astype(BF16)
        summed = (
            *(sums1[i] for i in range(3)),
            *(sums2[i] for i in range(3)),
            up_sum[0],
            sums2[3],
        )
        summed = jnp.concatenate([v.reshape(n_frames, -1) for v in summed], axis=1)
        mine = lax.psum_scatter(summed, "frames", scatter_dimension=0, tiled=True)
    rest_own = rest.own_sum(output)
    qkv.across(rest.then_x, rest.then_y)
    up.spread()
    input_grad, skip_grad = input_grads(meta, grad_z, full_skip, after=(rest_own,))
    down.finish()
    qkv.along((input_grad,), down.by_x, down.by_y, up.by_x, up.by_y)
    rest.across(down.far_low, down.far_high)
    qkv.spread()
    (grad_w_down,) = down.place()
    up.finish()
    rest.along((mine, grad_w_down), qkv.by_x, qkv.by_y)
    copies = jnp.broadcast_to(mine[None], (n_batch * n_seq,) + mine.shape)

    def exchange_all(array):
        return lax.all_to_all(array, ("batch", "seq"), split_axis=0, concat_axis=0, tiled=True)

    qkv.finish()
    (grad_w_up,) = up.place()
    total = exchange_all(tie(copies, qkv.far_low, qkv.far_high))
    rest.spread(grad_w_up)
    (grad_w_qkv,) = qkv.place(after=(grad_w_up,))
    rest.finish(grad_w_qkv)
    total = jnp.sum(total, axis=0).reshape(-1)
    vector_grads = [total[b : b + n] for b, n in zip(starts, sizes)]
    grad_w_skip, grad_w_out = rest.place(after=(grad_w_qkv,))

    def back(array):
        return array.reshape(1, 1, 1, tok, width)

    return (
        back(output),
        back(input_grad),
        back(skip_grad),
        grad_w_skip,
        grad_w_qkv,
        grad_w_out,
        grad_w_up,
        grad_w_down,
        *vector_grads,
    )


def solution(mesh):
    rows = P("batch", "seq", "frames", None, None)
    in_specs = (
        (rows, rows, P("batch", "frames", None), rows)
        + (P("frames", None),) * 5
        + (P("frames"),) * 8
    )
    out_specs = (rows,) * 3 + (P("frames", None),) * 5 + (P("frames"),) * 8
    return jax.shard_map(body, mesh=mesh, in_specs=in_specs, out_specs=out_specs, check_vma=False)
```
